256 devices in a mesh: member: 16 (over z, x_lo), lat: 8 (over y, core), lon: 2 (over x_hi).
Axes of the slice: x: 4 (x_hi: 2, x_lo: 2; x = x_hi * 2 + x_lo), y: 4, z: 8, core: 2. Of those that a mesh axis runs over, the one named last changes fastest.
Arguments:
- state: bfloat16 [100, 16, 720], P(None, 'lat', 'lon'), may hold values from -6 to 6
- target: bfloat16 [100, 16, 720], P(None, 'lat', 'lon'), may hold values from -6 to 6
- land_sea: int32 [16, 720], P('lat', 'lon'), may hold values 0 or 1
- seeds: int32 [16, 32], P('member'), may hold values from 0 to 65535
- w_in: bfloat16 [9, 100, 256], replicated, may hold values from -0.1875 to 0.1875
- w_mid: bfloat16 [9, 256, 256], replicated, may hold values from -0.125 to 0.125
- w_out: bfloat16 [100, 256], replicated, may hold values from -0.375 to 0.375
- w_noise: float32 [32, 256], replicated, may hold values from -1 to 1
Outputs:
- update_in: float32 [9, 100, 256], replicated
- update_mid: float32 [9, 256, 256], replicated
- update_out: float32 [100, 256], replicated
- update_noise: float32 [32, 256], replicated
- loss: float32 [], replicated
The draws below stay inside these ranges and needn't reach their ends.
All inputs are finite; a program needn't handle non-finite values. No bound on the sum of `land_sea` on one device may be relied on, other than what follows from the above.
Results may differ from the reference program's by a relative error of at most 0.0014.
Values may be sent and summed in bfloat16 or wider, within the bound.
No kernel may reach another device: no remote copies, remote signals or barrier semaphores. Data moves between devices by JAX's collectives and lax.ppermute only.
A program may use at most 64 MiB of HBM per device.

```python
import jax
import jax.numpy as jnp
from jax import lax

V = 100
C = 256
NOISE = 32
MEMBERS = 16
NLAT = 16
NLON = 720


def with_ends(values, rng, least, largest):
    dims = values.shape
    index_at = [jax.random.randint(jax.random.fold_in(rng, axis), (), 0, dims[axis]) for axis in range(len(dims))]
    values = values.at[tuple(index_at)].set(least)
    longest = dims.index(max(dims))
    index_at[longest] = (index_at[longest] + 1) % dims[longest]
    return values.at[tuple(index_at)].set(largest)


def block_levels(key, extent, shards, low, top_value):
    gain = 1.0
    for dim, blocks in shards:
        heights = jax.random.uniform(jax.random.fold_in(jax.random.fold_in(key, 6), dim), (blocks,), jnp.float32, low / len(shards), top_value / len(shards))
        gain = gain * jnp.repeat(jnp.exp(heights), extent[dim] // blocks).reshape((-1,) + (1,) * (len(extent) - 1 - dim))
    return gain


def centred(own_key, dims, deviation, limit, pieces=(), dtype=jnp.bfloat16):
    array = deviation * jax.random.normal(own_key, dims, jnp.float32)
    if pieces:
        array = array * block_levels(own_key, dims, pieces, -0.22, 0.18)
    return jnp.clip(array, -limit, limit).astype(dtype)


def setup_inputs(seed: int = 0) -> dict:
    keys = jax.random.split(jax.random.key(seed), 9)
    return {
        "state": centred(keys[0], (V, NLAT, NLON), 1.0, 6.0, ((1, 8), (2, 2))),
        "target": centred(keys[1], (V, NLAT, NLON), 1.0, 6.0, ((1, 8), (2, 2))),
        "land_sea": with_ends((jax.random.randint(keys[2], (NLAT, NLON), 0, 10) < 3).astype(jnp.int32), jax.random.fold_in(keys[2], 1), 0, 1),
        "seeds": with_ends(jax.random.randint(keys[3], (MEMBERS, NOISE), 0, 65536), jax.random.fold_in(keys[3], 1), 0, 65535).astype(jnp.int32),
        "w_in": centred(keys[4], (9, V, C), (9 * V) ** -0.5, 0.1875),
        "w_mid": centred(keys[5], (9, C, C), (9 * C) ** -0.5, 0.125),
        "w_out": centred(keys[6], (V, C), C ** -0.5, 0.375),
        "w_noise": centred(keys[7], (NOISE, C), NOISE ** -0.5, 1.0, (), jnp.float32),
    }


SMOOTH = 0.25

def pad_grid(fields):
    wrapped = jnp.concatenate([fields[:, :, -1:], fields, fields[:, :, :1]], axis=2)
    return jnp.pad(wrapped, ((0, 0), (1, 1), (0, 0)))

def shifted(padded, offset, row_count, col_count):
    row_shift = offset // 3
    col_shift = offset % 3
    window = padded[:, row_shift:row_shift + row_count, col_shift:col_shift + col_count]
    return window.reshape(padded.shape[0], row_count * col_count)

def conv_forward(weights, padded, row_count, col_count):
    summed = None
    for offset in range(9):
        window = shifted(padded, offset, row_count, col_count)
        part = lax.dot_general(weights[offset], window, (((0,), (0,)), ((), ())), preferred_element_type=jnp.float32)
        summed = part if summed is None else summed + part
    return summed

def conv_back(weights, padded, row_count, col_count):
    summed = None
    for offset in range(9):
        window = shifted(padded, 8 - offset, row_count, col_count)
        part = jnp.dot(weights[offset], window, preferred_element_type=jnp.float32)
        summed = part if summed is None else summed + part
    return summed

def weight_grad(padded, deltas, row_count, col_count):
    parts = []
    for offset in range(9):
        window = shifted(padded, offset, row_count, col_count)
        parts.append(lax.dot_general(window, deltas, (((1,), (1,)), ((), ())), preferred_element_type=jnp.float32))
    return jnp.stack(parts)

def gelu_pair(pre):
    return jax.jvp(jax.nn.gelu, (pre,), (jnp.ones_like(pre),))

def noise_vectors(seeds):
    return (seeds.astype(jnp.float32) - 32767.5) / 18918.0

def combine(outputs, target_flat, weights, slope_sum, spread_sum, members):
    misses = outputs - target_flat[None]
    radius = jnp.sqrt(misses * misses + SMOOTH * SMOOTH)
    gradients = weights[None] * (misses / radius / members - slope_sum / (members * (members - 1)))
    loss_term = jnp.sum(weights[None] * ((radius - SMOOTH) / members - spread_sum / (2 * members * (members - 1))))
    return (gradients, loss_term)

def pair_sums(outputs, others):

    def add_member(running, member_out):
        gap_value = outputs - member_out.astype(jnp.float32)[None]
        radius = jnp.sqrt(gap_value * gap_value + SMOOTH * SMOOTH)
        return ((running[0] + gap_value / radius, running[1] + radius - SMOOTH), None)
    blank = jnp.zeros(outputs.shape, jnp.float32)
    sums, _ = lax.scan(add_member, (blank, blank), others)
    return sums

def member_forward(state, w_in, w_mid, w_out, noise_bias):
    row_count, col_count = (state.shape[1], state.shape[2])
    channels = w_in.shape[2]
    state_pad = pad_grid(state)
    pre_in = conv_forward(w_in, state_pad, row_count, col_count) + noise_bias[:, None]
    act_in, slope_in = gelu_pair(pre_in)
    hidden_in = act_in.astype(jnp.bfloat16)
    hidden_pad = pad_grid(hidden_in.reshape(channels, row_count, col_count))
    pre_mid = conv_forward(w_mid, hidden_pad, row_count, col_count)
    act_mid, slope_mid = gelu_pair(pre_mid)
    hidden_out = (act_mid + hidden_in.astype(jnp.float32)).astype(jnp.bfloat16)
    flat_state = state.reshape(state.shape[0], -1).astype(jnp.float32)
    output = (flat_state + jnp.dot(w_out, hidden_out, preferred_element_type=jnp.float32)).astype(jnp.bfloat16)
    return (state_pad, hidden_pad, hidden_out, slope_in, slope_mid, output)

def member_grads(state, w_in, w_mid, w_out, noise_bias, latent, delta_out):
    row_count, col_count = (state.shape[1], state.shape[2])
    channels = w_in.shape[2]
    state_pad, hidden_pad, hidden_out, slope_in, slope_mid, _ = member_forward(state, w_in, w_mid, w_out, noise_bias)
    grad_out = lax.dot_general(delta_out, hidden_out, (((1,), (1,)), ((), ())), preferred_element_type=jnp.float32)
    upstream = lax.dot_general(w_out, delta_out, (((0,), (0,)), ((), ())), preferred_element_type=jnp.float32)
    delta_mid = (upstream * slope_mid).astype(jnp.bfloat16)
    delta_pad = pad_grid(delta_mid.reshape(channels, row_count, col_count))
    incoming = conv_back(w_mid, delta_pad, row_count, col_count) + upstream
    delta_in = (incoming * slope_in).astype(jnp.bfloat16)
    grad_mid = weight_grad(hidden_pad, delta_mid, row_count, col_count)
    grad_in = weight_grad(state_pad, delta_in, row_count, col_count)
    grad_noise = latent[:, None] * lax.optimization_barrier(jnp.sum(delta_in.astype(jnp.float32), axis=1))[None, :]
    return (grad_in, grad_mid, grad_out, grad_noise)

def normalize(gradient):
    return gradient / jnp.sqrt(jnp.mean(gradient * gradient) + 1e-06)

def reference(state, target, land_sea, seeds, w_in, w_mid, w_out, w_noise):
    latents = noise_vectors(seeds)
    biases = jnp.dot(latents, w_noise, precision=lax.Precision.HIGHEST)
    members = seeds.shape[0]
    outputs = lax.map(lambda noise_bias: member_forward(state, w_in, w_mid, w_out, noise_bias)[5], biases)
    target_flat = target.reshape(target.shape[0], -1).astype(jnp.float32)
    weights = 1.0 + land_sea.reshape(1, -1).astype(jnp.float32)
    outputs_f = outputs.astype(jnp.float32)
    slope_sum, spread_sum = pair_sums(outputs_f, outputs)
    gradients, summed = combine(outputs_f, target_flat, weights, slope_sum, spread_sum, members)
    deltas = gradients.astype(jnp.bfloat16)
    grad_in, grad_mid, grad_out, grad_noise = lax.map(lambda packed: member_grads(state, w_in, w_mid, w_out, packed[0], packed[1], packed[2]), (biases, latents, deltas))
    loss = summed / (outputs.shape[1] * outputs.shape[2])
    return (normalize(lax.optimization_barrier(jnp.sum(grad_in, axis=0))), normalize(lax.optimization_barrier(jnp.sum(grad_mid, axis=0))), normalize(lax.optimization_barrier(jnp.sum(grad_out, axis=0))), normalize(lax.optimization_barrier(jnp.sum(grad_noise, axis=0))), loss)
```

```python
import jax
import jax.numpy as jnp
from jax import lax
from jax.experimental import pallas as pl
from jax.experimental.pallas import tpu as pltpu
from jax.sharding import Mesh, PartitionSpec as P

f32 = jnp.float32
bf16 = jnp.bfloat16
SQ = 0.0625
GC = 0.7978845608028654
GA = 0.044715
V = 100
C = 256
M = 16
TC = 360
WP = 32
WH = 27
ROWS = 104
BR = 112
NB = 32
AX = ("z", "xl", "y", "c", "xh")
VMEM = 56 * 1024 * 1024


def perm(f, keep=None):
    out = []
    for i in range(256):
        z, xl, lat, xh = i >> 5, (i >> 4) & 1, (i >> 1) & 7, i & 1
        t = f(z, xl, lat, xh)
        if t is None:
            continue
        z2, xl2, lat2, xh2 = t
        out.append((i, (z2 % 8) * 32 + xl2 * 16 + lat2 * 2 + xh2))
    return out


def send(v, f):
    return lax.ppermute(v, AX, perm(f))


def lat_shift(v, d):
    def f(z, xl, lat, xh):
        return (z, xl, lat + d, xh) if 0 <= lat + d < 8 else None

    return send(v, f)


def params():
    return pltpu.CompilerParams(vmem_limit_bytes=VMEM)


def gelu(x):
    t = jnp.tanh(GC * (x + GA * x * x * x))
    return 0.5 * x * (1.0 + t)


def gelu_both(x):
    x2 = x * x
    t = jnp.tanh(GC * (x + GA * x2 * x))
    h = 0.5 * (1.0 + t)
    slope = h + 0.5 * x * (1.0 - t * t) * (GC * (1.0 + 3.0 * GA * x2))
    return x * h, slope


def gelu_slope(x):
    return gelu_both(x)[1]


def prep_kernel(state, target, land, x_out, edge_out, sc):
    sc[...] = jnp.zeros(sc.shape, f32)
    edge_out[...] = jnp.zeros(edge_out.shape, f32)
    for r in range(2):
        sc[0:V, 0:TC] = state[:, r, :].astype(f32)
        sc[104:105, 0:TC] = 1.0 + land[r : r + 1, :].astype(f32)
        x_out[r, :, 0:128] = sc[...].T
        sc[0:V, 0:TC] = target[:, r, :].astype(f32)
        x_out[r, :, 128:256] = sc[...].T
        edge_out[r, 0:3, :] = x_out[r, TC - 3 : TC, :]
        edge_out[r, 3:6, :] = x_out[r, 0:3, :]


def window_kernel(info, x, edge, win, ws):
    start = info[1]
    for r in range(2):
        ws[r, 8 : 8 + TC, :] = x[r, 0:TC, :]
        ws[r, 5:8, :] = edge[r, 0:3, :]
        ws[r, 8 + TC : 11 + TC, :] = edge[r, 3:6, :]
        ws[r, 11 + TC : 16 + TC, :] = jnp.zeros((5, 256), f32)
        base = pl.multiple_of(((start + 5) // 8) * 8, 8)
        near = ws[r, pl.ds(base, WP + 8), :]
        win[r, :, :] = pltpu.roll(near, WP + 8 - (start + 5 - base), 0)[0:WP].astype(bf16)


def main_kernel(
    info, n2, n1, own, s1, s2, seeds, w_in, w_mid, w_out, w_noise, g_out,
    S, T, SB, PB, HID, HO, SL, UP, OUT, DO, DM, INC, DS, QB, BIAS,
):
    own22 = info[2]
    lat = info[3]
    rows = (n2[1], n1[0], n1[1], own[0], own[1], s1[0], s1[1], s2[0])
    for k, row in enumerate(rows):
        S[32 * k : 32 * k + 32, :] = row[:, 0:128].astype(f32)
        T[32 * k : 32 * k + 32, :] = row[:, 128:256].astype(f32)
    S[256:264, :] = jnp.zeros((8, 128), f32)
    T[256:264, :] = jnp.zeros((8, 128), f32)
    QB[...] = jnp.broadcast_to(S[:, 104:105], QB.shape)
    for b in range(3):
        SB[b] = S[b : b + 256, :].astype(bf16)
    latents = (seeds[...].astype(f32) - 32767.5) / 18918.0
    BIAS[...] = jnp.dot(
        latents, w_noise[...], precision=lax.Precision.HIGHEST, preferred_element_type=f32
    )
    acc = None
    for a in range(3):
        for b in range(3):
            part = jnp.dot(
                SB[b, a * 32 : a * 32 + 192, 0:V], w_in[3 * a + b], preferred_element_type=f32
            )
            acc = part if acc is None else acc + part
    PB[...] = acc

    bias = BIAS[...]
    HID[162 * M : 164 * M, :] = jnp.zeros((2 * M, C), bf16)
    for r in range(6):
        gr = lat * 2 - 2 + r
        valid = jnp.where((gr >= 0) & (gr < 16), 1.0, 0.0).astype(f32)

        def hid_cell(i, carry, r=r, valid=valid):
            row = PB[pl.ds(r * 32 + i, 1), :]
            h = gelu(jnp.broadcast_to(row, (M, C)) + bias) * valid
            HID[pl.ds(pl.multiple_of((r * WH + i) * M, M), M), :] = h.astype(bf16)
            return carry

        lax.fori_loop(0, WH, hid_cell, 0, unroll=9)

    NR = WH * M

    def mid_row(r, carry):
        lhs = jnp.concatenate(
            [
                HID[pl.ds(pl.multiple_of(((r + a) * WH + b) * M, M), NR), :]
                for a in range(3)
                for b in range(3)
            ],
            axis=1,
        )
        pre = jnp.dot(lhs, w_mid[...].reshape(9 * C, C), preferred_element_type=f32)
        act, slope = gelu_both(pre)
        hid = HID[pl.ds(pl.multiple_of(((r + 1) * WH + 1) * M, M), NR), :].astype(f32)
        base = pl.multiple_of(r * NR, M)
        ho = (act + hid).astype(bf16)
        HO[pl.ds(base, NR), :] = ho
        SL[pl.ds(base, NR), :] = slope
        OUT[pl.ds(base, NR), 0:V] = lax.dot_general(
            ho, w_out[...], (((1,), (1,)), ((), ())), preferred_element_type=f32
        )
        return carry

    lax.fori_loop(0, 4, mid_row, 0)

    def cell_terms(r, i, with_loss):
        base = pl.multiple_of((r * WH + i) * M, M)
        srow = (r + 2) * 32 + i + 2
        st = S[pl.ds(srow, 1), :]
        tg = T[pl.ds(srow, 1), :]
        q = QB[pl.ds(srow, 1), :]
        o = (OUT[pl.ds(base, M), :] + st).astype(bf16).astype(f32)
        miss = o - tg
        e = miss * miss + SQ
        inv = lax.rsqrt(e)
        slope = miss * inv
        dist = e * inv - 0.25 if with_loss else None
        total = None
        spread = None
        for k in range(1, 9):
            u = o - pltpu.roll(o, k, 0)
            e = u * u + SQ
            inv = lax.rsqrt(e)
            s = u * inv
            if k < 8:
                s = s - pltpu.roll(s, M - k, 0)
            total = s if total is None else total + s
            if with_loss:
                d = e * inv - 0.25
                if k == 8:
                    d = 0.5 * d
                spread = d if spread is None else spread + d
        g = q * (slope * (1.0 / M) - total * (1.0 / (M * (M - 1))))
        DO[pl.ds(base, M), :] = g.astype(bf16)
        if with_loss:
            return q * (dist * (1.0 / M) - spread * (1.0 / (M * (M - 1))))
        return None

    loss = jnp.zeros((M, 128), f32)
    for r in (1, 2):

        def loss_cell(i, total, r=r):
            term = cell_terms(r, i, True)
            mine = (i >= 1) & ((i < 23) | ((i == 23) & (own22 > 0)))
            return total + jnp.where(mine, 1.0, 0.0) * term

        loss = lax.fori_loop(0, WH, loss_cell, loss, unroll=3)
    for r in (0, 3):

        def grad_cell(i, carry, r=r):
            cell_terms(r, i, False)
            return carry

        lax.fori_loop(0, WH, grad_cell, 0, unroll=3)
    lane = lax.broadcasted_iota(jnp.int32, (M, 128), 1)
    loss = jnp.sum(jnp.sum(jnp.where(lane < V, loss, 0.0), axis=0, keepdims=True), axis=1, keepdims=True)

    def up_row(r, carry):
        base = pl.multiple_of(r * NR, M)
        up = jnp.dot(DO[pl.ds(base, NR), 0:V], w_out[...], preferred_element_type=f32)
        UP[pl.ds(base, NR), :] = up
        DM[pl.ds(base, NR), :] = (up * SL[pl.ds(base, NR), :]).astype(bf16)
        return carry

    lax.fori_loop(0, 4, up_row, 0)
    DM[108 * M : 112 * M, :] = jnp.zeros((4 * M, C), bf16)

    wcat = jnp.concatenate([w_mid[t] for t in range(9)], axis=1)
    for r in range(2):
        lhs = jnp.concatenate(
            [
                DM[((r + 2 - a) * WH + 2 - b) * M : ((r + 2 - a) * WH + 2 - b) * M + NR, :]
                for a in range(3)
                for b in range(3)
            ],
            axis=1,
        )
        INC[r * NR : (r + 1) * NR, :] = lax.dot_general(
            lhs, wcat, (((1,), (1,)), ((), ())), preferred_element_type=f32
        )
    DS[...] = jnp.zeros(DS.shape, f32)
    dsum = jnp.zeros((M, C), f32)
    for r in range(2):

        def in_cell(i, total, r=r):
            x = jnp.broadcast_to(PB[pl.ds((r + 2) * 32 + i + 2, 1), :], (M, C)) + bias
            base = pl.multiple_of((r * WH + i) * M, M)
            upb = pl.multiple_of(((r + 1) * WH + 1 + i) * M, M)
            d = (INC[pl.ds(base, M), :] + UP[pl.ds(upb, M), :]) * gelu_slope(x)
            mine = jnp.where((i < 22) | (own22 > 0), 1.0, 0.0)
            d = d.astype(bf16).astype(f32) * mine
            DS[pl.ds(r * 32 + i + 2, 1), :] = jnp.sum(d, axis=0, keepdims=True)
            return total + d

        dsum = lax.fori_loop(0, 23, in_cell, dsum)

    g_out[:, ROWS:BR, :] = jnp.zeros((NB, BR - ROWS, C), f32)

    def put(row, value):
        done = 0
        n = value.shape[0]
        while done < n:
            k, i = divmod(row + done, ROWS)
            take = min(n - done, ROWS - i)
            g_out[k, i : i + take, :] = value[done : done + take, :]
            done += take

    cell = lax.broadcasted_iota(jnp.int32, (NR, C), 0) >> 4
    mine = (cell < 22) | ((cell == 22) & (own22 > 0))
    start = (WH + 1) * M
    dmc = jnp.concatenate(
        [
            jnp.where(mine, DM[start + r * NR : start + (r + 1) * NR, :].astype(f32), 0.0)
            for r in range(2)
        ],
        axis=0,
    )
    dmt = dmc.T.astype(bf16)
    for a in range(3):
        for b in range(3):
            hs = ((a + 1) * WH + b + 1) * M
            g = jnp.dot(dmt, HID[hs : hs + 2 * NR, :], preferred_element_type=f32)
            put((3 * a + b) * C, g.T)
    doc = jnp.concatenate(
        [
            jnp.where(
                mine[:, 0:128], DO[start + r * NR : start + (r + 1) * NR, :].astype(f32), 0.0
            )
            for r in range(2)
        ],
        axis=0,
    )
    dot_ = doc.T.astype(bf16)
    go = jnp.dot(dot_, HO[start : start + 2 * NR, :], preferred_element_type=f32)
    ds = DS[...]
    hi = ds.astype(bf16)
    lo = (ds - hi.astype(f32)).astype(bf16)
    both = jnp.concatenate([hi, lo], axis=1)
    for a in range(3):
        for b in range(3):
            g = lax.dot_general(
                SB[b, (a + 2) * 32 : (a + 2) * 32 + 64, :], both,
                (((0,), (0,)), ((), ())), preferred_element_type=f32,
            )
            put(9 * C + V * (3 * a + b), (g[:, 0:C] + g[:, C : 2 * C])[0:V, :])
    put(9 * C + 9 * V, go[0:V, :])
    put(9 * C + 10 * V, jnp.zeros((NB * ROWS - 9 * C - 10 * V, C), f32))
    gn = lax.dot_general(
        latents, dsum, (((0,), (0,)), ((), ())),
        precision=lax.Precision.HIGHEST, preferred_element_type=f32,
    )
    for k in range(NB):
        g_out[k, ROWS : ROWS + 1, :] = gn[k : k + 1, :]
    g_out[0, ROWS + 1 : ROWS + 2, :] = jnp.broadcast_to(loss, (1, C))


def final_kernel(t, o_in, o_mid, o_out, o_noise, o_loss):
    def get(row, n):
        parts = []
        done = 0
        while done < n:
            k, i = divmod(row + done, ROWS)
            take = min(n - done, ROWS - i)
            parts.append((done, take, t[k, i : i + take, :]))
            done += take
        return parts

    def norm(pieces, count, stores):
        total = jnp.zeros((1, C), f32)
        for p in pieces:
            for _, _, v in p:
                total = total + jnp.sum(v * v, axis=0, keepdims=True)
        ms = jnp.sum(total, axis=1, keepdims=True) * (1.0 / count)
        scale = lax.rsqrt(ms + 1e-6)
        for p, store in zip(pieces, stores):
            for done, take, v in p:
                store(done, take, v * scale)

    def into(ref, k):
        def f(done, take, v):
            ref[k, done : done + take, :] = v

        return f

    norm([get(C * k, C) for k in range(9)], 9 * C * C, [into(o_mid, k) for k in range(9)])
    norm(
        [get(9 * C + V * k, V) for k in range(9)], 9 * V * C, [into(o_in, k) for k in range(9)]
    )

    def out_store(done, take, v):
        o_out[done : done + take, :] = v

    norm([get(9 * C + 9 * V, V)], V * C, [out_store])

    def noise_store(done, take, v):
        o_noise[done : done + take, :] = v

    norm([[(k, 1, t[k, ROWS : ROWS + 1, :]) for k in range(NB)]], NB * C, [noise_store])
    o_loss[...] = t[0, ROWS + 1 : ROWS + 2, 0:128] * (1.0 / (V * 16 * 720))


def call(kernel, outs, scratch, n_smem, n_in, single=False):
    specs = [pl.BlockSpec(memory_space=pltpu.SMEM)] * n_smem
    specs += [pl.BlockSpec(memory_space=pltpu.VMEM)] * n_in
    out_specs = [pl.BlockSpec(memory_space=pltpu.VMEM)] * len(outs)
    shapes = [jax.ShapeDtypeStruct(s, d) for s, d in outs]
    return pl.pallas_call(
        kernel,
        out_shape=shapes[0] if single else shapes,
        in_specs=specs,
        out_specs=out_specs[0] if single else out_specs,
        scratch_shapes=scratch,
        compiler_params=params(),
    )


def sum_all(g):
    xy = ("xl", "y", "xh")
    core = lax.axis_index("c")

    def other(z, xl, lat, xh):
        return (z, xl, lat ^ 1, xh)

    g = g.reshape(2, 16, BR, C)
    theirs = lax.dynamic_index_in_dim(g, 1 - core, 0, False)
    mine = lax.dynamic_index_in_dim(g, core, 0, False)
    s = mine + send(theirs, other)
    s = lax.all_to_all(s, xy, 0, 0, tiled=True).sum(0)
    r1 = send(s, lambda z, xl, lat, xh: (z ^ 1, xl, lat, xh))
    r2 = send(s, lambda z, xl, lat, xh: (z ^ 2, xl, lat, xh))
    r3 = send(s, lambda z, xl, lat, xh: (z ^ 3, xl, lat, xh))
    s = (s + r1) + (r2 + r3)
    s = s + send(s, lambda z, xl, lat, xh: (z ^ 4, xl, lat, xh))
    half = lax.all_to_all(jnp.broadcast_to(s[None], (16,) + s.shape), xy, 0, 0, tiled=True)
    far = send(half, other)
    first = jnp.where(core == 0, half, far)
    second = jnp.where(core == 0, far, half)
    return jnp.concatenate([first, second], axis=0)


def gather_seeds(seeds):
    z = lax.axis_index("z")
    xl = lax.axis_index("xl")

    def spread(v, moves):
        return [v] + [
            send(v, lambda z, xl, lat, xh, d=d: (z ^ d[0], xl ^ d[1], lat, xh)) for d in moves
        ]

    near = jnp.concatenate(spread(seeds, ((0, 1), (1, 0), (1, 1))), axis=0)
    parts = spread(near, ((2, 0), (4, 0), (6, 0)))
    table = jnp.concatenate(parts, axis=0)
    member = z * 2 + xl
    order = jnp.bitwise_xor(jnp.arange(M, dtype=jnp.int32), member)
    return jnp.take(table, order, axis=0)


def body(state, target, land, seeds, w_in, w_mid, w_out, w_noise):
    z = lax.axis_index("z")
    xl = lax.axis_index("xl")
    lat = lax.axis_index("y") * 2 + lax.axis_index("c")
    member = z * 2 + xl
    info = jnp.stack([member, (45 * member) // 2, member % 2, lat]).astype(jnp.int32)
    x, edge = call(
        prep_kernel, [((2, 384, 256), f32), ((2, 8, 256), f32)],
        [pltpu.VMEM((128, 384), f32)], 0, 3,
    )(state, target, land)
    edge = send(edge, lambda z, xl, lat, xh: (z, xl, lat, xh ^ 1))
    win = call(
        window_kernel, [((2, WP, 256), bf16)], [pltpu.VMEM((2, 376, 256), f32)], 1, 2, True
    )(info, x, edge)
    n2, n1, s1, s2 = (lat_shift(win, d) for d in (2, 1, -1, -2))
    all_seeds = gather_seeds(seeds)
    g = call(
        main_kernel, [((NB, BR, C), f32)],
        [
            pltpu.VMEM((264, 128), f32),
            pltpu.VMEM((264, 128), f32),
            pltpu.VMEM((3, 256, 128), bf16),
            pltpu.VMEM((192, C), f32),
            pltpu.VMEM((164 * M, C), bf16),
            pltpu.VMEM((108 * M, C), bf16),
            pltpu.VMEM((108 * M, C), f32),
            pltpu.VMEM((108 * M, C), f32),
            pltpu.VMEM((108 * M, 128), f32),
            pltpu.VMEM((108 * M, 128), bf16),
            pltpu.VMEM((112 * M, C), bf16),
            pltpu.VMEM((54 * M, C), f32),
            pltpu.VMEM((64, C), f32),
            pltpu.VMEM((264, 128), f32),
            pltpu.VMEM((M, C), f32),
        ],
        1, 10, True,
    )(info, n2, n1, win, s1, s2, all_seeds, w_in, w_mid, w_out, w_noise)
    total = sum_all(g)
    o_in, o_mid, o_out, o_noise, o_loss = call(
        final_kernel,
        [((9, V, C), f32), ((9, C, C), f32), ((V, C), f32), ((NB, C), f32), ((1, 128), f32)],
        [], 0, 1,
    )(total)
    return o_in, o_mid, o_out, o_noise, o_loss[0, 0]


def solution(mesh):
    fine = Mesh(mesh.devices.reshape(8, 2, 4, 2, 2), AX)
    lat = ("y", "c")
    placed = (
        P(None, lat, "xh"), P(None, lat, "xh"), P(lat, "xh"), P(("z", "xl"), None),
        P(), P(), P(), P(),
    )
    return jax.shard_map(
        body, mesh=fine, in_specs=placed, out_specs=(P(), P(), P(), P(), P()), check_vma=False
    )
```

```python
import jax
import jax.numpy as jnp
from jax import lax
from jax.experimental import pallas as pl
from jax.experimental.pallas import tpu as pltpu
from jax.sharding import Mesh, PartitionSpec as P

f32 = jnp.float32
bf16 = jnp.bfloat16
SQ = 0.0625
GC = 0.7978845608028654
GA = 0.044715
V = 100
C = 256
M = 16
TC = 360
WP = 32
WH = 27
ROWS = 104
BR = 112
NB = 32
AX = ("z", "xl", "y", "c", "xh")
VMEM = 56 * 1024 * 1024


def perm(f):
    out = []
    for i in range(256):
        z, xl, lat, xh = i >> 5, (i >> 4) & 1, (i >> 1) & 7, i & 1
        z2, xl2, lat2, xh2 = f(z, xl, lat, xh)
        out.append((i, (z2 % 8) * 32 + xl2 * 16 + lat2 * 2 + xh2))
    return out


def send(v, f):
    return lax.ppermute(v, AX, perm(f))


def lat_shift(v, d):
    def f(z, xl, lat, xh):
        return (z, xl, (lat + d) % 8, xh)

    return send(v, f)


def params():
    return pltpu.CompilerParams(vmem_limit_bytes=VMEM)


def gelu(x):
    t = jnp.tanh(GC * (x + GA * x * x * x))
    return 0.5 * x * (1.0 + t)


def gelu_both(x):
    x2 = x * x
    t = jnp.tanh(GC * (x + GA * x2 * x))
    h = 0.5 * (1.0 + t)
    slope = h + 0.5 * x * (1.0 - t * t) * (GC * (1.0 + 3.0 * GA * x2))
    return x * h, slope


def gelu_slope(x):
    return gelu_both(x)[1]


def prep_kernel(state, target, land, x_out, edge_out, sc):
    sc[...] = jnp.zeros(sc.shape, f32)
    edge_out[...] = jnp.zeros(edge_out.shape, f32)
    for r in range(2):
        x_out[r, 0:8, :] = jnp.zeros((8, 256), f32)
        x_out[r, 8 + TC : 384, :] = jnp.zeros((376 - TC, 256), f32)
        sc[0:V, 0:TC] = state[:, r, :].astype(f32)
        sc[104:105, 0:TC] = 1.0 + land[r : r + 1, :].astype(f32)
        x_out[r, 8 : 8 + TC, 0:128] = sc[...].T[0:TC]
        sc[0:V, 0:TC] = target[:, r, :].astype(f32)
        x_out[r, 8 : 8 + TC, 128:256] = sc[...].T[0:TC]
        edge_out[r, 0:3, :] = x_out[r, TC + 5 : TC + 8, :]
        edge_out[r, 10:13, :] = x_out[r, 8:11, :]


def window_kernel(info, x, edge, sd0, sd1, sd2, sd3, win):
    m = info[0]
    start = info[1]
    row = lax.broadcasted_iota(jnp.int32, (16, 256), 0)
    low = (row < 3) & (m == 0)
    high = (row >= 10) & (row < 13) & (m == M - 1)
    for r in range(2):
        base = pl.multiple_of(((start + 5) // 8) * 8, 8)
        near = x[r, pl.ds(base, WP + 8), :]
        w = pltpu.roll(near, WP + 8 - (start + 5 - base), 0)[0:WP]
        e = edge[r]
        win[WP * r : WP * r + 16, :] = jnp.where(low, e, w[0:16]).astype(bf16)
        win[WP * r + 16 : WP * r + 32, :] = jnp.where(high, e, w[16:32]).astype(bf16)
    win[2 * WP : 2 * WP + 16, :] = jnp.zeros((16, 256), bf16)
    pad = jnp.zeros((12, 32), jnp.int32)
    sd = jnp.concatenate([sd0[...], sd1[...], sd2[...], sd3[...], pad], axis=0)
    win[2 * WP : 2 * WP + 16, 0:32] = (sd >> 8).astype(f32).astype(bf16)
    win[2 * WP : 2 * WP + 16, 128:160] = (sd & 255).astype(f32).astype(bf16)


def main_kernel(
    info, n2, n1, own, s1, s2, w_in, w_mid, w_out, w_noise, mine_out, theirs_out,
    S, T, SB, PB, HID, HO, SL, UP, OUT, DO, DM, INC, DS, QB, BIAS, SD, LT,
):
    own22 = info[2]
    lat = info[3]
    core = info[4]
    rows = ((n2, 1, -2), (n1, 0, -1), (n1, 1, -1), (own, 0, 0), (own, 1, 0),
            (s1, 0, 1), (s1, 1, 1), (s2, 0, 2))
    for k, (ref, r, d) in enumerate(rows):
        inside = (lat + d >= 0) & (lat + d < 8)
        row = ref[WP * r : WP * r + WP, :].astype(f32) * jnp.where(inside, 1.0, 0.0)
        S[WP * k : WP * k + WP, :] = row[:, 0:128]
        T[WP * k : WP * k + WP, :] = row[:, 128:256]
    S[256:264, :] = jnp.zeros((8, 128), f32)
    T[256:264, :] = jnp.zeros((8, 128), f32)
    QB[...] = jnp.broadcast_to(S[:, 104:105], QB.shape)
    for b in range(3):
        SB[b] = S[b : b + 256, :].astype(bf16)
    for d, ref in ((-1, n1), (0, own), (1, s1), (2, s2)):
        sd = ref[2 * WP : 2 * WP + 16, :].astype(f32)
        group = pl.multiple_of(((lat + d + 8) & 3) * 8, 8)
        SD[pl.ds(group, 8), :] = (sd[:, 0:128] * 256.0 + sd[:, 128:256])[0:8]
    for k in range(4):
        LT[4 * k : 4 * k + 4, :] = SD[8 * k : 8 * k + 4, :]
    latents = (LT[:, 0:32] - 32767.5) / 18918.0
    BIAS[...] = jnp.dot(
        latents, w_noise[...], precision=lax.Precision.HIGHEST, preferred_element_type=f32
    )
    acc = None
    for a in range(3):
        for b in range(3):
            part = jnp.dot(
                SB[b, a * 32 : a * 32 + 192, 0:V], w_in[3 * a + b], preferred_element_type=f32
            )
            acc = part if acc is None else acc + part
    PB[...] = acc

    bias = BIAS[...]
    HID[162 * M : 164 * M, :] = jnp.zeros((2 * M, C), bf16)
    for r in range(6):
        gr = lat * 2 - 2 + r
        valid = jnp.where((gr >= 0) & (gr < 16), 1.0, 0.0).astype(f32)

        def hid_cell(i, carry, r=r, valid=valid):
            row = PB[pl.ds(r * 32 + i, 1), :]
            h = gelu(jnp.broadcast_to(row, (M, C)) + bias) * valid
            HID[pl.ds(pl.multiple_of((r * WH + i) * M, M), M), :] = h.astype(bf16)
            return carry

        lax.fori_loop(0, WH, hid_cell, 0, unroll=9)

    NR = WH * M

    def mid_row(r, carry):
        lhs = jnp.concatenate(
            [
                HID[pl.ds(pl.multiple_of(((r + a) * WH + b) * M, M), NR), :]
                for a in range(3)
                for b in range(3)
            ],
            axis=1,
        )
        pre = jnp.dot(lhs, w_mid[...].reshape(9 * C, C), preferred_element_type=f32)
        act, slope = gelu_both(pre)
        hid = HID[pl.ds(pl.multiple_of(((r + 1) * WH + 1) * M, M), NR), :].astype(f32)
        base = pl.multiple_of(r * NR, M)
        ho = (act + hid).astype(bf16)
        HO[pl.ds(base, NR), :] = ho
        SL[pl.ds(base, NR), :] = slope
        OUT[pl.ds(base, NR), 0:V] = lax.dot_general(
            ho, w_out[...], (((1,), (1,)), ((), ())), preferred_element_type=f32
        )
        return carry

    lax.fori_loop(0, 4, mid_row, 0)

    def cell_terms(r, i, with_loss):
        base = pl.multiple_of((r * WH + i) * M, M)
        srow = (r + 2) * 32 + i + 2
        st = S[pl.ds(srow, 1), :]
        tg = T[pl.ds(srow, 1), :]
        q = QB[pl.ds(srow, 1), :]
        o = (OUT[pl.ds(base, M), :] + st).astype(bf16).astype(f32)
        miss = o - tg
        e = miss * miss + SQ
        inv = lax.rsqrt(e)
        slope = miss * inv
        dist = e * inv - 0.25 if with_loss else None
        total = None
        spread = None
        for k in range(1, 9):
            u = o - pltpu.roll(o, k, 0)
            e = u * u + SQ
            inv = lax.rsqrt(e)
            s = u * inv
            if k < 8:
                s = s - pltpu.roll(s, M - k, 0)
            total = s if total is None else total + s
            if with_loss:
                d = e * inv - 0.25
                if k == 8:
                    d = 0.5 * d
                spread = d if spread is None else spread + d
        g = q * (slope * (1.0 / M) - total * (1.0 / (M * (M - 1))))
        DO[pl.ds(base, M), :] = g.astype(bf16)
        if with_loss:
            return q * (dist * (1.0 / M) - spread * (1.0 / (M * (M - 1))))
        return None

    loss = jnp.zeros((M, 128), f32)
    for r in (1, 2):

        def loss_cell(i, total, r=r):
            term = cell_terms(r, i, True)
            mine = (i >= 1) & ((i < 23) | ((i == 23) & (own22 > 0)))
            return total + jnp.where(mine, 1.0, 0.0) * term

        loss = lax.fori_loop(0, WH, loss_cell, loss, unroll=3)
    for r in (0, 3):

        def grad_cell(i, carry, r=r):
            cell_terms(r, i, False)
            return carry

        lax.fori_loop(0, WH, grad_cell, 0, unroll=3)
    lane = lax.broadcasted_iota(jnp.int32, (M, 128), 1)
    loss = jnp.sum(jnp.sum(jnp.where(lane < V, loss, 0.0), axis=0, keepdims=True), axis=1, keepdims=True)

    def up_row(r, carry):
        base = pl.multiple_of(r * NR, M)
        up = jnp.dot(DO[pl.ds(base, NR), 0:V], w_out[...], preferred_element_type=f32)
        UP[pl.ds(base, NR), :] = up
        DM[pl.ds(base, NR), :] = (up * SL[pl.ds(base, NR), :]).astype(bf16)
        return carry

    lax.fori_loop(0, 4, up_row, 0)
    DM[108 * M : 112 * M, :] = jnp.zeros((4 * M, C), bf16)

    wcat = jnp.concatenate([w_mid[t] for t in range(9)], axis=1)
    for r in range(2):
        lhs = jnp.concatenate(
            [
                DM[((r + 2 - a) * WH + 2 - b) * M : ((r + 2 - a) * WH + 2 - b) * M + NR, :]
                for a in range(3)
                for b in range(3)
            ],
            axis=1,
        )
        INC[r * NR : (r + 1) * NR, :] = lax.dot_general(
            lhs, wcat, (((1,), (1,)), ((), ())), preferred_element_type=f32
        )
    DS[...] = jnp.zeros(DS.shape, f32)
    dsum = jnp.zeros((M, C), f32)
    for r in range(2):

        def in_cell(i, total, r=r):
            x = jnp.broadcast_to(PB[pl.ds((r + 2) * 32 + i + 2, 1), :], (M, C)) + bias
            base = pl.multiple_of((r * WH + i) * M, M)
            upb = pl.multiple_of(((r + 1) * WH + 1 + i) * M, M)
            d = (INC[pl.ds(base, M), :] + UP[pl.ds(upb, M), :]) * gelu_slope(x)
            mine = jnp.where((i < 22) | (own22 > 0), 1.0, 0.0)
            d = d.astype(bf16).astype(f32) * mine
            DS[pl.ds(r * 32 + i + 2, 1), :] = jnp.sum(d, axis=0, keepdims=True)
            return total + d

        dsum = lax.fori_loop(0, 23, in_cell, dsum)

    def store(k, lo, hi, value):
        @pl.when(core == k // 16)
        def _():
            mine_out[k % 16, lo:hi, :] = value

        @pl.when(core != k // 16)
        def _():
            theirs_out[k % 16, lo:hi, :] = value

    mine_out[:, ROWS:BR, :] = jnp.zeros((16, BR - ROWS, C), f32)
    theirs_out[:, ROWS:BR, :] = jnp.zeros((16, BR - ROWS, C), f32)
    peaks = []

    def put(row, value):
        done = 0
        n = value.shape[0]
        peaks.append(jnp.max(jnp.abs(value), axis=0, keepdims=True))
        while done < n:
            k, i = divmod(row + done, ROWS)
            take = min(n - done, ROWS - i)
            store(k, i, i + take, value[done : done + take, :])
            done += take

    cell = lax.broadcasted_iota(jnp.int32, (NR, C), 0) >> 4
    mine = (cell < 22) | ((cell == 22) & (own22 > 0))
    start = (WH + 1) * M
    dmc = jnp.concatenate(
        [
            jnp.where(mine, DM[start + r * NR : start + (r + 1) * NR, :].astype(f32), 0.0)
            for r in range(2)
        ],
        axis=0,
    )
    dmt = dmc.T.astype(bf16)
    for a in range(3):
        for b in range(3):
            hs = ((a + 1) * WH + b + 1) * M
            g = jnp.dot(dmt, HID[hs : hs + 2 * NR, :], preferred_element_type=f32)
            put((3 * a + b) * C, g.T)
    doc = jnp.concatenate(
        [
            jnp.where(
                mine[:, 0:128], DO[start + r * NR : start + (r + 1) * NR, :].astype(f32), 0.0
            )
            for r in range(2)
        ],
        axis=0,
    )
    dot_ = doc.T.astype(bf16)
    go = jnp.dot(dot_, HO[start : start + 2 * NR, :], preferred_element_type=f32)
    ds = DS[...]
    hi = ds.astype(bf16)
    lo = (ds - hi.astype(f32)).astype(bf16)
    both = jnp.concatenate([hi, lo], axis=1)
    for a in range(3):
        for b in range(3):
            g = lax.dot_general(
                SB[b, (a + 2) * 32 : (a + 2) * 32 + 64, :], both,
                (((0,), (0,)), ((), ())), preferred_element_type=f32,
            )
            put(9 * C + V * (3 * a + b), (g[:, 0:C] + g[:, C : 2 * C])[0:V, :])
    put(9 * C + 9 * V, go[0:V, :])
    put(9 * C + 10 * V, jnp.zeros((NB * ROWS - 9 * C - 10 * V, C), f32))
    gn = lax.dot_general(
        latents, dsum, (((0,), (0,)), ((), ())),
        precision=lax.Precision.HIGHEST, preferred_element_type=f32,
    )
    peaks.append(jnp.max(jnp.abs(gn), axis=0, keepdims=True))
    for k in range(NB):
        store(k, ROWS, ROWS + 1, gn[k : k + 1, :])
    store(0, ROWS + 1, ROWS + 2, jnp.broadcast_to(loss, (1, C)))
    peak = peaks[0]
    for p in peaks[1:]:
        peak = jnp.maximum(peak, p)
    peak = jnp.max(peak, axis=1, keepdims=True)
    lane = lax.broadcasted_iota(jnp.int32, (1, C), 1)
    top = jnp.where(lane < 128, peak, jnp.abs(loss))
    top = jnp.ceil(jnp.log(jnp.maximum(top, 1e-30)) * 1.4426950408889634)
    for k in range(16):
        mine_out[k, BR - 1 : BR, :] = top
        theirs_out[k, BR - 1 : BR, :] = top


def final_kernel(info, t, o_in, o_mid, o_out, o_noise, o_loss):
    core = info[4]

    def block(k):
        return ((k // 16) ^ core) * 16 + k % 16

    def get(row, n):
        parts = []
        done = 0
        while done < n:
            k, i = divmod(row + done, ROWS)
            take = min(n - done, ROWS - i)
            parts.append((done, take, t[block(k), i : i + take, :]))
            done += take
        return parts

    def norm(pieces, count, stores):
        total = jnp.zeros((1, C), f32)
        for p in pieces:
            for _, _, v in p:
                total = total + jnp.sum(v * v, axis=0, keepdims=True)
        ms = jnp.sum(total, axis=1, keepdims=True) * (1.0 / count)
        scale = lax.rsqrt(ms + 1e-6)
        for p, store in zip(pieces, stores):
            for done, take, v in p:
                store(done, take, v * scale)

    def into(ref, k):
        def f(done, take, v):
            ref[k, done : done + take, :] = v

        return f

    norm([get(C * k, C) for k in range(9)], 9 * C * C, [into(o_mid, k) for k in range(9)])
    norm(
        [get(9 * C + V * k, V) for k in range(9)], 9 * V * C, [into(o_in, k) for k in range(9)]
    )

    def out_store(done, take, v):
        o_out[done : done + take, :] = v

    norm([get(9 * C + 9 * V, V)], V * C, [out_store])

    def noise_store(done, take, v):
        o_noise[done : done + take, :] = v

    norm([[(k, 1, t[block(k), ROWS : ROWS + 1, :]) for k in range(NB)]], NB * C, [noise_store])
    o_loss[...] = t[block(0), ROWS + 1 : ROWS + 2, 0:128] * (1.0 / (V * 16 * 720))


def call(kernel, outs, scratch, n_smem, n_in, single=False):
    specs = [pl.BlockSpec(memory_space=pltpu.SMEM)] * n_smem
    specs += [pl.BlockSpec(memory_space=pltpu.VMEM)] * n_in
    out_specs = [pl.BlockSpec(memory_space=pltpu.VMEM)] * len(outs)
    shapes = [jax.ShapeDtypeStruct(s, d) for s, d in outs]
    return pl.pallas_call(
        kernel,
        out_shape=shapes[0] if single else shapes,
        in_specs=specs,
        out_specs=out_specs[0] if single else out_specs,
        scratch_shapes=scratch,
        compiler_params=params(),
    )


f16 = jnp.float16


def decode(msg):
    v = msg.astype(f32)
    e = v[..., BR - 1 : BR, 0:1]
    el = v[..., BR - 1 : BR, 128:129]
    row = lax.broadcasted_iota(jnp.int32, v.shape, v.ndim - 2)
    tail = lax.slice_in_dim(v, ROWS + 2, ROWS + 3, axis=v.ndim - 2) * (2.0**-11)
    power = jnp.where(row == ROWS + 1, el, e) - 14.0
    v = jnp.where(row == ROWS + 1, v + tail, v)
    return jnp.where(row > ROWS + 1, 0.0, v * jnp.exp2(power)), e, el


def encode(v, e, el):
    row = lax.broadcasted_iota(jnp.int32, v.shape, v.ndim - 2)
    lane = lax.broadcasted_iota(jnp.int32, v.shape, v.ndim - 1)
    big = v * jnp.exp2(14.0 - jnp.where(row == ROWS + 1, el, e))
    loss = lax.slice_in_dim(v, ROWS + 1, ROWS + 2, axis=v.ndim - 2) * jnp.exp2(14.0 - el)
    rest = (loss - lax.reduce_precision(loss, 5, 10)) * (2.0**11)
    big = jnp.where(row == ROWS + 2, rest, big)
    big = jnp.where(row == BR - 1, jnp.where(lane < 128, e, el), big)
    return big.astype(f16)


def sum_all(mine, theirs):
    xy = ("xl", "y", "xh")

    def other(z, xl, lat, xh):
        return (z, xl, lat ^ 1, xh)

    e = mine[0:1, BR - 1 : BR, 0:1]
    el = mine[0:1, BR - 1 : BR, 128:129]
    got, e1, el1 = decode(send(encode(theirs, e, el), other))
    s = jnp.where(lax.broadcasted_iota(jnp.int32, mine.shape, 1) > ROWS + 1, 0.0, mine) + got
    e, el = jnp.maximum(e, e1[0:1]) + 1.0, jnp.maximum(el, el1[0:1]) + 1.0
    got, e1, el1 = decode(lax.all_to_all(encode(s, e, el), xy, 0, 0, tiled=True))
    s = got.sum(0)
    e, el = jnp.max(e1, axis=0) + 4.0, jnp.max(el1, axis=0) + 4.0
    msg = encode(s, e, el)
    sets = [decode(msg)]
    for k in (1, 2, 3):
        sets.append(decode(send(msg, lambda z, xl, lat, xh, k=k: (z ^ k, xl, lat, xh))))
    s = (sets[0][0] + sets[1][0]) + (sets[2][0] + sets[3][0])
    e = jnp.maximum(jnp.maximum(sets[0][1], sets[1][1]), jnp.maximum(sets[2][1], sets[3][1])) + 2.0
    el = jnp.maximum(jnp.maximum(sets[0][2], sets[1][2]), jnp.maximum(sets[2][2], sets[3][2])) + 2.0
    msg = encode(s, e, el)
    v0, e0, el0 = decode(msg)
    v1, e1, el1 = decode(send(msg, lambda z, xl, lat, xh: (z ^ 4, xl, lat, xh)))
    msg = encode(v0 + v1, jnp.maximum(e0, e1) + 1.0, jnp.maximum(el0, el1) + 1.0)
    half = lax.all_to_all(jnp.broadcast_to(msg[None], (16,) + msg.shape), xy, 0, 0, tiled=True)
    far = send(half, other)
    return decode(jnp.concatenate([half, far], axis=0))[0]


def body(state, target, land, seeds, w_in, w_mid, w_out, w_noise):
    z = lax.axis_index("z")
    xl = lax.axis_index("xl")
    core = lax.axis_index("c")
    lat = lax.axis_index("y") * 2 + core
    member = z * 2 + xl
    info = jnp.stack([member, (45 * member) // 2, member % 2, lat, core]).astype(jnp.int32)
    x, edge = call(
        prep_kernel, [((2, 384, 256), f32), ((2, 16, 256), f32)],
        [pltpu.VMEM((128, 384), f32)], 0, 3,
    )(state, target, land)
    edge, seeds = lax.optimization_barrier((edge, seeds))
    edge = send(edge, lambda z, xl, lat, xh: (z, xl, lat, xh ^ 1))
    near = [
        send(
            seeds,
            lambda z, xl, lat, xh, k=k: (z ^ (2 * (lat % 4) + (k >> 1)), xl ^ (k & 1), lat, xh),
        )
        for k in range(4)
    ]
    win = call(window_kernel, [((80, 256), bf16)], [], 1, 6, True)(info, x, edge, *near)
    n2, n1, s1, s2 = (lat_shift(win, d) for d in (2, 1, -1, -2))
    mine, theirs = call(
        main_kernel, [((16, BR, C), f32), ((16, BR, C), f32)],
        [
            pltpu.VMEM((264, 128), f32),
            pltpu.VMEM((264, 128), f32),
            pltpu.VMEM((3, 256, 128), bf16),
            pltpu.VMEM((192, C), f32),
            pltpu.VMEM((164 * M, C), bf16),
            pltpu.VMEM((108 * M, C), bf16),
            pltpu.VMEM((108 * M, C), f32),
            pltpu.VMEM((108 * M, C), f32),
            pltpu.VMEM((108 * M, 128), f32),
            pltpu.VMEM((108 * M, 128), bf16),
            pltpu.VMEM((112 * M, C), bf16),
            pltpu.VMEM((54 * M, C), f32),
            pltpu.VMEM((64, C), f32),
            pltpu.VMEM((264, 128), f32),
            pltpu.VMEM((M, C), f32),
            pltpu.VMEM((32, 128), f32),
            pltpu.VMEM((M, 128), f32),
        ],
        1, 9,
    )(info, n2, n1, win, s1, s2, w_in, w_mid, w_out, w_noise)
    total = sum_all(mine, theirs)
    o_in, o_mid, o_out, o_noise, o_loss = call(
        final_kernel,
        [((9, V, C), f32), ((9, C, C), f32), ((V, C), f32), ((NB, C), f32), ((1, 128), f32)],
        [], 1, 1,
    )(info, total)
    return o_in, o_mid, o_out, o_noise, o_loss[0, 0]


def solution(mesh):
    fine = Mesh(mesh.devices.reshape(8, 2, 4, 2, 2), AX)
    lat = ("y", "c")
    placed = (
        P(None, lat, "xh"), P(None, lat, "xh"), P(lat, "xh"), P(("z", "xl"), None),
        P(), P(), P(), P(),
    )
    return jax.shard_map(
        body, mesh=fine, in_specs=placed, out_specs=(P(), P(), P(), P(), P()), check_vma=False
    )
```

```python
import jax
import jax.numpy as jnp
from jax import lax
from jax.experimental import pallas as pl
from jax.experimental.pallas import tpu as pltpu
from jax.sharding import Mesh, PartitionSpec as P

f32 = jnp.float32
bf16 = jnp.bfloat16
SQ = 0.0625
GC = 0.7978845608028654
GA = 0.044715
V = 100
C = 256
M = 16
TC = 360
WP = 32
WH = 27
ROWS = 104
BR = 112
NB = 32
AX = ("z", "xl", "y", "c", "xh")
VMEM = 56 * 1024 * 1024


def perm(f):
    out = []
    for i in range(256):
        z, xl, lat, xh = i >> 5, (i >> 4) & 1, (i >> 1) & 7, i & 1
        z2, xl2, lat2, xh2 = f(z, xl, lat, xh)
        out.append((i, (z2 % 8) * 32 + xl2 * 16 + lat2 * 2 + xh2))
    return out


def send(v, f):
    return lax.ppermute(v, AX, perm(f))


def lat_shift(v, d):
    def f(z, xl, lat, xh):
        return (z, xl, (lat + d) % 8, xh)

    return send(v, f)


def params():
    return pltpu.CompilerParams(vmem_limit_bytes=VMEM)


def gelu(x):
    t = jnp.tanh(GC * (x + GA * x * x * x))
    return 0.5 * x * (1.0 + t)


def gelu_both(x):
    x2 = x * x
    t = jnp.tanh(GC * (x + GA * x2 * x))
    h = 0.5 * (1.0 + t)
    slope = h + 0.5 * x * (1.0 - t * t) * (GC * (1.0 + 3.0 * GA * x2))
    return x * h, slope


def gelu_slope(x):
    return gelu_both(x)[1]


def prep_kernel(state, target, land, x_out, edge_out, sc):
    sc[...] = jnp.zeros(sc.shape, f32)
    edge_out[...] = jnp.zeros(edge_out.shape, f32)
    for r in range(2):
        x_out[r, 0:8, :] = jnp.zeros((8, 256), f32)
        x_out[r, 8 + TC : 384, :] = jnp.zeros((376 - TC, 256), f32)
        sc[0:V, 0:TC] = state[:, r, :].astype(f32)
        sc[104:105, 0:TC] = 1.0 + land[r : r + 1, :].astype(f32)
        x_out[r, 8 : 8 + TC, 0:128] = sc[...].T[0:TC]
        sc[0:V, 0:TC] = target[:, r, :].astype(f32)
        x_out[r, 8 : 8 + TC, 128:256] = sc[...].T[0:TC]
        edge_out[r, 0:3, :] = x_out[r, TC + 5 : TC + 8, :]
        edge_out[r, 10:13, :] = x_out[r, 8:11, :]


def window_kernel(info, x, edge, sd0, sd1, win):
    m = info[0]
    start = info[1]
    row = lax.broadcasted_iota(jnp.int32, (16, 256), 0)
    low = (row < 3) & (m == 0)
    high = (row >= 10) & (row < 13) & (m == M - 1)
    for r in range(2):
        base = pl.multiple_of(((start + 5) // 8) * 8, 8)
        near = x[r, pl.ds(base, WP + 8), :]
        w = pltpu.roll(near, WP + 8 - (start + 5 - base), 0)[0:WP]
        e = edge[16 * r : 16 * r + 16, :]
        win[WP * r : WP * r + 16, :] = jnp.where(low, e, w[0:16]).astype(bf16)
        win[WP * r + 16 : WP * r + 32, :] = jnp.where(high, e, w[16:32]).astype(bf16)
    win[2 * WP : 2 * WP + 16, :] = jnp.zeros((16, 256), bf16)
    pad = jnp.zeros((12, 32), jnp.int32)
    far = edge[32:34, 0:32].astype(jnp.int32)
    sd = jnp.concatenate([sd0[...], sd1[...], far, pad], axis=0)
    win[2 * WP : 2 * WP + 16, 0:32] = (sd >> 8).astype(f32).astype(bf16)
    win[2 * WP : 2 * WP + 16, 128:160] = (sd & 255).astype(f32).astype(bf16)


def main_kernel(
    info, n2, n1, own, s1, s2, w_in, w_mid, w_out, w_noise, g_out, e_out,
    S, T, SB, PB, HID, HO, SL, UP, OUT, DO, DM, INC, DS, QB, BIAS, SD, LT,
):
    own22 = info[2]
    lat = info[3]
    core = info[4]
    rows = ((n2, 1, -2), (n1, 0, -1), (n1, 1, -1), (own, 0, 0), (own, 1, 0),
            (s1, 0, 1), (s1, 1, 1), (s2, 0, 2))
    for k, (ref, r, d) in enumerate(rows):
        inside = (lat + d >= 0) & (lat + d < 8)
        row = ref[WP * r : WP * r + WP, :].astype(f32) * jnp.where(inside, 1.0, 0.0)
        S[WP * k : WP * k + WP, :] = row[:, 0:128]
        T[WP * k : WP * k + WP, :] = row[:, 128:256]
    S[256:264, :] = jnp.zeros((8, 128), f32)
    T[256:264, :] = jnp.zeros((8, 128), f32)
    QB[...] = jnp.broadcast_to(S[:, 104:105], QB.shape)
    for b in range(3):
        SB[b] = S[b : b + 256, :].astype(bf16)
    for d, ref in ((-1, n1), (0, own), (1, s1), (2, s2)):
        sd = ref[2 * WP : 2 * WP + 16, :].astype(f32)
        group = pl.multiple_of(((lat + d + 8) & 3) * 8, 8)
        SD[pl.ds(group, 8), :] = (sd[:, 0:128] * 256.0 + sd[:, 128:256])[0:8]
    for k in range(4):
        LT[4 * k : 4 * k + 4, :] = SD[8 * k : 8 * k + 4, :]
    latents = (LT[:, 0:32] - 32767.5) / 18918.0
    BIAS[...] = jnp.dot(
        latents, w_noise[...], precision=lax.Precision.HIGHEST, preferred_element_type=f32
    )
    acc = None
    for a in range(3):
        for b in range(3):
            part = jnp.dot(
                SB[b, a * 32 : a * 32 + 192, 0:V], w_in[3 * a + b], preferred_element_type=f32
            )
            acc = part if acc is None else acc + part
    PB[...] = acc

    bias = BIAS[...]
    HID[162 * M : 164 * M, :] = jnp.zeros((2 * M, C), bf16)
    for r in range(6):
        gr = lat * 2 - 2 + r
        valid = jnp.where((gr >= 0) & (gr < 16), 1.0, 0.0).astype(f32)

        def hid_cell(i, carry, r=r, valid=valid):
            row = PB[pl.ds(r * 32 + i, 1), :]
            h = gelu(jnp.broadcast_to(row, (M, C)) + bias) * valid
            HID[pl.ds(pl.multiple_of((r * WH + i) * M, M), M), :] = h.astype(bf16)
            return carry

        lax.fori_loop(0, WH, hid_cell, 0, unroll=9)

    NR = WH * M

    def mid_row(r, carry):
        lhs = jnp.concatenate(
            [
                HID[pl.ds(pl.multiple_of(((r + a) * WH + b) * M, M), NR), :]
                for a in range(3)
                for b in range(3)
            ],
            axis=1,
        )
        pre = jnp.dot(lhs, w_mid[...].reshape(9 * C, C), preferred_element_type=f32)
        act, slope = gelu_both(pre)
        hid = HID[pl.ds(pl.multiple_of(((r + 1) * WH + 1) * M, M), NR), :].astype(f32)
        base = pl.multiple_of(r * NR, M)
        ho = (act + hid).astype(bf16)
        HO[pl.ds(base, NR), :] = ho
        SL[pl.ds(base, NR), :] = slope
        OUT[pl.ds(base, NR), 0:V] = lax.dot_general(
            ho, w_out[...], (((1,), (1,)), ((), ())), preferred_element_type=f32
        )
        return carry

    lax.fori_loop(0, 4, mid_row, 0)

    def cell_terms(r, i, with_loss):
        base = pl.multiple_of((r * WH + i) * M, M)
        srow = (r + 2) * 32 + i + 2
        st = S[pl.ds(srow, 1), :]
        tg = T[pl.ds(srow, 1), :]
        q = QB[pl.ds(srow, 1), :]
        o = (OUT[pl.ds(base, M), :] + st).astype(bf16).astype(f32)
        miss = o - tg
        e = miss * miss + SQ
        inv = lax.rsqrt(e)
        slope = miss * inv
        dist = e * inv - 0.25 if with_loss else None
        total = None
        spread = None
        for k in range(1, 9):
            u = o - pltpu.roll(o, k, 0)
            e = u * u + SQ
            inv = lax.rsqrt(e)
            s = u * inv
            if k < 8:
                s = s - pltpu.roll(s, M - k, 0)
            total = s if total is None else total + s
            if with_loss:
                d = e * inv - 0.25
                if k == 8:
                    d = 0.5 * d
                spread = d if spread is None else spread + d
        g = q * (slope * (1.0 / M) - total * (1.0 / (M * (M - 1))))
        DO[pl.ds(base, M), :] = g.astype(bf16)
        if with_loss:
            return q * (dist * (1.0 / M) - spread * (1.0 / (M * (M - 1))))
        return None

    loss = jnp.zeros((M, 128), f32)
    for r in (1, 2):

        def loss_cell(i, total, r=r):
            term = cell_terms(r, i, True)
            mine = (i >= 1) & ((i < 23) | ((i == 23) & (own22 > 0)))
            return total + jnp.where(mine, 1.0, 0.0) * term

        loss = lax.fori_loop(0, WH, loss_cell, loss, unroll=3)
    for r in (0, 3):

        def grad_cell(i, carry, r=r):
            cell_terms(r, i, False)
            return carry

        lax.fori_loop(0, WH, grad_cell, 0, unroll=3)
    lane = lax.broadcasted_iota(jnp.int32, (M, 128), 1)
    loss = jnp.sum(jnp.sum(jnp.where(lane < V, loss, 0.0), axis=0, keepdims=True), axis=1, keepdims=True)

    def up_row(r, carry):
        base = pl.multiple_of(r * NR, M)
        up = jnp.dot(DO[pl.ds(base, NR), 0:V], w_out[...], preferred_element_type=f32)
        UP[pl.ds(base, NR), :] = up
        DM[pl.ds(base, NR), :] = (up * SL[pl.ds(base, NR), :]).astype(bf16)
        return carry

    lax.fori_loop(0, 4, up_row, 0)
    DM[108 * M : 112 * M, :] = jnp.zeros((4 * M, C), bf16)

    wcat = jnp.concatenate([w_mid[t] for t in range(9)], axis=1)
    for r in range(2):
        lhs = jnp.concatenate(
            [
                DM[((r + 2 - a) * WH + 2 - b) * M : ((r + 2 - a) * WH + 2 - b) * M + NR, :]
                for a in range(3)
                for b in range(3)
            ],
            axis=1,
        )
        INC[r * NR : (r + 1) * NR, :] = lax.dot_general(
            lhs, wcat, (((1,), (1,)), ((), ())), preferred_element_type=f32
        )
    DS[...] = jnp.zeros(DS.shape, f32)
    dsum = jnp.zeros((M, C), f32)
    for r in range(2):

        def in_cell(i, total, r=r):
            x = jnp.broadcast_to(PB[pl.ds((r + 2) * 32 + i + 2, 1), :], (M, C)) + bias
            base = pl.multiple_of((r * WH + i) * M, M)
            upb = pl.multiple_of(((r + 1) * WH + 1 + i) * M, M)
            d = (INC[pl.ds(base, M), :] + UP[pl.ds(upb, M), :]) * gelu_slope(x)
            mine = jnp.where((i < 22) | (own22 > 0), 1.0, 0.0)
            d = d.astype(bf16).astype(f32) * mine
            DS[pl.ds(r * 32 + i + 2, 1), :] = jnp.sum(d, axis=0, keepdims=True)
            return total + d

        dsum = lax.fori_loop(0, 23, in_cell, dsum)

    def store(k, lo, hi, value):
        g_out[(k // 16) ^ core, k % 16, lo:hi, :] = value

    g_out[:, :, ROWS:BR, :] = jnp.zeros((2, 16, BR - ROWS, C), f32)
    peaks = []

    def put(row, value):
        done = 0
        n = value.shape[0]
        peaks.append(jnp.max(jnp.abs(value), axis=0, keepdims=True))
        while done < n:
            k, i = divmod(row + done, ROWS)
            take = min(n - done, ROWS - i)
            store(k, i, i + take, value[done : done + take, :])
            done += take

    cell = lax.broadcasted_iota(jnp.int32, (NR, C), 0) >> 4
    mine = (cell < 22) | ((cell == 22) & (own22 > 0))
    start = (WH + 1) * M
    dmc = jnp.concatenate(
        [
            jnp.where(mine, DM[start + r * NR : start + (r + 1) * NR, :].astype(f32), 0.0)
            for r in range(2)
        ],
        axis=0,
    )
    dmt = dmc.T.astype(bf16)
    for a in range(3):
        for b in range(3):
            hs = ((a + 1) * WH + b + 1) * M
            g = jnp.dot(dmt, HID[hs : hs + 2 * NR, :], preferred_element_type=f32)
            put((3 * a + b) * C, g.T)
    doc = jnp.concatenate(
        [
            jnp.where(
                mine[:, 0:128], DO[start + r * NR : start + (r + 1) * NR, :].astype(f32), 0.0
            )
            for r in range(2)
        ],
        axis=0,
    )
    dot_ = doc.T.astype(bf16)
    go = jnp.dot(dot_, HO[start : start + 2 * NR, :], preferred_element_type=f32)
    ds = DS[...]
    hi = ds.astype(bf16)
    lo = (ds - hi.astype(f32)).astype(bf16)
    both = jnp.concatenate([hi, lo], axis=1)
    for a in range(3):
        for b in range(3):
            g = lax.dot_general(
                SB[b, (a + 2) * 32 : (a + 2) * 32 + 64, :], both,
                (((0,), (0,)), ((), ())), preferred_element_type=f32,
            )
            put(9 * C + V * (3 * a + b), (g[:, 0:C] + g[:, C : 2 * C])[0:V, :])
    put(9 * C + 9 * V, go[0:V, :])
    put(9 * C + 10 * V, jnp.zeros((NB * ROWS - 9 * C - 10 * V, C), f32))
    gn = lax.dot_general(
        latents, dsum, (((0,), (0,)), ((), ())),
        precision=lax.Precision.HIGHEST, preferred_element_type=f32,
    )
    peaks.append(jnp.max(jnp.abs(gn), axis=0, keepdims=True))
    for k in range(NB):
        store(k, ROWS, ROWS + 1, gn[k : k + 1, :])
    store(0, ROWS + 1, ROWS + 3, jnp.broadcast_to(loss, (2, C)))
    peak = peaks[0]
    for p in peaks[1:]:
        peak = jnp.maximum(peak, p)
    peak = jnp.max(peak, axis=1, keepdims=True)
    lane = lax.broadcasted_iota(jnp.int32, (8, 256), 1)
    e_out[...] = exponent(jnp.where(lane < 128, peak, jnp.abs(loss)))


def exponent(bound):
    return jnp.ceil(jnp.log(jnp.maximum(bound, 1e-30)) * 1.4426950408889634)


def power(e):
    return jnp.exp2(e)


def plane_kernel(msg, out):
    total = None
    bound = None
    row = lax.broadcasted_iota(jnp.int32, (BR, C), 0)
    for j in range(16):
        v = msg[j]
        e = v[BR - 1 : BR, :]
        grad = power(e[:, 0:1] - 14.0)
        loss = power(e[:, 128:129] - 14.0)
        f = jnp.where(row == ROWS + 1, loss, jnp.where(row == ROWS + 2, loss * 2.0**-11, grad))
        v = v * f
        total = v if total is None else total + v
        b = power(e)
        bound = b if bound is None else bound + b
    out[...] = total
    out[BR - 1 : BR, :] = bound


def scale_kernel(a, b, out):
    s = a[...] + b[...]
    e = exponent(s[BR - 1 : BR, :])
    grad = power(14.0 - e[:, 0:1])
    loss = power(14.0 - e[:, 128:129])
    row = lax.broadcasted_iota(jnp.int32, (BR, C), 0)
    f = jnp.where((row == ROWS + 1) | (row == ROWS + 2), loss, grad)
    out[...] = jnp.where(row == BR - 1, e, s * f)


def final_kernel(info, half, far, o_in, o_mid, o_out, o_noise, o_loss, t):
    core = info[4]
    row = lax.broadcasted_iota(jnp.int32, (BR, C), 0)
    is_loss = (row == ROWS + 1) | (row == ROWS + 2)
    for slot, ref in ((core, half), (1 - core, far)):
        for k in range(16):
            e = ref[k, BR - 1 : BR, :]
            f = jnp.where(is_loss, power(e[:, 128:129] - 14.0), power(e[:, 0:1] - 14.0))
            t[slot * 16 + k] = ref[k] * f

    def get(row, n):
        parts = []
        done = 0
        while done < n:
            k, i = divmod(row + done, ROWS)
            take = min(n - done, ROWS - i)
            parts.append((done, take, t[k, i : i + take, :]))
            done += take
        return parts

    def norm(pieces, count, stores):
        total = jnp.zeros((1, C), f32)
        for p in pieces:
            for _, _, v in p:
                total = total + jnp.sum(v * v, axis=0, keepdims=True)
        ms = jnp.sum(total, axis=1, keepdims=True) * (1.0 / count)
        scale = lax.rsqrt(ms + 1e-6)
        for p, store in zip(pieces, stores):
            for done, take, v in p:
                store(done, take, v * scale)

    def into(ref, k):
        def f(done, take, v):
            ref[k, done : done + take, :] = v

        return f

    norm([get(C * k, C) for k in range(9)], 9 * C * C, [into(o_mid, k) for k in range(9)])
    norm(
        [get(9 * C + V * k, V) for k in range(9)], 9 * V * C, [into(o_in, k) for k in range(9)]
    )

    def out_store(done, take, v):
        o_out[done : done + take, :] = v

    norm([get(9 * C + 9 * V, V)], V * C, [out_store])

    def noise_store(done, take, v):
        o_noise[done : done + take, :] = v

    norm([[(k, 1, t[k, ROWS : ROWS + 1, :]) for k in range(NB)]], NB * C, [noise_store])
    o_loss[...] = (t[0, ROWS + 1 : ROWS + 2, 0:128] + t[0, ROWS + 2 : ROWS + 3, 0:128]) * (1.0 / (V * 16 * 720))


def call(kernel, outs, scratch, n_smem, n_in, single=False):
    specs = [pl.BlockSpec(memory_space=pltpu.SMEM)] * n_smem
    specs += [pl.BlockSpec(memory_space=pltpu.VMEM)] * n_in
    out_specs = [pl.BlockSpec(memory_space=pltpu.VMEM)] * len(outs)
    shapes = [jax.ShapeDtypeStruct(s, d) for s, d in outs]
    return pl.pallas_call(
        kernel,
        out_shape=shapes[0] if single else shapes,
        in_specs=specs,
        out_specs=out_specs[0] if single else out_specs,
        scratch_shapes=scratch,
        compiler_params=params(),
    )


f16 = jnp.float16


def sum_all(g, e):
    xy = ("xl", "y", "xh")

    def other(z, xl, lat, xh):
        return (z, xl, lat ^ 1, xh)

    e = jnp.maximum(e, send(e, other)) + 1.0
    grow = jnp.exp2(14.0 - e)
    s = g[0] + send(g[1], other)
    row = lax.broadcasted_iota(jnp.int32, s.shape, 1)
    lane = lax.broadcasted_iota(jnp.int32, s.shape, 2)
    s = s * jnp.where((row == ROWS + 1) | (row == ROWS + 2), grow[0, 128], grow[0, 0])
    s = jnp.where(row == ROWS + 2, (s - lax.reduce_precision(s, 5, 10)) * 2.0**11, s)
    s = jnp.where(row == BR - 1, jnp.where(lane < 128, e[0, 0], e[0, 128]), s)
    got = lax.all_to_all(s.astype(f16), xy, 0, 0, tiled=True)
    s = call(plane_kernel, [((BR, C), f32)], [], 0, 1, True)(got.astype(f32))
    r1, r2, r3 = (
        send(s, lambda z, xl, lat, xh, k=k: (z ^ k, xl, lat, xh)) for k in (1, 2, 3)
    )
    s = (s + r1) + (r2 + r3)
    far = send(s, lambda z, xl, lat, xh: (7 - z, xl, lat, xh))
    s = call(scale_kernel, [((BR, C), f32)], [], 0, 2, True)(s, far).astype(f16)
    half = lax.all_to_all(jnp.broadcast_to(s[None], (16,) + s.shape), xy, 0, 0, tiled=True)
    far = send(half, other)
    return half.astype(f32), far.astype(f32)


def body(state, target, land, seeds, w_in, w_mid, w_out, w_noise):
    z = lax.axis_index("z")
    xl = lax.axis_index("xl")
    core = lax.axis_index("c")
    lat = lax.axis_index("y") * 2 + core
    member = z * 2 + xl
    info = jnp.stack([member, (45 * member) // 2, member % 2, lat, core]).astype(jnp.int32)
    near = [
        send(
            seeds,
            lambda z, xl, lat, xh, k=k: (z ^ (2 * (lat % 4) + xh), xl ^ k, lat, xh),
        )
        for k in range(2)
    ]
    x, edge = call(
        prep_kernel, [((2, 384, 256), f32), ((2, 16, 256), f32)],
        [pltpu.VMEM((128, 384), f32)], 0, 3,
    )(state, target, land)
    edge = jnp.concatenate([edge.reshape(32, 256), jnp.pad(
        jnp.concatenate(near, axis=0).astype(f32), ((0, 6), (0, 224)))], axis=0)
    edge = send(edge, lambda z, xl, lat, xh: (z, xl, lat, xh ^ 1))
    win = call(window_kernel, [((80, 256), bf16)], [], 1, 4, True)(info, x, edge, *near)
    n2, n1, s1, s2 = (lat_shift(win, d) for d in (2, 1, -1, -2))
    g, e = call(
        main_kernel, [((2, 16, BR, C), f32), ((8, 256), f32)],
        [
            pltpu.VMEM((264, 128), f32),
            pltpu.VMEM((264, 128), f32),
            pltpu.VMEM((3, 256, 128), bf16),
            pltpu.VMEM((192, C), f32),
            pltpu.VMEM((164 * M, C), bf16),
            pltpu.VMEM((108 * M, C), bf16),
            pltpu.VMEM((108 * M, C), f32),
            pltpu.VMEM((108 * M, C), f32),
            pltpu.VMEM((108 * M, 128), f32),
            pltpu.VMEM((108 * M, 128), bf16),
            pltpu.VMEM((112 * M, C), bf16),
            pltpu.VMEM((54 * M, C), f32),
            pltpu.VMEM((64, C), f32),
            pltpu.VMEM((264, 128), f32),
            pltpu.VMEM((M, C), f32),
            pltpu.VMEM((32, 128), f32),
            pltpu.VMEM((M, 128), f32),
        ],
        1, 9,
    )(info, n2, n1, win, s1, s2, w_in, w_mid, w_out, w_noise)
    half, far = sum_all(g, e)
    o_in, o_mid, o_out, o_noise, o_loss = call(
        final_kernel,
        [((9, V, C), f32), ((9, C, C), f32), ((V, C), f32), ((NB, C), f32), ((1, 128), f32)],
        [pltpu.VMEM((NB, BR, C), f32)], 1, 2,
    )(info, half, far)
    return o_in, o_mid, o_out, o_noise, o_loss[0, 0]


def solution(mesh):
    fine = Mesh(mesh.devices.reshape(8, 2, 4, 2, 2), AX)
    lat = ("y", "c")
    placed = (
        P(None, lat, "xh"), P(None, lat, "xh"), P(lat, "xh"), P(("z", "xl"), None),
        P(), P(), P(), P(),
    )
    return jax.shard_map(
        body, mesh=fine, in_specs=placed, out_specs=(P(), P(), P(), P(), P()), check_vma=False
    )
```

```python
import jax
import jax.numpy as jnp
from jax import lax
from jax.experimental import pallas as pl
from jax.experimental.pallas import tpu as pltpu
from jax.sharding import Mesh, PartitionSpec as P

f32 = jnp.float32
bf16 = jnp.bfloat16
SQ = 0.0625
GC = 0.7978845608028654
GA = 0.044715
V = 100
C = 256
M = 16
TC = 360
WP = 32
WH = 27
ROWS = 104
BR = 112
NB = 32
AX = ("z", "xl", "y", "c", "xh")
VMEM = 56 * 1024 * 1024


def perm(f):
    out = []
    for i in range(256):
        z, xl, lat, xh = i >> 5, (i >> 4) & 1, (i >> 1) & 7, i & 1
        z2, xl2, lat2, xh2 = f(z, xl, lat, xh)
        out.append((i, (z2 % 8) * 32 + xl2 * 16 + lat2 * 2 + xh2))
    return out


def send(v, f):
    return lax.ppermute(v, AX, perm(f))


def lat_shift(v, d):
    def f(z, xl, lat, xh):
        return (z, xl, (lat + d) % 8, xh)

    return send(v, f)


def member_index():
    return lax.axis_index("z") * 2 + lax.axis_index("xl")


def lat_index():
    return lax.axis_index("y") * 2 + lax.axis_index("c")


def params():
    return pltpu.CompilerParams(vmem_limit_bytes=VMEM)


def gelu(x):
    t = jnp.tanh(GC * (x + GA * x * x * x))
    return 0.5 * x * (1.0 + t)


def gelu_both(x):
    x2 = x * x
    t = jnp.tanh(GC * (x + GA * x2 * x))
    h = 0.5 * (1.0 + t)
    slope = h + 0.5 * x * (1.0 - t * t) * (GC * (1.0 + 3.0 * GA * x2))
    return x * h, slope


def gelu_slope(x):
    return gelu_both(x)[1]


def prep_kernel(state, target, land, seeds, x_out, edge_out, seeds_out, sc):
    sc[...] = jnp.zeros(sc.shape, f32)
    edge_out[...] = jnp.zeros(edge_out.shape, f32)
    seeds_out[...] = jnp.broadcast_to(seeds[...], seeds_out.shape)
    for r in range(2):
        x_out[r, 0:8, :] = jnp.zeros((8, 256), f32)
        x_out[r, 8 + TC : 384, :] = jnp.zeros((376 - TC, 256), f32)
        sc[0:V, 0:TC] = state[:, r, :].astype(f32)
        sc[104:105, 0:TC] = 1.0 + land[r : r + 1, :].astype(f32)
        x_out[r, 8 : 8 + TC, 0:128] = sc[...].T[0:TC]
        sc[0:V, 0:TC] = target[:, r, :].astype(f32)
        x_out[r, 8 : 8 + TC, 128:256] = sc[...].T[0:TC]
        edge_out[16 * r : 16 * r + 3, :] = x_out[r, TC + 5 : TC + 8, :]
        edge_out[16 * r + 10 : 16 * r + 13, :] = x_out[r, 8:11, :]


def window_kernel(x, edge, win):
    m = member_index()
    start = (45 * m) // 2
    row = lax.broadcasted_iota(jnp.int32, (16, 256), 0)
    low = (row < 3) & (m == 0)
    high = (row >= 10) & (row < 13) & (m == M - 1)
    for r in range(2):
        base = pl.multiple_of(((start + 5) // 8) * 8, 8)
        near = x[r, pl.ds(base, WP + 8), :]
        w = pltpu.roll(near, WP + 8 - (start + 5 - base), 0)[0:WP]
        e = edge[16 * r : 16 * r + 16, :]
        win[WP * r : WP * r + 16, :] = jnp.where(low, e, w[0:16]).astype(bf16)
        win[WP * r + 16 : WP * r + 32, :] = jnp.where(high, e, w[16:32]).astype(bf16)


def main_kernel(
    n2, n1, own, s1, s2, seeds, w_in, w_mid, w_out, w_noise, mine_out, theirs_out, e_out,
    S, T, SB, PB, HID, HO, SL, UP, OUT, DO, DM, INC, DS, QB, BIAS, g_out, sems,
):
    own22 = member_index() % 2
    lat = lat_index()
    core = lax.axis_index("c")
    rows = ((n2, 1, -2), (n1, 0, -1), (n1, 1, -1), (own, 0, 0), (own, 1, 0),
            (s1, 0, 1), (s1, 1, 1), (s2, 0, 2))
    for k, (ref, r, d) in enumerate(rows):
        inside = (lat + d >= 0) & (lat + d < 8)
        row = ref[WP * r : WP * r + WP, :].astype(f32) * jnp.where(inside, 1.0, 0.0)
        S[WP * k : WP * k + WP, :] = row[:, 0:128]
        T[WP * k : WP * k + WP, :] = row[:, 128:256]
    S[256:264, :] = jnp.zeros((8, 128), f32)
    T[256:264, :] = jnp.zeros((8, 128), f32)
    QB[...] = jnp.broadcast_to(S[:, 104:105], QB.shape)
    for b in range(3):
        SB[b] = S[b : b + 256, :].astype(bf16)
    latents = (seeds[...].astype(f32) - 32767.5) / 18918.0
    BIAS[...] = jnp.dot(
        latents, w_noise[...], precision=lax.Precision.HIGHEST, preferred_element_type=f32
    )
    acc = None
    for a in range(3):
        for b in range(3):
            part = jnp.dot(
                SB[b, a * 32 : a * 32 + 192, 0:V], w_in[3 * a + b], preferred_element_type=f32
            )
            acc = part if acc is None else acc + part
    PB[...] = acc

    bias = BIAS[...]
    HID[162 * M : 164 * M, :] = jnp.zeros((2 * M, C), bf16)
    for r in range(6):
        gr = lat * 2 - 2 + r
        valid = jnp.where((gr >= 0) & (gr < 16), 1.0, 0.0).astype(f32)

        def hid_cell(i, carry, r=r, valid=valid):
            row = PB[pl.ds(r * 32 + i, 1), :]
            h = gelu(jnp.broadcast_to(row, (M, C)) + bias) * valid
            HID[pl.ds(pl.multiple_of((r * WH + i) * M, M), M), :] = h.astype(bf16)
            return carry

        lax.fori_loop(0, WH, hid_cell, 0, unroll=9)

    NR = WH * M

    def mid_row(r, carry):
        lhs = jnp.concatenate(
            [
                HID[pl.ds(pl.multiple_of(((r + a) * WH + b) * M, M), NR), :]
                for a in range(3)
                for b in range(3)
            ],
            axis=1,
        )
        pre = jnp.dot(lhs, w_mid[...].reshape(9 * C, C), preferred_element_type=f32)
        act, slope = gelu_both(pre)
        hid = HID[pl.ds(pl.multiple_of(((r + 1) * WH + 1) * M, M), NR), :].astype(f32)
        base = pl.multiple_of(r * NR, M)
        ho = (act + hid).astype(bf16)
        HO[pl.ds(base, NR), :] = ho
        SL[pl.ds(base, NR), :] = slope
        OUT[pl.ds(base, NR), 0:V] = lax.dot_general(
            ho, w_out[...], (((1,), (1,)), ((), ())), preferred_element_type=f32
        )
        return carry

    lax.fori_loop(0, 4, mid_row, 0)

    def cell_terms(r, i, with_loss):
        base = pl.multiple_of((r * WH + i) * M, M)
        srow = (r + 2) * 32 + i + 2
        st = S[pl.ds(srow, 1), :]
        tg = T[pl.ds(srow, 1), :]
        q = QB[pl.ds(srow, 1), :]
        o = (OUT[pl.ds(base, M), :] + st).astype(bf16).astype(f32)
        miss = o - tg
        e = miss * miss + SQ
        inv = lax.rsqrt(e)
        slope = miss * inv
        dist = e * inv - 0.25 if with_loss else None
        total = None
        spread = None
        for k in range(1, 9):
            u = o - pltpu.roll(o, k, 0)
            e = u * u + SQ
            inv = lax.rsqrt(e)
            s = u * inv
            if k < 8:
                s = s - pltpu.roll(s, M - k, 0)
            total = s if total is None else total + s
            if with_loss:
                d = e * inv - 0.25
                if k == 8:
                    d = 0.5 * d
                spread = d if spread is None else spread + d
        g = q * (slope * (1.0 / M) - total * (1.0 / (M * (M - 1))))
        DO[pl.ds(base, M), :] = g.astype(bf16)
        if with_loss:
            return q * (dist * (1.0 / M) - spread * (1.0 / (M * (M - 1))))
        return None

    loss = jnp.zeros((M, 128), f32)
    for r in (1, 2):

        def loss_cell(i, total, r=r):
            term = cell_terms(r, i, True)
            mine = (i >= 1) & ((i < 23) | ((i == 23) & (own22 > 0)))
            return total + jnp.where(mine, 1.0, 0.0) * term

        loss = lax.fori_loop(0, WH, loss_cell, loss, unroll=3)
    for r in (0, 3):

        def grad_cell(i, carry, r=r):
            cell_terms(r, i, False)
            return carry

        lax.fori_loop(0, WH, grad_cell, 0, unroll=3)
    lane = lax.broadcasted_iota(jnp.int32, (M, 128), 1)
    loss = jnp.sum(jnp.sum(jnp.where(lane < V, loss, 0.0), axis=0, keepdims=True), axis=1, keepdims=True)

    def up_row(r, carry):
        base = pl.multiple_of(r * NR, M)
        up = jnp.dot(DO[pl.ds(base, NR), 0:V], w_out[...], preferred_element_type=f32)
        UP[pl.ds(base, NR), :] = up
        DM[pl.ds(base, NR), :] = (up * SL[pl.ds(base, NR), :]).astype(bf16)
        return carry

    lax.fori_loop(0, 4, up_row, 0)
    DM[108 * M : 112 * M, :] = jnp.zeros((4 * M, C), bf16)

    wcat = jnp.concatenate([w_mid[t] for t in range(9)], axis=1)
    for r in range(2):
        lhs = jnp.concatenate(
            [
                DM[((r + 2 - a) * WH + 2 - b) * M : ((r + 2 - a) * WH + 2 - b) * M + NR, :]
                for a in range(3)
                for b in range(3)
            ],
            axis=1,
        )
        INC[r * NR : (r + 1) * NR, :] = lax.dot_general(
            lhs, wcat, (((1,), (1,)), ((), ())), preferred_element_type=f32
        )
    DS[...] = jnp.zeros(DS.shape, f32)
    dsum = jnp.zeros((M, C), f32)
    for r in range(2):

        def in_cell(i, total, r=r):
            x = jnp.broadcast_to(PB[pl.ds((r + 2) * 32 + i + 2, 1), :], (M, C)) + bias
            base = pl.multiple_of((r * WH + i) * M, M)
            upb = pl.multiple_of(((r + 1) * WH + 1 + i) * M, M)
            d = (INC[pl.ds(base, M), :] + UP[pl.ds(upb, M), :]) * gelu_slope(x)
            mine = jnp.where((i < 22) | (own22 > 0), 1.0, 0.0)
            d = d.astype(bf16).astype(f32) * mine
            DS[pl.ds(r * 32 + i + 2, 1), :] = jnp.sum(d, axis=0, keepdims=True)
            return total + d

        dsum = lax.fori_loop(0, 23, in_cell, dsum)

    def store(k, lo, hi, value):
        g_out[(k // 16) ^ core, k % 16, lo:hi, :] = value

    g_out[:, :, ROWS:BR, :] = jnp.zeros((2, 16, BR - ROWS, C), f32)
    peaks = []

    def put(row, value):
        done = 0
        n = value.shape[0]
        peaks.append(jnp.max(jnp.abs(value), axis=0, keepdims=True))
        while done < n:
            k, i = divmod(row + done, ROWS)
            take = min(n - done, ROWS - i)
            store(k, i, i + take, value[done : done + take, :])
            done += take

    cell = lax.broadcasted_iota(jnp.int32, (NR, C), 0) >> 4
    mine = (cell < 22) | ((cell == 22) & (own22 > 0))
    start = (WH + 1) * M
    dmc = jnp.concatenate(
        [
            jnp.where(mine, DM[start + r * NR : start + (r + 1) * NR, :].astype(f32), 0.0)
            for r in range(2)
        ],
        axis=0,
    )
    dmt = dmc.T.astype(bf16)
    for a in range(3):
        for b in range(3):
            hs = ((a + 1) * WH + b + 1) * M
            g = jnp.dot(dmt, HID[hs : hs + 2 * NR, :], preferred_element_type=f32)
            put((3 * a + b) * C, g.T)
    doc = jnp.concatenate(
        [
            jnp.where(
                mine[:, 0:128], DO[start + r * NR : start + (r + 1) * NR, :].astype(f32), 0.0
            )
            for r in range(2)
        ],
        axis=0,
    )
    dot_ = doc.T.astype(bf16)
    go = jnp.dot(dot_, HO[start : start + 2 * NR, :], preferred_element_type=f32)
    ds = DS[...]
    hi = ds.astype(bf16)
    lo = (ds - hi.astype(f32)).astype(bf16)
    both = jnp.concatenate([hi, lo], axis=1)
    for a in range(3):
        for b in range(3):
            g = lax.dot_general(
                SB[b, (a + 2) * 32 : (a + 2) * 32 + 64, :], both,
                (((0,), (0,)), ((), ())), preferred_element_type=f32,
            )
            put(9 * C + V * (3 * a + b), (g[:, 0:C] + g[:, C : 2 * C])[0:V, :])
    put(9 * C + 9 * V, go[0:V, :])
    put(9 * C + 10 * V, jnp.zeros((NB * ROWS - 9 * C - 10 * V, C), f32))
    gn = lax.dot_general(
        latents, dsum, (((0,), (0,)), ((), ())),
        precision=lax.Precision.HIGHEST, preferred_element_type=f32,
    )
    peaks.append(jnp.max(jnp.abs(gn), axis=0, keepdims=True))
    for k in range(NB):
        store(k, ROWS, ROWS + 1, gn[k : k + 1, :])
    loss = jnp.broadcast_to(loss * (1.0 / (V * 16 * 720)), (1, C))
    first = loss.astype(bf16).astype(f32)
    store(0, ROWS + 1, ROWS + 2, first)
    store(0, ROWS + 2, ROWS + 3, loss - first)
    peaks.append(jnp.abs(loss))
    peak = peaks[0]
    for p in peaks[1:]:
        peak = jnp.maximum(peak, p)
    peak = jnp.broadcast_to(jnp.max(peak, axis=1, keepdims=True), (8, C))
    e_out[...] = exponent(peak)
    moves = [
        pltpu.make_async_copy(g_out.at[i], ref, sems.at[i])
        for i, ref in enumerate((mine_out, theirs_out))
    ]
    for move in moves:
        move.start()
    for move in moves:
        move.wait()


def exponent(bound):
    return jnp.ceil(jnp.log2(jnp.maximum(bound, 1e-30)))


def final_kernel(half, far, o_in, o_mid, o_out, o_noise, o_loss, t, u, in_sems, out_sems):
    core = lax.axis_index("c")
    steps = []
    for i, (slot, ref) in enumerate(((core, half), (1 - core, far))):
        for j in range(4):
            first = slot * 16 + 4 * j
            move = pltpu.make_async_copy(
                ref.at[pl.ds(4 * j, 4)], t.at[pl.ds(first, 4)], in_sems.at[4 * i + j]
            )
            move.start()
            steps.append((first, move))
    for first, move in steps:
        move.wait()
        for k in range(4):
            f = jnp.exp2(t[first + k, BR - 1 : BR, :] - 14.0)
            t[first + k] = t[first + k] * f

    def get(row, n):
        parts = []
        done = 0
        while done < n:
            k, i = divmod(row + done, ROWS)
            take = min(n - done, ROWS - i)
            parts.append((done, take, k, i))
            done += take
        return parts

    def scale_of(pieces, count):
        total = jnp.zeros((8, C), f32)
        ragged = jnp.zeros((1, C), f32)
        for p in pieces:
            for _, take, k, i in p:
                v = t[k, i : i + take, :]
                v = v * v
                if take % 8 == 0:
                    total = total + jnp.sum(v.reshape(take // 8, 8, C), axis=0)
                else:
                    ragged = ragged + jnp.sum(v, axis=0, keepdims=True)
        total = jnp.sum(total, axis=0, keepdims=True) + ragged
        ms = jnp.sum(total, axis=1, keepdims=True) * (1.0 / count)
        return lax.rsqrt(ms + 1e-6)

    moves = []

    def emit(pieces, scale, buf, out, k):
        for done, take, b, i in pieces:
            buf[done : done + take, :] = t[b, i : i + take, :] * scale
        if out is not None:
            move = pltpu.make_async_copy(buf, out, out_sems.at[k])
            move.start()
            moves.append(move)

    pieces = [get(C * k, C) for k in range(9)]
    scale = scale_of(pieces, 9 * C * C)
    for k in range(9):
        emit(pieces[k], scale, u.at[k], o_mid.at[k], k)
    pieces = [get(9 * C + V * k, V) for k in range(9)]
    scale = scale_of(pieces, 9 * V * C)
    for k in range(9):
        emit(pieces[k], scale, o_in.at[k], None, 0)
    pieces = get(9 * C + 9 * V, V)
    emit(pieces, scale_of([pieces], V * C), o_out, None, 0)
    pieces = [(k, 1, k, ROWS) for k in range(NB)]
    emit(pieces, scale_of([pieces], NB * C), o_noise, None, 0)
    o_loss[...] = t[0, ROWS + 1 : ROWS + 2, 0:128] + t[0, ROWS + 2 : ROWS + 3, 0:128]
    for move in moves:
        move.wait()


def call(kernel, outs, scratch, ins, place=None):
    place = place or {}
    vmem = pl.BlockSpec(memory_space=pltpu.VMEM)
    left = pl.BlockSpec(memory_space=pl.ANY)
    return pl.pallas_call(
        kernel,
        out_shape=[jax.ShapeDtypeStruct(s, d) for s, d in outs],
        in_specs=[left if ("in", i) in place else vmem for i in range(len(ins))],
        out_specs=[left if ("out", i) in place else vmem for i in range(len(outs))],
        scratch_shapes=scratch,
        compiler_params=params(),
    )(*ins)


f16 = jnp.float16


def sum_all(mine, theirs, e):
    xy = ("xl", "y", "xh")

    def other(z, xl, lat, xh):
        return (z, xl, lat ^ 1, xh)

    e = (jnp.maximum(e, send(e, other)) + 1.0)[0:1]
    last = (jnp.arange(BR, dtype=jnp.int32) == BR - 1)[:, None]
    tag = jnp.where(last, e, 0.0)
    s = (mine + send(theirs, other)) * jnp.exp2(14.0 - e)[None] + tag[None]
    got = lax.all_to_all(s.astype(f16), xy, 0, 0, tiled=True)
    q = jnp.exp2(got[:, BR - 1 : BR, :].astype(f32) - 14.0)
    s = jnp.sum(jnp.where(last[None], 2.0**14, got.astype(f32)) * q, axis=0)
    r1, r2, r3 = (
        send(s, lambda z, xl, lat, xh, k=k: (z ^ k, xl, lat, xh)) for k in (1, 2, 3)
    )
    s = (s + r1) + (r2 + r3)
    s = s + send(s, lambda z, xl, lat, xh: (7 - z, xl, lat, xh))
    e = exponent(s[BR - 1 : BR, :])
    s = jnp.where(last, e, s * jnp.exp2(14.0 - e)).astype(f16)
    half = lax.all_to_all(jnp.broadcast_to(s[None], (16,) + s.shape), xy, 0, 0, tiled=True)
    far = send(half, other)
    return half.astype(f32), far.astype(f32)


def body(state, target, land, seeds, w_in, w_mid, w_out, w_noise):
    x, edge, seeds = call(
        prep_kernel, [((2, 384, 256), f32), ((32, 256), f32), ((M, 32), jnp.int32)],
        [pltpu.VMEM((128, 384), f32)], (state, target, land, seeds),
    )
    edge = send(edge, lambda z, xl, lat, xh: (z, xl, lat, xh ^ 1))
    seeds = lax.all_to_all(seeds, ("z", "xl"), 0, 0, tiled=True)
    (win,) = call(window_kernel, [((2 * WP, 256), bf16)], [], (x, edge))
    win, seeds = lax.optimization_barrier((win, seeds))
    n2, n1, s1, s2 = (lat_shift(win, d) for d in (2, 1, -1, -2))
    mine, theirs, e = call(
        main_kernel, [((16, BR, C), f32), ((16, BR, C), f32), ((8, C), f32)],
        [
            pltpu.VMEM((264, 128), f32),
            pltpu.VMEM((264, 128), f32),
            pltpu.VMEM((3, 256, 128), bf16),
            pltpu.VMEM((192, C), f32),
            pltpu.VMEM((164 * M, C), bf16),
            pltpu.VMEM((108 * M, C), bf16),
            pltpu.VMEM((108 * M, C), f32),
            pltpu.VMEM((108 * M, C), f32),
            pltpu.VMEM((108 * M, 128), f32),
            pltpu.VMEM((108 * M, 128), bf16),
            pltpu.VMEM((112 * M, C), bf16),
            pltpu.VMEM((54 * M, C), f32),
            pltpu.VMEM((64, C), f32),
            pltpu.VMEM((264, 128), f32),
            pltpu.VMEM((M, C), f32),
            pltpu.VMEM((2, 16, BR, C), f32),
            pltpu.SemaphoreType.DMA((2,)),
        ],
        (n2, n1, win, s1, s2, seeds, w_in, w_mid, w_out, w_noise),
        {("out", 0), ("out", 1)},
    )
    half, far = sum_all(mine, theirs, e)
    o_in, o_mid, o_out, o_noise, o_loss = call(
        final_kernel,
        [((9, V, C), f32), ((9, C, C), f32), ((V, C), f32), ((NB, C), f32), ((1, 128), f32)],
        [
            pltpu.VMEM((NB, BR, C), f32),
            pltpu.VMEM((9, C, C), f32),
            pltpu.SemaphoreType.DMA((8,)),
            pltpu.SemaphoreType.DMA((9,)),
        ],
        (half, far),
        {("in", 0), ("in", 1), ("out", 1)},
    )
    return o_in, o_mid, o_out, o_noise, o_loss[0, 0]


def solution(mesh):
    fine = Mesh(mesh.devices.reshape(8, 2, 4, 2, 2), AX)
    lat = ("y", "c")
    placed = (
        P(None, lat, "xh"), P(None, lat, "xh"), P(lat, "xh"), P(("z", "xl"), None),
        P(), P(), P(), P(),
    )
    return jax.shard_map(
        body, mesh=fine, in_specs=placed, out_specs=(P(), P(), P(), P(), P()), check_vma=False
    )
```

```python
import jax
import jax.numpy as jnp
from jax import lax
from jax.experimental import pallas as pl
from jax.experimental.pallas import tpu as pltpu
from jax.sharding import Mesh, PartitionSpec as P

f32 = jnp.float32
bf16 = jnp.bfloat16
SQ = 0.0625
GC = 0.7978845608028654
GA = 0.044715
V = 100
C = 256
M = 16
TC = 360
WP = 32
WH = 27
ROWS = 104
BR = 112
NB = 32
AX = ("z", "xl", "y", "c", "xh")


def perm(f):
    out = []
    for i in range(256):
        z, xl, lat, xh = i >> 5, (i >> 4) & 1, (i >> 1) & 7, i & 1
        z2, xl2, lat2, xh2 = f(z, xl, lat, xh)
        out.append((i, (z2 % 8) * 32 + xl2 * 16 + lat2 * 2 + xh2))
    return out


def send(v, f):
    return lax.ppermute(v, AX, perm(f))


def lat_shift(v, d):
    def f(z, xl, lat, xh):
        return (z, xl, (lat + d) % 8, xh)

    return send(v, f)


def member_index():
    return lax.axis_index("z") * 2 + lax.axis_index("xl")


def lat_index():
    return lax.axis_index("y") * 2 + lax.axis_index("c")


def params(limit=None):
    return pltpu.CompilerParams(vmem_limit_bytes=(limit or 16) * 1024 * 1024)


def gelu(x):
    t = jnp.tanh(GC * (x + GA * x * x * x))
    return 0.5 * x * (1.0 + t)


def gelu_both(x):
    x2 = x * x
    t = jnp.tanh(GC * (x + GA * x2 * x))
    h = 0.5 * (1.0 + t)
    slope = h + 0.5 * x * (1.0 - t * t) * (GC * (1.0 + 3.0 * GA * x2))
    return x * h, slope


def gelu_slope(x):
    return gelu_both(x)[1]


def prep_kernel(
    state, target, land, seeds, w_in, w_out, w_noise,
    x_out, edge_out, seeds_out, w_in_out, w_out_out, w_noise_out, sc, sems,
):
    moves = [
        pltpu.make_async_copy(w, out, sems.at[i])
        for i, (w, out) in enumerate(((w_in, w_in_out), (w_out, w_out_out), (w_noise, w_noise_out)))
    ]
    for move in moves:
        move.start()
    sc[...] = jnp.zeros(sc.shape, f32)
    edge_out[...] = jnp.zeros(edge_out.shape, f32)
    seeds_out[...] = jnp.broadcast_to(seeds[...], seeds_out.shape)
    for r in range(2):
        x_out[r, 0:8, :] = jnp.zeros((8, 256), f32)
        x_out[r, 8 + TC : 384, :] = jnp.zeros((376 - TC, 256), f32)
        sc[0:V, 0:TC] = state[:, r, :].astype(f32)
        sc[104:105, 0:TC] = 1.0 + land[r : r + 1, :].astype(f32)
        x_out[r, 8 : 8 + TC, 0:128] = sc[...].T[0:TC]
        sc[0:V, 0:TC] = target[:, r, :].astype(f32)
        x_out[r, 8 : 8 + TC, 128:256] = sc[...].T[0:TC]
        edge_out[16 * r : 16 * r + 3, :] = x_out[r, TC + 5 : TC + 8, :]
        edge_out[16 * r + 10 : 16 * r + 13, :] = x_out[r, 8:11, :]
    for move in moves:
        move.wait()


def window_kernel(x, edge, win):
    m = member_index()
    start = (45 * m) // 2
    row = lax.broadcasted_iota(jnp.int32, (16, 256), 0)
    low = (row < 3) & (m == 0)
    high = (row >= 10) & (row < 13) & (m == M - 1)
    for r in range(2):
        base = pl.multiple_of(((start + 5) // 8) * 8, 8)
        near = x[r, pl.ds(base, WP + 8), :]
        w = pltpu.roll(near, WP + 8 - (start + 5 - base), 0)[0:WP]
        e = edge[16 * r : 16 * r + 16, :]
        win[WP * r : WP * r + 16, :] = jnp.where(low, e, w[0:16]).astype(bf16)
        win[WP * r + 16 : WP * r + 32, :] = jnp.where(high, e, w[16:32]).astype(bf16)


def main_kernel(
    n2, n1, own, s1, s2, seeds, w_in, w_mid, w_out, w_noise, g_out, e_out,
    S, T, SB, PB, HID, HO, SL, UP, OUT, DO, DM, INC, DS, QB, BIAS,
):
    own22 = member_index() % 2
    lat = lat_index()
    core = lax.axis_index("c")
    rows = ((n2, 1, -2), (n1, 0, -1), (n1, 1, -1), (own, 0, 0), (own, 1, 0),
            (s1, 0, 1), (s1, 1, 1), (s2, 0, 2))
    for k, (ref, r, d) in enumerate(rows):
        inside = (lat + d >= 0) & (lat + d < 8)
        row = ref[WP * r : WP * r + WP, :].astype(f32) * jnp.where(inside, 1.0, 0.0)
        S[WP * k : WP * k + WP, :] = row[:, 0:128]
        T[WP * k : WP * k + WP, :] = row[:, 128:256]
    S[256:264, :] = jnp.zeros((8, 128), f32)
    T[256:264, :] = jnp.zeros((8, 128), f32)
    QB[...] = jnp.broadcast_to(S[:, 104:105], QB.shape)
    for b in range(3):
        SB[b] = S[b : b + 256, :].astype(bf16)
    latents = (seeds[...].astype(f32) - 32767.5) / 18918.0
    BIAS[...] = jnp.dot(
        latents, w_noise[...], precision=lax.Precision.HIGHEST, preferred_element_type=f32
    )
    acc = None
    for a in range(3):
        for b in range(3):
            part = jnp.dot(
                SB[b, a * 32 : a * 32 + 192, 0:V], w_in[3 * a + b], preferred_element_type=f32
            )
            acc = part if acc is None else acc + part
    PB[...] = acc

    bias = BIAS[...]
    HID[162 * M : 164 * M, :] = jnp.zeros((2 * M, C), bf16)
    for r in range(6):
        gr = lat * 2 - 2 + r
        valid = jnp.where((gr >= 0) & (gr < 16), 1.0, 0.0).astype(f32)

        def hid_cell(i, carry, r=r, valid=valid):
            row = PB[pl.ds(r * 32 + i, 1), :]
            h = gelu(jnp.broadcast_to(row, (M, C)) + bias) * valid
            HID[pl.ds(pl.multiple_of((r * WH + i) * M, M), M), :] = h.astype(bf16)
            return carry

        lax.fori_loop(0, WH, hid_cell, 0, unroll=9)

    NR = WH * M

    def mid_row(r, carry):
        lhs = jnp.concatenate(
            [
                HID[pl.ds(pl.multiple_of(((r + a) * WH + b) * M, M), NR), :]
                for a in range(3)
                for b in range(3)
            ],
            axis=1,
        )
        pre = jnp.dot(lhs, w_mid[...].reshape(9 * C, C), preferred_element_type=f32)
        act, slope = gelu_both(pre)
        hid = HID[pl.ds(pl.multiple_of(((r + 1) * WH + 1) * M, M), NR), :].astype(f32)
        base = pl.multiple_of(r * NR, M)
        ho = (act + hid).astype(bf16)
        HO[pl.ds(base, NR), :] = ho
        SL[pl.ds(base, NR), :] = slope
        OUT[pl.ds(base, NR), 0:V] = lax.dot_general(
            ho, w_out[...], (((1,), (1,)), ((), ())), preferred_element_type=f32
        )
        return carry

    lax.fori_loop(0, 4, mid_row, 0)

    def cell_terms(r, i, with_loss):
        base = pl.multiple_of((r * WH + i) * M, M)
        srow = (r + 2) * 32 + i + 2
        st = S[pl.ds(srow, 1), :]
        tg = T[pl.ds(srow, 1), :]
        q = QB[pl.ds(srow, 1), :]
        o = (OUT[pl.ds(base, M), :] + st).astype(bf16).astype(f32)
        miss = o - tg
        e = miss * miss + SQ
        inv = lax.rsqrt(e)
        slope = miss * inv
        dist = e * inv - 0.25 if with_loss else None
        total = None
        spread = None
        for k in range(1, 9):
            u = o - pltpu.roll(o, k, 0)
            e = u * u + SQ
            inv = lax.rsqrt(e)
            s = u * inv
            if k < 8:
                s = s - pltpu.roll(s, M - k, 0)
            total = s if total is None else total + s
            if with_loss:
                d = e * inv - 0.25
                if k == 8:
                    d = 0.5 * d
                spread = d if spread is None else spread + d
        g = q * (slope * (1.0 / M) - total * (1.0 / (M * (M - 1))))
        DO[pl.ds(base, M), :] = g.astype(bf16)
        if with_loss:
            return q * (dist * (1.0 / M) - spread * (1.0 / (M * (M - 1))))
        return None

    loss = jnp.zeros((M, 128), f32)
    for r in (1, 2):

        def loss_cell(i, total, r=r):
            term = cell_terms(r, i, True)
            mine = (i >= 1) & ((i < 23) | ((i == 23) & (own22 > 0)))
            return total + jnp.where(mine, 1.0, 0.0) * term

        loss = lax.fori_loop(0, WH, loss_cell, loss, unroll=3)
    for r in (0, 3):

        def grad_cell(i, carry, r=r):
            cell_terms(r, i, False)
            return carry

        lax.fori_loop(0, WH, grad_cell, 0, unroll=3)
    lane = lax.broadcasted_iota(jnp.int32, (M, 128), 1)
    loss = jnp.sum(jnp.sum(jnp.where(lane < V, loss, 0.0), axis=0, keepdims=True), axis=1, keepdims=True)

    def up_row(r, carry):
        base = pl.multiple_of(r * NR, M)
        up = jnp.dot(DO[pl.ds(base, NR), 0:V], w_out[...], preferred_element_type=f32)
        UP[pl.ds(base, NR), :] = up
        DM[pl.ds(base, NR), :] = (up * SL[pl.ds(base, NR), :]).astype(bf16)
        return carry

    lax.fori_loop(0, 4, up_row, 0)
    DM[108 * M : 112 * M, :] = jnp.zeros((4 * M, C), bf16)

    wcat = jnp.concatenate([w_mid[t] for t in range(9)], axis=1)
    for r in range(2):
        lhs = jnp.concatenate(
            [
                DM[((r + 2 - a) * WH + 2 - b) * M : ((r + 2 - a) * WH + 2 - b) * M + NR, :]
                for a in range(3)
                for b in range(3)
            ],
            axis=1,
        )
        INC[r * NR : (r + 1) * NR, :] = lax.dot_general(
            lhs, wcat, (((1,), (1,)), ((), ())), preferred_element_type=f32
        )
    DS[...] = jnp.zeros(DS.shape, f32)
    dsum = jnp.zeros((M, C), f32)
    for r in range(2):

        def in_cell(i, total, r=r):
            x = jnp.broadcast_to(PB[pl.ds((r + 2) * 32 + i + 2, 1), :], (M, C)) + bias
            base = pl.multiple_of((r * WH + i) * M, M)
            upb = pl.multiple_of(((r + 1) * WH + 1 + i) * M, M)
            d = (INC[pl.ds(base, M), :] + UP[pl.ds(upb, M), :]) * gelu_slope(x)
            mine = jnp.where((i < 22) | (own22 > 0), 1.0, 0.0)
            d = d.astype(bf16).astype(f32) * mine
            DS[pl.ds(r * 32 + i + 2, 1), :] = jnp.sum(d, axis=0, keepdims=True)
            return total + d

        dsum = lax.fori_loop(0, 23, in_cell, dsum)

    def store(k, lo, hi, value):
        g_out[(k // 16) ^ core, k % 16, lo:hi, :] = value

    g_out[:, :, ROWS:BR, :] = jnp.zeros((2, 16, BR - ROWS, C), f32)
    peaks = []

    def put(row, value):
        done = 0
        n = value.shape[0]
        peaks.append(jnp.max(jnp.abs(value), axis=0, keepdims=True))
        while done < n:
            k, i = divmod(row + done, ROWS)
            take = min(n - done, ROWS - i)
            store(k, i, i + take, value[done : done + take, :])
            done += take

    cell = lax.broadcasted_iota(jnp.int32, (NR, C), 0) >> 4
    mine = (cell < 22) | ((cell == 22) & (own22 > 0))
    start = (WH + 1) * M
    dmc = jnp.concatenate(
        [
            jnp.where(mine, DM[start + r * NR : start + (r + 1) * NR, :].astype(f32), 0.0)
            for r in range(2)
        ],
        axis=0,
    )
    dmt = dmc.T.astype(bf16)
    for a in range(3):
        for b in range(3):
            hs = ((a + 1) * WH + b + 1) * M
            g = jnp.dot(dmt, HID[hs : hs + 2 * NR, :], preferred_element_type=f32)
            put((3 * a + b) * C, g.T)
    doc = jnp.concatenate(
        [
            jnp.where(
                mine[:, 0:128], DO[start + r * NR : start + (r + 1) * NR, :].astype(f32), 0.0
            )
            for r in range(2)
        ],
        axis=0,
    )
    dot_ = doc.T.astype(bf16)
    go = jnp.dot(dot_, HO[start : start + 2 * NR, :], preferred_element_type=f32)
    ds = DS[...]
    hi = ds.astype(bf16)
    lo = (ds - hi.astype(f32)).astype(bf16)
    both = jnp.concatenate([hi, lo], axis=1)
    for a in range(3):
        for b in range(3):
            g = lax.dot_general(
                SB[b, (a + 2) * 32 : (a + 2) * 32 + 64, :], both,
                (((0,), (0,)), ((), ())), preferred_element_type=f32,
            )
            put(9 * C + V * (3 * a + b), (g[:, 0:C] + g[:, C : 2 * C])[0:V, :])
    put(9 * C + 9 * V, go[0:V, :])
    put(9 * C + 10 * V, jnp.zeros((NB * ROWS - 9 * C - 10 * V, C), f32))
    gn = lax.dot_general(
        latents, dsum, (((0,), (0,)), ((), ())),
        precision=lax.Precision.HIGHEST, preferred_element_type=f32,
    )
    peaks.append(jnp.max(jnp.abs(gn), axis=0, keepdims=True))
    for k in range(NB):
        store(k, ROWS, ROWS + 1, gn[k : k + 1, :])
    loss = jnp.broadcast_to(loss * (1.0 / (V * 16 * 720)), (1, C))
    first = loss.astype(bf16).astype(f32)
    store(0, ROWS + 1, ROWS + 2, first)
    store(0, ROWS + 2, ROWS + 3, loss - first)
    peaks.append(jnp.abs(loss))
    peak = peaks[0]
    for p in peaks[1:]:
        peak = jnp.maximum(peak, p)
    peak = jnp.broadcast_to(jnp.max(peak, axis=1, keepdims=True), (8, C))
    e_out[...] = exponent(peak)


def exponent(bound):
    return jnp.ceil(jnp.log2(jnp.maximum(bound, 1e-30)))


def final_kernel(half, far, o_in, o_mid, o_out, o_noise, o_loss, t, u, out_sems):
    core = lax.axis_index("c")
    for slot, ref in ((core, half), (1 - core, far)):
        for k in range(16):
            f = jnp.exp2(ref[k, BR - 1 : BR, :] - 14.0)
            t[slot * 16 + k] = ref[k] * f

    def get(row, n):
        parts = []
        done = 0
        while done < n:
            k, i = divmod(row + done, ROWS)
            take = min(n - done, ROWS - i)
            parts.append((done, take, k, i))
            done += take
        return parts

    def scale_of(pieces, count):
        total = jnp.zeros((8, C), f32)
        ragged = jnp.zeros((1, C), f32)
        for p in pieces:
            for _, take, k, i in p:
                v = t[k, i : i + take, :]
                v = v * v
                if take % 8 == 0:
                    total = total + jnp.sum(v.reshape(take // 8, 8, C), axis=0)
                else:
                    ragged = ragged + jnp.sum(v, axis=0, keepdims=True)
        total = jnp.sum(total, axis=0, keepdims=True) + ragged
        ms = jnp.sum(total, axis=1, keepdims=True) * (1.0 / count)
        return lax.rsqrt(ms + 1e-6)

    moves = []

    def emit(pieces, scale, buf, out, k):
        for done, take, b, i in pieces:
            buf[done : done + take, :] = t[b, i : i + take, :] * scale
        if out is not None:
            move = pltpu.make_async_copy(buf, out, out_sems.at[k])
            move.start()
            moves.append(move)

    pieces = [get(C * k, C) for k in range(9)]
    scale = scale_of(pieces, 9 * C * C)
    for k in range(9):
        emit(pieces[k], scale, u.at[k], o_mid.at[k], k)
    pieces = [get(9 * C + V * k, V) for k in range(9)]
    scale = scale_of(pieces, 9 * V * C)
    for k in range(9):
        emit(pieces[k], scale, o_in.at[k], None, 0)
    pieces = get(9 * C + 9 * V, V)
    emit(pieces, scale_of([pieces], V * C), o_out, None, 0)
    pieces = [(k, 1, k, ROWS) for k in range(NB)]
    emit(pieces, scale_of([pieces], NB * C), o_noise, None, 0)
    o_loss[...] = t[0, ROWS + 1 : ROWS + 2, 0:128] + t[0, ROWS + 2 : ROWS + 3, 0:128]
    for move in moves:
        move.wait()


def call(kernel, outs, scratch, ins, place=None, kept=(), limit=None):
    place = place or {}
    vmem = pl.BlockSpec(memory_space=pltpu.VMEM)
    left = pl.BlockSpec(memory_space=pl.ANY)
    ins = [
        pltpu.with_memory_space_constraint(v, pltpu.VMEM) if i in kept else v
        for i, v in enumerate(ins)
    ]
    return pl.pallas_call(
        kernel,
        out_shape=[
            pltpu.VMEM(o[0], o[1]) if len(o) > 2 else jax.ShapeDtypeStruct(*o) for o in outs
        ],
        in_specs=[left if ("in", i) in place else vmem for i in range(len(ins))],
        out_specs=[left if ("out", i) in place else vmem for i in range(len(outs))],
        scratch_shapes=scratch,
        compiler_params=params(limit),
    )(*ins)


f16 = jnp.float16


def sum_all(mine, theirs, e):
    xy = ("xl", "y", "xh")

    def other(z, xl, lat, xh):
        return (z, xl, lat ^ 1, xh)

    e = (jnp.maximum(e, send(e, other)) + 1.0)[0:1]
    last = (jnp.arange(BR, dtype=jnp.int32) == BR - 1)[:, None]
    tag = jnp.where(last, e, 0.0)
    s = (mine + send(theirs, other)) * jnp.exp2(14.0 - e)[None] + tag[None]
    got = lax.all_to_all(s.astype(f16), xy, 0, 0, tiled=True)
    q = jnp.exp2(got[:, BR - 1 : BR, :].astype(f32) - 14.0)
    s = jnp.sum(jnp.where(last[None], 2.0**14, got.astype(f32)) * q, axis=0)
    r1, r2, r3 = (
        send(s, lambda z, xl, lat, xh, k=k: (z ^ k, xl, lat, xh)) for k in (1, 2, 3)
    )
    s = (s + r1) + (r2 + r3)
    s = s + send(s, lambda z, xl, lat, xh: (7 - z, xl, lat, xh))
    e = exponent(s[BR - 1 : BR, :])
    s = jnp.where(last, e, s * jnp.exp2(14.0 - e)).astype(f16)
    half = lax.all_to_all(jnp.broadcast_to(s[None], (16,) + s.shape), xy, 0, 0, tiled=True)
    far = send(half, other)
    return half.astype(f32), far.astype(f32)


def body(state, target, land, seeds, w_in, w_mid, w_out, w_noise):
    x, edge, seeds, w_in, w_out, w_noise = call(
        prep_kernel,
        [
            ((2, 384, 256), f32, 1), ((32, 256), f32, 1), ((M, 32), jnp.int32, 1),
            ((9, V, C), bf16, 1), ((V, C), bf16, 1), ((NB, C), f32, 1),
        ],
        [pltpu.VMEM((128, 384), f32), pltpu.SemaphoreType.DMA((3,))],
        (state, target, land, seeds, w_in, w_out, w_noise),
        {("in", 4), ("in", 5), ("in", 6)},
    )
    edge = send(edge, lambda z, xl, lat, xh: (z, xl, lat, xh ^ 1))
    seeds = lax.all_to_all(seeds, ("z", "xl"), 0, 0, tiled=True)
    (win,) = call(window_kernel, [((2 * WP, 256), bf16, 1)], [], (x, edge), kept=(0, 1))
    win, seeds = lax.optimization_barrier((win, seeds))
    n2, n1, s1, s2 = (lat_shift(win, d) for d in (2, 1, -1, -2))
    g, e = call(
        main_kernel, [((2, 16, BR, C), f32, 1), ((8, C), f32, 1)],
        [
            pltpu.VMEM((264, 128), f32),
            pltpu.VMEM((264, 128), f32),
            pltpu.VMEM((3, 256, 128), bf16),
            pltpu.VMEM((192, C), f32),
            pltpu.VMEM((164 * M, C), bf16),
            pltpu.VMEM((108 * M, C), bf16),
            pltpu.VMEM((108 * M, C), f32),
            pltpu.VMEM((108 * M, C), f32),
            pltpu.VMEM((108 * M, 128), f32),
            pltpu.VMEM((108 * M, 128), bf16),
            pltpu.VMEM((112 * M, C), bf16),
            pltpu.VMEM((54 * M, C), f32),
            pltpu.VMEM((64, C), f32),
            pltpu.VMEM((264, 128), f32),
            pltpu.VMEM((M, C), f32),
        ],
        (n2, n1, win, s1, s2, seeds, w_in, w_mid, w_out, w_noise),
        kept=(0, 1, 2, 3, 4, 5, 6, 8, 9),
        limit=32,
    )
    half, far = sum_all(g[0], g[1], e)
    o_in, o_mid, o_out, o_noise, o_loss = call(
        final_kernel,
        [((9, V, C), f32), ((9, C, C), f32), ((V, C), f32), ((NB, C), f32), ((1, 128), f32)],
        [
            pltpu.VMEM((NB, BR, C), f32),
            pltpu.VMEM((9, C, C), f32),
            pltpu.SemaphoreType.DMA((9,)),
        ],
        (half, far),
        {("out", 1)},
        kept=(0, 1),
    )
    return o_in, o_mid, o_out, o_noise, o_loss[0, 0]


def solution(mesh):
    fine = Mesh(mesh.devices.reshape(8, 2, 4, 2, 2), AX)
    lat = ("y", "c")
    placed = (
        P(None, lat, "xh"), P(None, lat, "xh"), P(lat, "xh"), P(("z", "xl"), None),
        P(), P(), P(), P(),
    )
    return jax.shard_map(
        body, mesh=fine, in_specs=placed, out_specs=(P(), P(), P(), P(), P()), check_vma=False
    )
```

```python
import jax
import jax.numpy as jnp
from jax import lax
from jax.experimental import pallas as pl
from jax.experimental.pallas import tpu as pltpu
from jax.sharding import Mesh, PartitionSpec as P

f32 = jnp.float32
bf16 = jnp.bfloat16
SQ = 0.0625
GC = 0.7978845608028654
GA = 0.044715
V = 100
C = 256
M = 16
TC = 360
WP = 32
WH = 27
ROWS = 104
BR = 112
NB = 32
AX = ("z", "xl", "y", "c", "xh")


def perm(f):
    out = []
    for i in range(256):
        z, xl, lat, xh = i >> 5, (i >> 4) & 1, (i >> 1) & 7, i & 1
        z2, xl2, lat2, xh2 = f(z, xl, lat, xh)
        out.append((i, (z2 % 8) * 32 + xl2 * 16 + lat2 * 2 + xh2))
    return out


def send(v, f):
    return lax.ppermute(v, AX, perm(f))


def lat_shift(v, d):
    def f(z, xl, lat, xh):
        return (z, xl, (lat + d) % 8, xh)

    return send(v, f)


def member_index():
    return lax.axis_index("z") * 2 + lax.axis_index("xl")


def lat_index():
    return lax.axis_index("y") * 2 + lax.axis_index("c")


def params(limit=None):
    return pltpu.CompilerParams(vmem_limit_bytes=(limit or 16) * 1024 * 1024)


def gelu(x):
    t = jnp.tanh(GC * (x + GA * x * x * x))
    return 0.5 * x * (1.0 + t)


def gelu_both(x):
    x2 = x * x
    t = jnp.tanh(GC * (x + GA * x2 * x))
    h = 0.5 * (1.0 + t)
    slope = h + 0.5 * x * (1.0 - t * t) * (GC * (1.0 + 3.0 * GA * x2))
    return x * h, slope


def gelu_slope(x):
    return gelu_both(x)[1]


def prep_kernel(
    state, target, land, seeds, w_in, w_out, w_noise,
    x_out, edge_out, seeds_out, w_in_out, w_out_out, w_noise_out, sc, sems,
):
    moves = [
        pltpu.make_async_copy(w, out, sems.at[i])
        for i, (w, out) in enumerate(((w_in, w_in_out), (w_out, w_out_out), (w_noise, w_noise_out)))
    ]
    for move in moves:
        move.start()
    sc[...] = jnp.zeros(sc.shape, f32)
    edge_out[...] = jnp.zeros(edge_out.shape, f32)
    seeds_out[...] = jnp.broadcast_to(seeds[...], seeds_out.shape)
    for r in range(2):
        x_out[r, 0:8, :] = jnp.zeros((8, 256), f32)
        x_out[r, 8 + TC : 384, :] = jnp.zeros((376 - TC, 256), f32)
        sc[0:V, 0:TC] = state[:, r, :].astype(f32)
        sc[104:105, 0:TC] = 1.0 + land[r : r + 1, :].astype(f32)
        x_out[r, 8 : 8 + TC, 0:128] = sc[...].T[0:TC]
        sc[0:V, 0:TC] = target[:, r, :].astype(f32)
        x_out[r, 8 : 8 + TC, 128:256] = sc[...].T[0:TC]
        edge_out[16 * r : 16 * r + 3, :] = x_out[r, TC + 5 : TC + 8, :]
        edge_out[16 * r + 10 : 16 * r + 13, :] = x_out[r, 8:11, :]
    for move in moves:
        move.wait()


def window_kernel(x, edge, win):
    m = member_index()
    start = (45 * m) // 2
    row = lax.broadcasted_iota(jnp.int32, (16, 256), 0)
    low = (row < 3) & (m == 0)
    high = (row >= 10) & (row < 13) & (m == M - 1)
    for r in range(2):
        base = pl.multiple_of(((start + 5) // 8) * 8, 8)
        near = x[r, pl.ds(base, WP + 8), :]
        w = pltpu.roll(near, WP + 8 - (start + 5 - base), 0)[0:WP]
        e = edge[16 * r : 16 * r + 16, :]
        win[WP * r : WP * r + 16, :] = jnp.where(low, e, w[0:16]).astype(bf16)
        win[WP * r + 16 : WP * r + 32, :] = jnp.where(high, e, w[16:32]).astype(bf16)


def main_kernel(
    n2, n1, own, s1, s2, seeds, w_in, w_mid, w_out, w_noise, g_out, e_out,
    S, T, SB, PB, HID, HO, SL, UP, OUT, DO, DM, INC, DS, QB, BIAS,
):
    own22 = member_index() % 2
    lat = lat_index()
    core = lax.axis_index("c")
    rows = ((n2, 1, -2), (n1, 0, -1), (n1, 1, -1), (own, 0, 0), (own, 1, 0),
            (s1, 0, 1), (s1, 1, 1), (s2, 0, 2))
    for k, (ref, r, d) in enumerate(rows):
        inside = (lat + d >= 0) & (lat + d < 8)
        row = ref[WP * r : WP * r + WP, :].astype(f32) * jnp.where(inside, 1.0, 0.0)
        S[WP * k : WP * k + WP, :] = row[:, 0:128]
        T[WP * k : WP * k + WP, :] = row[:, 128:256]
    S[256:264, :] = jnp.zeros((8, 128), f32)
    T[256:264, :] = jnp.zeros((8, 128), f32)
    QB[...] = jnp.broadcast_to(S[:, 104:105], QB.shape)
    for b in range(3):
        SB[b] = S[b : b + 256, :].astype(bf16)
    latents = (seeds[...].astype(f32) - 32767.5) / 18918.0
    BIAS[...] = jnp.dot(
        latents, w_noise[...], precision=lax.Precision.HIGHEST, preferred_element_type=f32
    )
    acc = None
    for a in range(3):
        for b in range(3):
            part = jnp.dot(
                SB[b, a * 32 : a * 32 + 192, 0:V], w_in[3 * a + b], preferred_element_type=f32
            )
            acc = part if acc is None else acc + part
    PB[...] = acc

    bias = BIAS[...]
    HID[162 * M : 164 * M, :] = jnp.zeros((2 * M, C), bf16)
    for r in range(6):
        gr = lat * 2 - 2 + r
        valid = jnp.where((gr >= 0) & (gr < 16), 1.0, 0.0).astype(f32)

        def hid_cell(i, carry, r=r, valid=valid):
            row = PB[pl.ds(r * 32 + i, 1), :]
            h = gelu(jnp.broadcast_to(row, (M, C)) + bias) * valid
            HID[pl.ds(pl.multiple_of((r * WH + i) * M, M), M), :] = h.astype(bf16)
            return carry

        lax.fori_loop(0, WH, hid_cell, 0, unroll=9)

    NR = WH * M

    def mid_row(r, carry):
        lhs = jnp.concatenate(
            [
                HID[pl.ds(pl.multiple_of(((r + a) * WH + b) * M, M), NR), :]
                for a in range(3)
                for b in range(3)
            ],
            axis=1,
        )
        pre = jnp.dot(lhs, w_mid[...].reshape(9 * C, C), preferred_element_type=f32)
        act, slope = gelu_both(pre)
        hid = HID[pl.ds(pl.multiple_of(((r + 1) * WH + 1) * M, M), NR), :].astype(f32)
        base = pl.multiple_of(r * NR, M)
        ho = (act + hid).astype(bf16)
        HO[pl.ds(base, NR), :] = ho
        SL[pl.ds(base, NR), :] = slope
        OUT[pl.ds(base, NR), 0:V] = lax.dot_general(
            ho, w_out[...], (((1,), (1,)), ((), ())), preferred_element_type=f32
        )
        return carry

    lax.fori_loop(0, 4, mid_row, 0)

    def cell_terms(r, i, with_loss):
        base = pl.multiple_of((r * WH + i) * M, M)
        srow = (r + 2) * 32 + i + 2
        st = S[pl.ds(srow, 1), :]
        tg = T[pl.ds(srow, 1), :]
        q = QB[pl.ds(srow, 1), :]
        o = (OUT[pl.ds(base, M), :] + st).astype(bf16).astype(f32)
        miss = o - tg
        e = miss * miss + SQ
        inv = lax.rsqrt(e)
        slope = miss * inv
        dist = e * inv - 0.25 if with_loss else None
        total = None
        spread = None
        for k in range(1, 9):
            u = o - pltpu.roll(o, k, 0)
            e = u * u + SQ
            inv = lax.rsqrt(e)
            s = u * inv
            if k < 8:
                s = s - pltpu.roll(s, M - k, 0)
            total = s if total is None else total + s
            if with_loss:
                d = e * inv - 0.25
                if k == 8:
                    d = 0.5 * d
                spread = d if spread is None else spread + d
        g = q * (slope * (1.0 / M) - total * (1.0 / (M * (M - 1))))
        DO[pl.ds(base, M), :] = g.astype(bf16)
        if with_loss:
            return q * (dist * (1.0 / M) - spread * (1.0 / (M * (M - 1))))
        return None

    loss = jnp.zeros((M, 128), f32)
    for r in (1, 2):

        def loss_cell(i, total, r=r):
            term = cell_terms(r, i, True)
            mine = (i >= 1) & ((i < 23) | ((i == 23) & (own22 > 0)))
            return total + jnp.where(mine, 1.0, 0.0) * term

        loss = lax.fori_loop(0, WH, loss_cell, loss, unroll=3)
    for r in (0, 3):

        def grad_cell(i, carry, r=r):
            cell_terms(r, i, False)
            return carry

        lax.fori_loop(0, WH, grad_cell, 0, unroll=3)
    lane = lax.broadcasted_iota(jnp.int32, (M, 128), 1)
    loss = jnp.sum(jnp.sum(jnp.where(lane < V, loss, 0.0), axis=0, keepdims=True), axis=1, keepdims=True)

    UP[...] = jnp.dot(DO[:, 0:V], w_out[...], preferred_element_type=f32)

    def mid_cell(i, carry):
        at = pl.multiple_of(i * 2 * M, M)
        DM[pl.ds(at, 2 * M), :] = (UP[pl.ds(at, 2 * M), :] * SL[pl.ds(at, 2 * M), :]).astype(bf16)
        return carry

    lax.fori_loop(0, 54, mid_cell, 0, unroll=6)
    DM[108 * M : 112 * M, :] = jnp.zeros((4 * M, C), bf16)

    wcat = jnp.concatenate([w_mid[t] for t in range(9)], axis=1)
    for r in range(2):
        lhs = jnp.concatenate(
            [
                DM[((r + 2 - a) * WH + 2 - b) * M : ((r + 2 - a) * WH + 2 - b) * M + NR, :]
                for a in range(3)
                for b in range(3)
            ],
            axis=1,
        )
        INC[r * NR : (r + 1) * NR, :] = lax.dot_general(
            lhs, wcat, (((1,), (1,)), ((), ())), preferred_element_type=f32
        )
    DS[...] = jnp.zeros(DS.shape, f32)
    dsum = jnp.zeros((M, C), f32)
    for r in range(2):

        def in_cell(i, total, r=r):
            x = jnp.broadcast_to(PB[pl.ds((r + 2) * 32 + i + 2, 1), :], (M, C)) + bias
            base = pl.multiple_of((r * WH + i) * M, M)
            upb = pl.multiple_of(((r + 1) * WH + 1 + i) * M, M)
            d = (INC[pl.ds(base, M), :] + UP[pl.ds(upb, M), :]) * gelu_slope(x)
            mine = jnp.where((i < 22) | (own22 > 0), 1.0, 0.0)
            d = d.astype(bf16).astype(f32) * mine
            DS[pl.ds(r * 32 + i + 2, 1), :] = jnp.sum(d, axis=0, keepdims=True)
            return total + d

        dsum = lax.fori_loop(0, 23, in_cell, dsum)

    def store(k, lo, hi, value):
        g_out[(k // 16) ^ core, k % 16, lo:hi, :] = value

    g_out[:, :, ROWS:BR, :] = jnp.zeros((2, 16, BR - ROWS, C), f32)
    peaks = []

    def put(row, value):
        done = 0
        n = value.shape[0]
        peaks.append(jnp.max(jnp.abs(value), axis=0, keepdims=True))
        while done < n:
            k, i = divmod(row + done, ROWS)
            take = min(n - done, ROWS - i)
            store(k, i, i + take, value[done : done + take, :])
            done += take

    cell = lax.broadcasted_iota(jnp.int32, (NR, C), 0) >> 4
    mine = (cell < 22) | ((cell == 22) & (own22 > 0))
    start = (WH + 1) * M
    dmc = jnp.concatenate(
        [
            jnp.where(mine, DM[start + r * NR : start + (r + 1) * NR, :].astype(f32), 0.0)
            for r in range(2)
        ],
        axis=0,
    )
    dmt = dmc.T.astype(bf16)
    for a in range(3):
        for b in range(3):
            hs = ((a + 1) * WH + b + 1) * M
            g = jnp.dot(dmt, HID[hs : hs + 2 * NR, :], preferred_element_type=f32)
            put((3 * a + b) * C, g.T)
    doc = jnp.concatenate(
        [
            jnp.where(
                mine[:, 0:128], DO[start + r * NR : start + (r + 1) * NR, :].astype(f32), 0.0
            )
            for r in range(2)
        ],
        axis=0,
    )
    dot_ = doc.T.astype(bf16)
    go = jnp.dot(dot_, HO[start : start + 2 * NR, :], preferred_element_type=f32)
    ds = DS[...]
    hi = ds.astype(bf16)
    lo = (ds - hi.astype(f32)).astype(bf16)
    both = jnp.concatenate([hi, lo], axis=1)
    for a in range(3):
        for b in range(3):
            g = lax.dot_general(
                SB[b, (a + 2) * 32 : (a + 2) * 32 + 64, :], both,
                (((0,), (0,)), ((), ())), preferred_element_type=f32,
            )
            put(9 * C + V * (3 * a + b), (g[:, 0:C] + g[:, C : 2 * C])[0:V, :])
    put(9 * C + 9 * V, go[0:V, :])
    put(9 * C + 10 * V, jnp.zeros((NB * ROWS - 9 * C - 10 * V, C), f32))
    gn = lax.dot_general(
        latents, dsum, (((0,), (0,)), ((), ())),
        precision=lax.Precision.HIGHEST, preferred_element_type=f32,
    )
    peaks.append(jnp.max(jnp.abs(gn), axis=0, keepdims=True))
    for k in range(NB):
        store(k, ROWS, ROWS + 1, gn[k : k + 1, :])
    loss = jnp.broadcast_to(loss * (1.0 / (V * 16 * 720)), (1, C))
    first = loss.astype(bf16).astype(f32)
    store(0, ROWS + 1, ROWS + 2, first)
    store(0, ROWS + 2, ROWS + 3, loss - first)
    peaks.append(jnp.abs(loss))
    peak = peaks[0]
    for p in peaks[1:]:
        peak = jnp.maximum(peak, p)
    peak = jnp.broadcast_to(jnp.max(peak, axis=1, keepdims=True), (8, C))
    e_out[...] = exponent(peak)


def exponent(bound):
    return jnp.ceil(jnp.log2(jnp.maximum(bound, 1e-30)))


def final_kernel(half, far, o_in, o_mid, o_out, o_noise, o_loss, t, u, out_sems):
    core = lax.axis_index("c")
    for slot, ref in ((core, half), (1 - core, far)):
        for k in range(16):
            f = jnp.exp2(ref[k, BR - 1 : BR, :] - 14.0)
            t[slot * 16 + k] = ref[k] * f

    def get(row, n):
        parts = []
        done = 0
        while done < n:
            k, i = divmod(row + done, ROWS)
            take = min(n - done, ROWS - i)
            parts.append((done, take, k, i))
            done += take
        return parts

    def scale_of(pieces, count):
        total = jnp.zeros((8, C), f32)
        ragged = jnp.zeros((1, C), f32)
        for p in pieces:
            for _, take, k, i in p:
                v = t[k, i : i + take, :]
                v = v * v
                if take % 8 == 0:
                    total = total + jnp.sum(v.reshape(take // 8, 8, C), axis=0)
                else:
                    ragged = ragged + jnp.sum(v, axis=0, keepdims=True)
        total = jnp.sum(total, axis=0, keepdims=True) + ragged
        ms = jnp.sum(total, axis=1, keepdims=True) * (1.0 / count)
        return lax.rsqrt(ms + 1e-6)

    moves = []

    def emit(pieces, scale, buf, out, k):
        for done, take, b, i in pieces:
            buf[done : done + take, :] = t[b, i : i + take, :] * scale
        if out is not None:
            move = pltpu.make_async_copy(buf, out, out_sems.at[k])
            move.start()
            moves.append(move)

    pieces = [get(C * k, C) for k in range(9)]
    scale = scale_of(pieces, 9 * C * C)
    for k in range(9):
        emit(pieces[k], scale, u.at[k], o_mid.at[k], k)
    pieces = [get(9 * C + V * k, V) for k in range(9)]
    scale = scale_of(pieces, 9 * V * C)
    for k in range(9):
        emit(pieces[k], scale, o_in.at[k], None, 0)
    pieces = get(9 * C + 9 * V, V)
    emit(pieces, scale_of([pieces], V * C), o_out, None, 0)
    pieces = [(k, 1, k, ROWS) for k in range(NB)]
    emit(pieces, scale_of([pieces], NB * C), o_noise, None, 0)
    o_loss[...] = t[0, ROWS + 1 : ROWS + 2, 0:128] + t[0, ROWS + 2 : ROWS + 3, 0:128]
    for move in moves:
        move.wait()


def call(kernel, outs, scratch, ins, place=None, kept=(), limit=None):
    place = place or {}
    vmem = pl.BlockSpec(memory_space=pltpu.VMEM)
    left = pl.BlockSpec(memory_space=pl.ANY)
    ins = [
        pltpu.with_memory_space_constraint(v, pltpu.VMEM if i in kept else pltpu.HBM)
        for i, v in enumerate(ins)
    ]
    return pl.pallas_call(
        kernel,
        out_shape=[
            pltpu.VMEM(o[0], o[1]) if len(o) > 2 else jax.ShapeDtypeStruct(*o) for o in outs
        ],
        in_specs=[left if ("in", i) in place else vmem for i in range(len(ins))],
        out_specs=[left if ("out", i) in place else vmem for i in range(len(outs))],
        scratch_shapes=scratch,
        compiler_params=params(limit),
    )(*ins)


f16 = jnp.float16


def sum_all(mine, theirs, e):
    xy = ("xl", "y", "xh")

    def other(z, xl, lat, xh):
        return (z, xl, lat ^ 1, xh)

    e = (jnp.maximum(e, send(e, other)) + 1.0)[0:1]
    last = (jnp.arange(BR, dtype=jnp.int32) == BR - 1)[:, None]
    tag = jnp.where(last, e, 0.0)
    s = (mine + send(theirs, other)) * jnp.exp2(14.0 - e)[None] + tag[None]
    got = lax.all_to_all(s.astype(f16), xy, 0, 0, tiled=True)
    q = jnp.exp2(got[:, BR - 1 : BR, :].astype(f32) - 14.0)
    s = jnp.sum(jnp.where(last[None], 2.0**14, got.astype(f32)) * q, axis=0)
    r1, r2, r3 = (
        send(s, lambda z, xl, lat, xh, k=k: (z ^ k, xl, lat, xh)) for k in (1, 2, 3)
    )
    s = (s + r1) + (r2 + r3)
    s = s + send(s, lambda z, xl, lat, xh: (7 - z, xl, lat, xh))
    e = exponent(s[BR - 1 : BR, :])
    s = jnp.where(last, e, s * jnp.exp2(14.0 - e)).astype(f16)
    half = lax.all_to_all(jnp.broadcast_to(s[None], (16,) + s.shape), xy, 0, 0, tiled=True)
    far = send(half, other)
    return half.astype(f32), far.astype(f32)


def body(state, target, land, seeds, w_in, w_mid, w_out, w_noise):
    x, edge, seeds, w_in, w_out, w_noise = call(
        prep_kernel,
        [
            ((2, 384, 256), f32, 1), ((32, 256), f32, 1), ((M, 32), jnp.int32, 1),
            ((9, V, C), bf16, 1), ((V, C), bf16, 1), ((NB, C), f32, 1),
        ],
        [pltpu.VMEM((128, 384), f32), pltpu.SemaphoreType.DMA((3,))],
        (state, target, land, seeds, w_in, w_out, w_noise),
        {("in", 4), ("in", 5), ("in", 6)},
    )
    edge = send(edge, lambda z, xl, lat, xh: (z, xl, lat, xh ^ 1))
    seeds = lax.all_to_all(seeds, ("z", "xl"), 0, 0, tiled=True)
    (win,) = call(window_kernel, [((2 * WP, 256), bf16, 1)], [], (x, edge), kept=(0, 1))
    win, seeds = lax.optimization_barrier((win, seeds))
    n2, n1, s1, s2 = (lat_shift(win, d) for d in (2, 1, -1, -2))
    g, e = call(
        main_kernel, [((2, 16, BR, C), f32, 1), ((8, C), f32, 1)],
        [
            pltpu.VMEM((264, 128), f32),
            pltpu.VMEM((264, 128), f32),
            pltpu.VMEM((3, 256, 128), bf16),
            pltpu.VMEM((192, C), f32),
            pltpu.VMEM((164 * M, C), bf16),
            pltpu.VMEM((108 * M, C), bf16),
            pltpu.VMEM((108 * M, C), f32),
            pltpu.VMEM((108 * M, C), f32),
            pltpu.VMEM((108 * M, 128), f32),
            pltpu.VMEM((108 * M, 128), bf16),
            pltpu.VMEM((112 * M, C), bf16),
            pltpu.VMEM((54 * M, C), f32),
            pltpu.VMEM((64, C), f32),
            pltpu.VMEM((264, 128), f32),
            pltpu.VMEM((M, C), f32),
        ],
        (n2, n1, win, s1, s2, seeds, w_in, w_mid, w_out, w_noise),
        kept=range(10),
        limit=32,
    )
    half, far = sum_all(g[0], g[1], e)
    o_in, o_mid, o_out, o_noise, o_loss = call(
        final_kernel,
        [((9, V, C), f32), ((9, C, C), f32), ((V, C), f32), ((NB, C), f32), ((1, 128), f32)],
        [
            pltpu.VMEM((NB, BR, C), f32),
            pltpu.VMEM((9, C, C), f32),
            pltpu.SemaphoreType.DMA((9,)),
        ],
        (half, far),
        {("out", 1)},
        kept=(0, 1),
    )
    return o_in, o_mid, o_out, o_noise, o_loss[0, 0]


def solution(mesh):
    fine = Mesh(mesh.devices.reshape(8, 2, 4, 2, 2), AX)
    lat = ("y", "c")
    placed = (
        P(None, lat, "xh"), P(None, lat, "xh"), P(lat, "xh"), P(("z", "xl"), None),
        P(), P(), P(), P(),
    )
    return jax.shard_map(
        body, mesh=fine, in_specs=placed, out_specs=(P(), P(), P(), P(), P()), check_vma=False
    )
```

```python
import jax
import jax.numpy as jnp
from jax import lax
from jax.experimental import pallas as pl
from jax.experimental.pallas import tpu as pltpu
from jax.sharding import Mesh, PartitionSpec as P

f32 = jnp.float32
bf16 = jnp.bfloat16
SQ = 0.0625
GC = 0.7978845608028654
GA = 0.044715
V = 100
C = 256
M = 16
TC = 360
WP = 32
WH = 27
ROWS = 104
BR = 112
NB = 32
AX = ("z", "xl", "y", "c", "xh")


def perm(f):
    out = []
    for i in range(256):
        z, xl, lat, xh = i >> 5, (i >> 4) & 1, (i >> 1) & 7, i & 1
        z2, xl2, lat2, xh2 = f(z, xl, lat, xh)
        out.append((i, (z2 % 8) * 32 + xl2 * 16 + lat2 * 2 + xh2))
    return out


def send(v, f):
    return lax.ppermute(v, AX, perm(f))


def lat_shift(v, d):
    def f(z, xl, lat, xh):
        return (z, xl, (lat + d) % 8, xh)

    return send(v, f)


def member_index():
    return lax.axis_index("z") * 2 + lax.axis_index("xl")


def lat_index():
    return lax.axis_index("y") * 2 + lax.axis_index("c")


def params(limit=None):
    return pltpu.CompilerParams(vmem_limit_bytes=(limit or 16) * 1024 * 1024)


def gelu(x):
    t = jnp.tanh(GC * (x + GA * x * x * x))
    return 0.5 * x * (1.0 + t)


def gelu_both(x):
    x2 = x * x
    t = jnp.tanh(GC * (x + GA * x2 * x))
    h = 0.5 * (1.0 + t)
    slope = h + 0.5 * x * (1.0 - t * t) * (GC * (1.0 + 3.0 * GA * x2))
    return x * h, slope


def gelu_slope(x):
    return gelu_both(x)[1]


def prep_kernel(
    state, target, land, seeds, w_in, w_out, w_noise,
    x_out, edge_out, seeds_out, w_in_out, w_out_out, w_noise_out, sc, sems,
):
    moves = [
        pltpu.make_async_copy(w, out, sems.at[i])
        for i, (w, out) in enumerate(((w_in, w_in_out), (w_out, w_out_out), (w_noise, w_noise_out)))
    ]
    for move in moves:
        move.start()
    sc[...] = jnp.zeros(sc.shape, f32)
    edge_out[...] = jnp.zeros(edge_out.shape, f32)
    seeds_out[...] = jnp.broadcast_to(seeds[...], seeds_out.shape)
    for r in range(2):
        x_out[r, 0:8, :] = jnp.zeros((8, 256), f32)
        x_out[r, 8 + TC : 384, :] = jnp.zeros((376 - TC, 256), f32)
        sc[0:V, 0:TC] = state[:, r, :].astype(f32)
        sc[104:105, 0:TC] = 1.0 + land[r : r + 1, :].astype(f32)
        x_out[r, 8 : 8 + TC, 0:128] = sc[...].T[0:TC]
        sc[0:V, 0:TC] = target[:, r, :].astype(f32)
        x_out[r, 8 : 8 + TC, 128:256] = sc[...].T[0:TC]
        edge_out[16 * r : 16 * r + 3, :] = x_out[r, TC + 5 : TC + 8, :]
        edge_out[16 * r + 10 : 16 * r + 13, :] = x_out[r, 8:11, :]
    for move in moves:
        move.wait()


def window_kernel(x, edge, win):
    m = member_index()
    start = (45 * m) // 2
    row = lax.broadcasted_iota(jnp.int32, (16, 256), 0)
    low = (row < 3) & (m == 0)
    high = (row >= 10) & (row < 13) & (m == M - 1)
    for r in range(2):
        base = pl.multiple_of(((start + 5) // 8) * 8, 8)
        near = x[r, pl.ds(base, WP + 8), :]
        w = pltpu.roll(near, WP + 8 - (start + 5 - base), 0)[0:WP]
        e = edge[16 * r : 16 * r + 16, :]
        win[WP * r : WP * r + 16, :] = jnp.where(low, e, w[0:16]).astype(bf16)
        win[WP * r + 16 : WP * r + 32, :] = jnp.where(high, e, w[16:32]).astype(bf16)


def main_kernel(
    n2, n1, own, s1, s2, seeds, w_in, w_mid, w_out, w_noise, g_out, e_out,
    S, T, SB, PB, HID, HO, SL, UP, OUT, DO, DM, INC, DS, QB, BIAS,
):
    own22 = member_index() % 2
    lat = lat_index()
    core = lax.axis_index("c")
    rows = ((n2, 1, -2), (n1, 0, -1), (n1, 1, -1), (own, 0, 0), (own, 1, 0),
            (s1, 0, 1), (s1, 1, 1), (s2, 0, 2))
    for k, (ref, r, d) in enumerate(rows):
        inside = (lat + d >= 0) & (lat + d < 8)
        row = ref[WP * r : WP * r + WP, :].astype(f32) * jnp.where(inside, 1.0, 0.0)
        S[WP * k : WP * k + WP, :] = row[:, 0:128]
        T[WP * k : WP * k + WP, :] = row[:, 128:256]
    S[256:264, :] = jnp.zeros((8, 128), f32)
    T[256:264, :] = jnp.zeros((8, 128), f32)
    QB[...] = jnp.broadcast_to(S[:, 104:105], QB.shape)
    for b in range(3):
        SB[b] = S[b : b + 256, :].astype(bf16)
    latents = (seeds[...].astype(f32) - 32767.5) / 18918.0
    BIAS[...] = jnp.dot(
        latents, w_noise[...], precision=lax.Precision.HIGHEST, preferred_element_type=f32
    )
    acc = None
    for a in range(3):
        for b in range(3):
            part = jnp.dot(
                SB[b, a * 32 : a * 32 + 192, 0:V], w_in[3 * a + b], preferred_element_type=f32
            )
            acc = part if acc is None else acc + part
    PB[...] = acc

    bias = BIAS[...]
    HID[162 * M : 164 * M, :] = jnp.zeros((2 * M, C), bf16)
    for r in range(6):
        gr = lat * 2 - 2 + r
        valid = jnp.where((gr >= 0) & (gr < 16), 1.0, 0.0).astype(f32)

        def hid_cell(i, carry, r=r, valid=valid):
            row = PB[pl.ds(r * 32 + i, 1), :]
            h = gelu(jnp.broadcast_to(row, (M, C)) + bias) * valid
            HID[pl.ds(pl.multiple_of((r * WH + i) * M, M), M), :] = h.astype(bf16)
            return carry

        lax.fori_loop(0, WH, hid_cell, 0, unroll=9)

    NR = WH * M

    def mid_row(r, carry):
        lhs = jnp.concatenate(
            [
                HID[pl.ds(pl.multiple_of(((r + a) * WH + b) * M, M), NR), :]
                for a in range(3)
                for b in range(3)
            ],
            axis=1,
        )
        pre = jnp.dot(lhs, w_mid[...].reshape(9 * C, C), preferred_element_type=f32)
        act, slope = gelu_both(pre)
        hid = HID[pl.ds(pl.multiple_of(((r + 1) * WH + 1) * M, M), NR), :].astype(f32)
        base = pl.multiple_of(r * NR, M)
        ho = (act + hid).astype(bf16)
        HO[pl.ds(base, NR), :] = ho
        SL[pl.ds(base, NR), :] = slope
        OUT[pl.ds(base, NR), 0:V] = lax.dot_general(
            ho, w_out[...], (((1,), (1,)), ((), ())), preferred_element_type=f32
        )
        return carry

    lax.fori_loop(0, 4, mid_row, 0)

    def cell_terms(r, i, with_loss):
        base = pl.multiple_of((r * WH + i) * M, M)
        srow = (r + 2) * 32 + i + 2
        st = S[pl.ds(srow, 1), :]
        tg = T[pl.ds(srow, 1), :]
        q = QB[pl.ds(srow, 1), :]
        o = (OUT[pl.ds(base, M), :] + st).astype(bf16).astype(f32)
        miss = o - tg
        e = miss * miss + SQ
        inv = lax.rsqrt(e)
        slope = miss * inv
        dist = e * inv - 0.25 if with_loss else None
        total = None
        spread = None
        for k in range(1, 9):
            u = o - pltpu.roll(o, k, 0)
            e = u * u + SQ
            inv = lax.rsqrt(e)
            s = u * inv
            if k < 8:
                s = s - pltpu.roll(s, M - k, 0)
            total = s if total is None else total + s
            if with_loss:
                d = e * inv - 0.25
                if k == 8:
                    d = 0.5 * d
                spread = d if spread is None else spread + d
        g = q * (slope * (1.0 / M) - total * (1.0 / (M * (M - 1))))
        DO[pl.ds(base, M), :] = g.astype(bf16)
        if with_loss:
            return q * (dist * (1.0 / M) - spread * (1.0 / (M * (M - 1))))
        return None

    loss = jnp.zeros((M, 128), f32)
    for r in (1, 2):

        def loss_cell(i, total, r=r):
            term = cell_terms(r, i, True)
            mine = (i >= 1) & ((i < 23) | ((i == 23) & (own22 > 0)))
            return total + jnp.where(mine, 1.0, 0.0) * term

        loss = lax.fori_loop(0, WH, loss_cell, loss, unroll=3)
    for r in (0, 3):

        def grad_cell(i, carry, r=r):
            cell_terms(r, i, False)
            return carry

        lax.fori_loop(0, WH, grad_cell, 0, unroll=3)
    lane = lax.broadcasted_iota(jnp.int32, (M, 128), 1)
    loss = jnp.sum(jnp.sum(jnp.where(lane < V, loss, 0.0), axis=0, keepdims=True), axis=1, keepdims=True)

    UP[...] = jnp.dot(DO[:, 0:V], w_out[...], preferred_element_type=f32)

    def mid_cell(i, carry):
        at = pl.multiple_of(i * 2 * M, M)
        DM[pl.ds(at, 2 * M), :] = (UP[pl.ds(at, 2 * M), :] * SL[pl.ds(at, 2 * M), :]).astype(bf16)
        return carry

    lax.fori_loop(0, 54, mid_cell, 0, unroll=6)
    DM[108 * M : 112 * M, :] = jnp.zeros((4 * M, C), bf16)

    wcat = jnp.concatenate([w_mid[t] for t in range(9)], axis=1)
    for r in range(2):
        lhs = jnp.concatenate(
            [
                DM[((r + 2 - a) * WH + 2 - b) * M : ((r + 2 - a) * WH + 2 - b) * M + NR, :]
                for a in range(3)
                for b in range(3)
            ],
            axis=1,
        )
        INC[r * NR : (r + 1) * NR, :] = lax.dot_general(
            lhs, wcat, (((1,), (1,)), ((), ())), preferred_element_type=f32
        )
    DS[...] = jnp.zeros(DS.shape, f32)
    dsum = jnp.zeros((M, C), f32)
    for r in range(2):

        def in_cell(i, total, r=r):
            x = jnp.broadcast_to(PB[pl.ds((r + 2) * 32 + i + 2, 1), :], (M, C)) + bias
            base = pl.multiple_of((r * WH + i) * M, M)
            upb = pl.multiple_of(((r + 1) * WH + 1 + i) * M, M)
            d = (INC[pl.ds(base, M), :] + UP[pl.ds(upb, M), :]) * gelu_slope(x)
            mine = jnp.where((i < 22) | (own22 > 0), 1.0, 0.0)
            d = d.astype(bf16).astype(f32) * mine
            DS[pl.ds(r * 32 + i + 2, 1), :] = jnp.sum(d, axis=0, keepdims=True)
            return total + d

        dsum = lax.fori_loop(0, 23, in_cell, dsum)

    def store(k, lo, hi, value):
        g_out[(k // 16) ^ core, k % 16, lo:hi, :] = value

    g_out[:, :, ROWS:BR, :] = jnp.zeros((2, 16, BR - ROWS, C), f32)
    peaks = []

    def put(row, value):
        done = 0
        n = value.shape[0]
        peaks.append(jnp.max(jnp.abs(value), axis=0, keepdims=True))
        while done < n:
            k, i = divmod(row + done, ROWS)
            take = min(n - done, ROWS - i)
            store(k, i, i + take, value[done : done + take, :])
            done += take

    cell = lax.broadcasted_iota(jnp.int32, (NR, C), 0) >> 4
    mine = (cell < 22) | ((cell == 22) & (own22 > 0))
    start = (WH + 1) * M
    dmc = jnp.concatenate(
        [
            jnp.where(mine, DM[start + r * NR : start + (r + 1) * NR, :].astype(f32), 0.0)
            for r in range(2)
        ],
        axis=0,
    )
    dmt = dmc.T.astype(bf16)
    for a in range(3):
        for b in range(3):
            hs = ((a + 1) * WH + b + 1) * M
            g = jnp.dot(dmt, HID[hs : hs + 2 * NR, :], preferred_element_type=f32)
            put((3 * a + b) * C, g.T)
    doc = jnp.concatenate(
        [
            jnp.where(
                mine[:, 0:128], DO[start + r * NR : start + (r + 1) * NR, :].astype(f32), 0.0
            )
            for r in range(2)
        ],
        axis=0,
    )
    dot_ = doc.T.astype(bf16)
    go = jnp.dot(dot_, HO[start : start + 2 * NR, :], preferred_element_type=f32)
    ds = DS[...]
    hi = ds.astype(bf16)
    lo = (ds - hi.astype(f32)).astype(bf16)
    both = jnp.concatenate([hi, lo], axis=1)
    for a in range(3):
        for b in range(3):
            g = lax.dot_general(
                SB[b, (a + 2) * 32 : (a + 2) * 32 + 64, :], both,
                (((0,), (0,)), ((), ())), preferred_element_type=f32,
            )
            put(9 * C + V * (3 * a + b), (g[:, 0:C] + g[:, C : 2 * C])[0:V, :])
    put(9 * C + 9 * V, go[0:V, :])
    put(9 * C + 10 * V, jnp.zeros((NB * ROWS - 9 * C - 10 * V, C), f32))
    gn = lax.dot_general(
        latents, dsum, (((0,), (0,)), ((), ())),
        precision=lax.Precision.HIGHEST, preferred_element_type=f32,
    )
    peaks.append(jnp.max(jnp.abs(gn), axis=0, keepdims=True))
    for k in range(NB):
        store(k, ROWS, ROWS + 1, gn[k : k + 1, :])
    loss = jnp.broadcast_to(loss * (1.0 / (V * 16 * 720)), (1, C))
    first = loss.astype(bf16).astype(f32)
    store(0, ROWS + 1, ROWS + 2, first)
    store(0, ROWS + 2, ROWS + 3, loss - first)
    peaks.append(jnp.abs(loss))
    peak = peaks[0]
    for p in peaks[1:]:
        peak = jnp.maximum(peak, p)
    peak = jnp.broadcast_to(jnp.max(peak, axis=1, keepdims=True), (8, C))
    e_out[...] = exponent(peak)


def exponent(bound):
    return jnp.ceil(jnp.log2(jnp.maximum(bound, 1e-30)))


def final_kernel(half, far, o_in, o_mid, o_out, o_noise, o_loss, t, u, out_sems):
    core = lax.axis_index("c")
    for slot, ref in ((core, half), (1 - core, far)):
        for k in range(16):
            f = jnp.exp2(ref[k, BR - 1 : BR, :] - 14.0)
            t[slot * 16 + k] = ref[k] * f

    def get(row, n):
        parts = []
        done = 0
        while done < n:
            k, i = divmod(row + done, ROWS)
            take = min(n - done, ROWS - i)
            parts.append((done, take, k, i))
            done += take
        return parts

    def scale_of(pieces, count):
        total = jnp.zeros((8, C), f32)
        ragged = jnp.zeros((1, C), f32)
        for p in pieces:
            for _, take, k, i in p:
                v = t[k, i : i + take, :]
                v = v * v
                if take % 8 == 0:
                    total = total + jnp.sum(v.reshape(take // 8, 8, C), axis=0)
                else:
                    ragged = ragged + jnp.sum(v, axis=0, keepdims=True)
        total = jnp.sum(total, axis=0, keepdims=True) + ragged
        ms = jnp.sum(total, axis=1, keepdims=True) * (1.0 / count)
        return lax.rsqrt(ms + 1e-6)

    moves = []

    def emit(pieces, scale, buf, out, k):
        for done, take, b, i in pieces:
            buf[done : done + take, :] = t[b, i : i + take, :] * scale
        if out is not None:
            move = pltpu.make_async_copy(buf, out, out_sems.at[k])
            move.start()
            moves.append(move)

    pieces = [get(C * k, C) for k in range(9)]
    scale = scale_of(pieces, 9 * C * C)
    for k in range(9):
        emit(pieces[k], scale, u.at[k], o_mid.at[k], k)
    pieces = [get(9 * C + V * k, V) for k in range(9)]
    scale = scale_of(pieces, 9 * V * C)
    for k in range(9):
        emit(pieces[k], scale, o_in.at[k], None, 0)
    pieces = get(9 * C + 9 * V, V)
    emit(pieces, scale_of([pieces], V * C), o_out, None, 0)
    pieces = [(k, 1, k, ROWS) for k in range(NB)]
    emit(pieces, scale_of([pieces], NB * C), o_noise, None, 0)
    o_loss[...] = t[0, ROWS + 1 : ROWS + 2, 0:128] + t[0, ROWS + 2 : ROWS + 3, 0:128]
    for move in moves:
        move.wait()


def call(kernel, outs, scratch, ins, place=None, kept=(), limit=None):
    place = place or {}
    vmem = pl.BlockSpec(memory_space=pltpu.VMEM)
    left = pl.BlockSpec(memory_space=pl.ANY)
    ins = [
        pltpu.with_memory_space_constraint(v, pltpu.VMEM if i in kept else pltpu.HBM)
        for i, v in enumerate(ins)
    ]
    return pl.pallas_call(
        kernel,
        out_shape=[
            pltpu.VMEM(o[0], o[1]) if len(o) > 2 else jax.ShapeDtypeStruct(*o) for o in outs
        ],
        in_specs=[left if ("in", i) in place else vmem for i in range(len(ins))],
        out_specs=[left if ("out", i) in place else vmem for i in range(len(outs))],
        scratch_shapes=scratch,
        compiler_params=params(limit),
    )(*ins)


f16 = jnp.float16


def is_last():
    return (jnp.arange(BR, dtype=jnp.int32) == BR - 1)[:, None]


def coded(s):
    e = exponent(s[BR - 1 : BR, :])
    return jnp.where(is_last(), e, s * jnp.exp2(14.0 - e)).astype(f16)


def decoded(msg):
    q = jnp.exp2(msg[..., BR - 1 : BR, :].astype(f32) - 14.0)
    return jnp.where(is_last(), 2.0**14, msg.astype(f32)) * q


def sum_all(mine, theirs, e):
    xy = ("xl", "y", "xh")

    def other(z, xl, lat, xh):
        return (z, xl, lat ^ 1, xh)

    e = (jnp.maximum(e, send(e, other)) + 1.0)[0:1]
    tag = jnp.where(is_last(), e, 0.0)
    s = (mine + send(theirs, other)) * jnp.exp2(14.0 - e)[None] + tag[None]
    got = lax.all_to_all(s.astype(f16), xy, 0, 0, tiled=True)
    s = jnp.sum(decoded(got), axis=0)
    s = coded(s)
    r0, r1, r2, r3 = (
        decoded(send(s, lambda z, xl, lat, xh, k=k: (z ^ k, xl, lat, xh)) if k else s)
        for k in range(4)
    )
    s = coded((r0 + r1) + (r2 + r3))
    s = coded(decoded(s) + decoded(send(s, lambda z, xl, lat, xh: (7 - z, xl, lat, xh))))
    half = lax.all_to_all(jnp.broadcast_to(s[None], (16,) + s.shape), xy, 0, 0, tiled=True)
    far = send(half, other)
    return half.astype(f32), far.astype(f32)


def body(state, target, land, seeds, w_in, w_mid, w_out, w_noise):
    x, edge, seeds, w_in, w_out, w_noise = call(
        prep_kernel,
        [
            ((2, 384, 256), f32, 1), ((32, 256), f32, 1), ((M, 32), jnp.int32, 1),
            ((9, V, C), bf16, 1), ((V, C), bf16, 1), ((NB, C), f32, 1),
        ],
        [pltpu.VMEM((128, 384), f32), pltpu.SemaphoreType.DMA((3,))],
        (state, target, land, seeds, w_in, w_out, w_noise),
        {("in", 4), ("in", 5), ("in", 6)},
    )
    edge = send(edge, lambda z, xl, lat, xh: (z, xl, lat, xh ^ 1))
    seeds = lax.all_to_all(seeds, ("z", "xl"), 0, 0, tiled=True)
    (win,) = call(window_kernel, [((2 * WP, 256), bf16, 1)], [], (x, edge), kept=(0, 1))
    win, seeds = lax.optimization_barrier((win, seeds))
    n2, n1, s1, s2 = (lat_shift(win, d) for d in (2, 1, -1, -2))
    g, e = call(
        main_kernel, [((2, 16, BR, C), f32, 1), ((8, C), f32, 1)],
        [
            pltpu.VMEM((264, 128), f32),
            pltpu.VMEM((264, 128), f32),
            pltpu.VMEM((3, 256, 128), bf16),
            pltpu.VMEM((192, C), f32),
            pltpu.VMEM((164 * M, C), bf16),
            pltpu.VMEM((108 * M, C), bf16),
            pltpu.VMEM((108 * M, C), f32),
            pltpu.VMEM((108 * M, C), f32),
            pltpu.VMEM((108 * M, 128), f32),
            pltpu.VMEM((108 * M, 128), bf16),
            pltpu.VMEM((112 * M, C), bf16),
            pltpu.VMEM((54 * M, C), f32),
            pltpu.VMEM((64, C), f32),
            pltpu.VMEM((264, 128), f32),
            pltpu.VMEM((M, C), f32),
        ],
        (n2, n1, win, s1, s2, seeds, w_in, w_mid, w_out, w_noise),
        kept=range(10),
        limit=32,
    )
    half, far = sum_all(g[0], g[1], e)
    o_in, o_mid, o_out, o_noise, o_loss = call(
        final_kernel,
        [((9, V, C), f32), ((9, C, C), f32), ((V, C), f32), ((NB, C), f32), ((1, 128), f32)],
        [
            pltpu.VMEM((NB, BR, C), f32),
            pltpu.VMEM((9, C, C), f32),
            pltpu.SemaphoreType.DMA((9,)),
        ],
        (half, far),
        {("out", 1)},
        kept=(0, 1),
    )
    return o_in, o_mid, o_out, o_noise, o_loss[0, 0]


def solution(mesh):
    fine = Mesh(mesh.devices.reshape(8, 2, 4, 2, 2), AX)
    lat = ("y", "c")
    placed = (
        P(None, lat, "xh"), P(None, lat, "xh"), P(lat, "xh"), P(("z", "xl"), None),
        P(), P(), P(), P(),
    )
    return jax.shard_map(
        body, mesh=fine, in_specs=placed, out_specs=(P(), P(), P(), P(), P()), check_vma=False
    )
```

```python
import jax
import jax.numpy as jnp
from jax import lax
from jax.experimental import pallas as pl
from jax.experimental.pallas import tpu as pltpu
from jax.sharding import Mesh, PartitionSpec as P

f32 = jnp.float32
bf16 = jnp.bfloat16
SQ = 0.0625
GC = 0.7978845608028654
GA = 0.044715
V = 100
C = 256
M = 16
TC = 360
WP = 32
WH = 27
ROWS = 104
BR = 112
NB = 32
AX = ("z", "xl", "y", "c", "xh")


def perm(f):
    out = []
    for i in range(256):
        z, xl, lat, xh = i >> 5, (i >> 4) & 1, (i >> 1) & 7, i & 1
        z2, xl2, lat2, xh2 = f(z, xl, lat, xh)
        out.append((i, (z2 % 8) * 32 + xl2 * 16 + lat2 * 2 + xh2))
    return out


def send(v, f):
    return lax.ppermute(v, AX, perm(f))


def lat_shift(v, d):
    def f(z, xl, lat, xh):
        return (z, xl, (lat + d) % 8, xh)

    return send(v, f)


def member_index():
    return lax.axis_index("z") * 2 + lax.axis_index("xl")


def lat_index():
    return lax.axis_index("y") * 2 + lax.axis_index("c")


def params(limit=None):
    return pltpu.CompilerParams(vmem_limit_bytes=(limit or 16) * 1024 * 1024)


def gelu(x):
    t = jnp.tanh(GC * (x + GA * x * x * x))
    return 0.5 * x * (1.0 + t)


def gelu_both(x):
    x2 = x * x
    t = jnp.tanh(GC * (x + GA * x2 * x))
    h = 0.5 * (1.0 + t)
    slope = h + 0.5 * x * (1.0 - t * t) * (GC * (1.0 + 3.0 * GA * x2))
    return x * h, slope


def gelu_slope(x):
    return gelu_both(x)[1]


def prep_kernel(
    state, target, land, seeds, w_in, w_out, w_noise,
    x_out, edge_out, seeds_out, w_in_out, w_out_out, w_noise_out, sc, sems,
):
    moves = [
        pltpu.make_async_copy(w, out, sems.at[i])
        for i, (w, out) in enumerate(((w_in, w_in_out), (w_out, w_out_out), (w_noise, w_noise_out)))
    ]
    for move in moves:
        move.start()
    sc[...] = jnp.zeros(sc.shape, f32)
    edge_out[...] = jnp.zeros(edge_out.shape, f32)
    seeds_out[...] = jnp.broadcast_to(seeds[...], seeds_out.shape)
    for r in range(2):
        x_out[r, 0:8, :] = jnp.zeros((8, 256), f32)
        x_out[r, 8 + TC : 384, :] = jnp.zeros((376 - TC, 256), f32)
        sc[0:V, 0:TC] = state[:, r, :].astype(f32)
        sc[104:105, 0:TC] = 1.0 + land[r : r + 1, :].astype(f32)
        x_out[r, 8 : 8 + TC, 0:128] = sc[...].T[0:TC]
        sc[0:V, 0:TC] = target[:, r, :].astype(f32)
        x_out[r, 8 : 8 + TC, 128:256] = sc[...].T[0:TC]
        edge_out[16 * r : 16 * r + 3, :] = x_out[r, TC + 5 : TC + 8, :]
        edge_out[16 * r + 10 : 16 * r + 13, :] = x_out[r, 8:11, :]
    for move in moves:
        move.wait()


def window_kernel(x, edge, win):
    m = member_index()
    start = (45 * m) // 2
    row = lax.broadcasted_iota(jnp.int32, (16, 256), 0)
    low = (row < 3) & (m == 0)
    high = (row >= 10) & (row < 13) & (m == M - 1)
    for r in range(2):
        base = pl.multiple_of(((start + 5) // 8) * 8, 8)
        near = x[r, pl.ds(base, WP + 8), :]
        w = pltpu.roll(near, WP + 8 - (start + 5 - base), 0)[0:WP]
        e = edge[16 * r : 16 * r + 16, :]
        win[WP * r : WP * r + 16, :] = jnp.where(low, e, w[0:16]).astype(bf16)
        win[WP * r + 16 : WP * r + 32, :] = jnp.where(high, e, w[16:32]).astype(bf16)


def main_kernel(
    n2, n1, own, s1, s2, seeds, w_in, w_mid, w_out, w_noise, g_out, e_out,
    S, T, SB, PB, HID, HO, SL, UP, OUT, DO, DM, INC, DS, QB, BIAS,
):
    own22 = member_index() % 2
    lat = lat_index()
    core = lax.axis_index("c")
    rows = ((n2, 1, -2), (n1, 0, -1), (n1, 1, -1), (own, 0, 0), (own, 1, 0),
            (s1, 0, 1), (s1, 1, 1), (s2, 0, 2))
    for k, (ref, r, d) in enumerate(rows):
        inside = (lat + d >= 0) & (lat + d < 8)
        row = ref[WP * r : WP * r + WP, :].astype(f32) * jnp.where(inside, 1.0, 0.0)
        S[WP * k : WP * k + WP, :] = row[:, 0:128]
        T[WP * k : WP * k + WP, :] = row[:, 128:256]
    S[256:264, :] = jnp.zeros((8, 128), f32)
    T[256:264, :] = jnp.zeros((8, 128), f32)
    QB[...] = jnp.broadcast_to(S[:, 104:105], QB.shape)
    for b in range(3):
        SB[b] = S[b : b + 256, :].astype(bf16)
    latents = (seeds[...].astype(f32) - 32767.5) / 18918.0
    BIAS[...] = jnp.dot(
        latents, w_noise[...], precision=lax.Precision.HIGHEST, preferred_element_type=f32
    )
    acc = None
    for a in range(3):
        for b in range(3):
            part = jnp.dot(
                SB[b, a * 32 : a * 32 + 192, 0:V], w_in[3 * a + b], preferred_element_type=f32
            )
            acc = part if acc is None else acc + part
    PB[...] = acc

    bias = BIAS[...]
    HID[162 * M : 164 * M, :] = jnp.zeros((2 * M, C), bf16)
    for r in range(6):
        gr = lat * 2 - 2 + r
        valid = jnp.where((gr >= 0) & (gr < 16), 1.0, 0.0).astype(f32)

        def hid_cell(i, carry, r=r, valid=valid):
            row = PB[pl.ds(r * 32 + i, 1), :]
            h = gelu(jnp.broadcast_to(row, (M, C)) + bias) * valid
            HID[pl.ds(pl.multiple_of((r * WH + i) * M, M), M), :] = h.astype(bf16)
            return carry

        lax.fori_loop(0, WH, hid_cell, 0, unroll=27)

    NR = WH * M

    MC = 54 * M

    def mid_row(r, carry):
        base = pl.multiple_of(r * MC, M)
        lhs = jnp.concatenate(
            [
                HID[pl.ds(pl.multiple_of(base + (a * WH + b) * M, M), MC), :]
                for a in range(3)
                for b in range(3)
            ],
            axis=1,
        )
        pre = jnp.dot(lhs, w_mid[...].reshape(9 * C, C), preferred_element_type=f32)
        act, slope = gelu_both(pre)
        hid = HID[pl.ds(pl.multiple_of(base + (WH + 1) * M, M), MC), :].astype(f32)
        ho = (act + hid).astype(bf16)
        HO[pl.ds(base, MC), :] = ho
        SL[pl.ds(base, MC), :] = slope
        OUT[pl.ds(base, MC), 0:V] = lax.dot_general(
            ho, w_out[...], (((1,), (1,)), ((), ())), preferred_element_type=f32
        )
        return carry

    lax.fori_loop(0, 2, mid_row, 0)

    def cell_terms(r, i, with_loss):
        base = pl.multiple_of((r * WH + i) * M, M)
        srow = (r + 2) * 32 + i + 2
        st = S[pl.ds(srow, 1), :]
        tg = T[pl.ds(srow, 1), :]
        q = QB[pl.ds(srow, 1), :]
        o = (OUT[pl.ds(base, M), :] + st).astype(bf16).astype(f32)
        miss = o - tg
        e = miss * miss + SQ
        inv = lax.rsqrt(e)
        slope = miss * inv
        dist = e * inv - 0.25 if with_loss else None
        total = None
        spread = None
        for k in range(1, 9):
            u = o - pltpu.roll(o, k, 0)
            e = u * u + SQ
            inv = lax.rsqrt(e)
            s = u * inv
            if k < 8:
                s = s - pltpu.roll(s, M - k, 0)
            total = s if total is None else total + s
            if with_loss:
                d = e * inv - 0.25
                if k == 8:
                    d = 0.5 * d
                spread = d if spread is None else spread + d
        g = q * (slope * (1.0 / M) - total * (1.0 / (M * (M - 1))))
        DO[pl.ds(base, M), :] = g.astype(bf16)
        if with_loss:
            return q * (dist * (1.0 / M) - spread * (1.0 / (M * (M - 1))))
        return None

    loss = jnp.zeros((M, 128), f32)
    for r in (1, 2):

        def loss_cell(i, total, r=r):
            term = cell_terms(r, i, True)
            mine = (i >= 1) & ((i < 23) | ((i == 23) & (own22 > 0)))
            return total + jnp.where(mine, 1.0, 0.0) * term

        loss = lax.fori_loop(0, WH, loss_cell, loss, unroll=9)
    for r in (0, 3):

        def grad_cell(i, carry, r=r):
            cell_terms(r, i, False)
            return carry

        lax.fori_loop(0, WH, grad_cell, 0, unroll=9)
    lane = lax.broadcasted_iota(jnp.int32, (M, 128), 1)
    loss = jnp.sum(jnp.sum(jnp.where(lane < V, loss, 0.0), axis=0, keepdims=True), axis=1, keepdims=True)

    UP[...] = jnp.dot(DO[:, 0:V], w_out[...], preferred_element_type=f32)

    def mid_cell(i, carry):
        at = pl.multiple_of(i * 2 * M, M)
        DM[pl.ds(at, 2 * M), :] = (UP[pl.ds(at, 2 * M), :] * SL[pl.ds(at, 2 * M), :]).astype(bf16)
        return carry

    lax.fori_loop(0, 54, mid_cell, 0, unroll=6)
    DM[108 * M : 112 * M, :] = jnp.zeros((4 * M, C), bf16)

    wcat = jnp.concatenate([w_mid[t] for t in range(9)], axis=1)
    for r in range(2):
        lhs = jnp.concatenate(
            [
                DM[((r + 2 - a) * WH + 2 - b) * M : ((r + 2 - a) * WH + 2 - b) * M + NR, :]
                for a in range(3)
                for b in range(3)
            ],
            axis=1,
        )
        INC[r * NR : (r + 1) * NR, :] = lax.dot_general(
            lhs, wcat, (((1,), (1,)), ((), ())), preferred_element_type=f32
        )
    DS[...] = jnp.zeros(DS.shape, f32)
    dsum = jnp.zeros((M, C), f32)
    for r in range(2):

        def in_cell(i, total, r=r):
            x = jnp.broadcast_to(PB[pl.ds((r + 2) * 32 + i + 2, 1), :], (M, C)) + bias
            base = pl.multiple_of((r * WH + i) * M, M)
            upb = pl.multiple_of(((r + 1) * WH + 1 + i) * M, M)
            d = (INC[pl.ds(base, M), :] + UP[pl.ds(upb, M), :]) * gelu_slope(x)
            mine = jnp.where((i < 22) | (own22 > 0), 1.0, 0.0)
            d = d.astype(bf16).astype(f32) * mine
            DS[pl.ds(r * 32 + i + 2, 1), :] = jnp.sum(d, axis=0, keepdims=True)
            return total + d

        dsum = lax.fori_loop(0, 23, in_cell, dsum, unroll=4)

    def store(k, lo, hi, value):
        g_out[(k // 16) ^ core, k % 16, lo:hi, :] = value

    g_out[:, :, ROWS:BR, :] = jnp.zeros((2, 16, BR - ROWS, C), f32)
    peaks = []

    def put(row, value):
        done = 0
        n = value.shape[0]
        peaks.append(jnp.max(jnp.abs(value), axis=0, keepdims=True))
        while done < n:
            k, i = divmod(row + done, ROWS)
            take = min(n - done, ROWS - i)
            store(k, i, i + take, value[done : done + take, :])
            done += take

    cell = lax.broadcasted_iota(jnp.int32, (NR, C), 0) >> 4
    mine = (cell < 22) | ((cell == 22) & (own22 > 0))
    start = (WH + 1) * M
    dmc = jnp.concatenate(
        [
            jnp.where(mine, DM[start + r * NR : start + (r + 1) * NR, :].astype(f32), 0.0)
            for r in range(2)
        ],
        axis=0,
    )
    dmt = dmc.T.astype(bf16)
    for a in range(3):
        for b in range(3):
            hs = ((a + 1) * WH + b + 1) * M
            g = jnp.dot(dmt, HID[hs : hs + 2 * NR, :], preferred_element_type=f32)
            put((3 * a + b) * C, g.T)
    doc = jnp.concatenate(
        [
            jnp.where(
                mine[:, 0:128], DO[start + r * NR : start + (r + 1) * NR, :].astype(f32), 0.0
            )
            for r in range(2)
        ],
        axis=0,
    )
    dot_ = doc.T.astype(bf16)
    go = jnp.dot(dot_, HO[start : start + 2 * NR, :], preferred_element_type=f32)
    ds = DS[...]
    hi = ds.astype(bf16)
    lo = (ds - hi.astype(f32)).astype(bf16)
    both = jnp.concatenate([hi, lo], axis=1)
    for a in range(3):
        for b in range(3):
            g = lax.dot_general(
                SB[b, (a + 2) * 32 : (a + 2) * 32 + 64, :], both,
                (((0,), (0,)), ((), ())), preferred_element_type=f32,
            )
            put(9 * C + V * (3 * a + b), (g[:, 0:C] + g[:, C : 2 * C])[0:V, :])
    put(9 * C + 9 * V, go[0:V, :])
    put(9 * C + 10 * V, jnp.zeros((NB * ROWS - 9 * C - 10 * V, C), f32))
    gn = lax.dot_general(
        latents, dsum, (((0,), (0,)), ((), ())),
        precision=lax.Precision.HIGHEST, preferred_element_type=f32,
    )
    peaks.append(jnp.max(jnp.abs(gn), axis=0, keepdims=True))
    for k in range(NB):
        store(k, ROWS, ROWS + 1, gn[k : k + 1, :])
    loss = jnp.broadcast_to(loss * (1.0 / (V * 16 * 720)), (1, C))
    first = loss.astype(bf16).astype(f32)
    store(0, ROWS + 1, ROWS + 2, first)
    store(0, ROWS + 2, ROWS + 3, loss - first)
    peaks.append(jnp.abs(loss))
    peak = peaks[0]
    for p in peaks[1:]:
        peak = jnp.maximum(peak, p)
    peak = jnp.broadcast_to(jnp.max(peak, axis=1, keepdims=True), (8, C))
    e_out[...] = exponent(peak)


def exponent(bound):
    return jnp.ceil(jnp.log2(jnp.maximum(bound, 1e-30)))


def final_kernel(half, far, o_in, o_mid, o_out, o_noise, o_loss, t, u, out_sems):
    core = lax.axis_index("c")
    for slot, ref in ((core, half), (1 - core, far)):
        for k in range(16):
            f = jnp.exp2(ref[k, BR - 1 : BR, :] - 14.0)
            t[slot * 16 + k] = ref[k] * f

    def get(row, n):
        parts = []
        done = 0
        while done < n:
            k, i = divmod(row + done, ROWS)
            take = min(n - done, ROWS - i)
            parts.append((done, take, k, i))
            done += take
        return parts

    def scale_of(pieces, count):
        total = jnp.zeros((8, C), f32)
        ragged = jnp.zeros((1, C), f32)
        for p in pieces:
            for _, take, k, i in p:
                v = t[k, i : i + take, :]
                v = v * v
                if take % 8 == 0:
                    total = total + jnp.sum(v.reshape(take // 8, 8, C), axis=0)
                else:
                    ragged = ragged + jnp.sum(v, axis=0, keepdims=True)
        total = jnp.sum(total, axis=0, keepdims=True) + ragged
        ms = jnp.sum(total, axis=1, keepdims=True) * (1.0 / count)
        return lax.rsqrt(ms + 1e-6)

    moves = []

    def emit(pieces, scale, buf, out, k):
        for done, take, b, i in pieces:
            buf[done : done + take, :] = t[b, i : i + take, :] * scale
        if out is not None:
            move = pltpu.make_async_copy(buf, out, out_sems.at[k])
            move.start()
            moves.append(move)

    pieces = [get(C * k, C) for k in range(9)]
    scale = scale_of(pieces, 9 * C * C)
    for k in range(9):
        emit(pieces[k], scale, u.at[k], o_mid.at[k], k)
    pieces = [get(9 * C + V * k, V) for k in range(9)]
    scale = scale_of(pieces, 9 * V * C)
    for k in range(9):
        emit(pieces[k], scale, o_in.at[k], None, 0)
    pieces = get(9 * C + 9 * V, V)
    emit(pieces, scale_of([pieces], V * C), o_out, None, 0)
    pieces = [(k, 1, k, ROWS) for k in range(NB)]
    emit(pieces, scale_of([pieces], NB * C), o_noise, None, 0)
    o_loss[...] = t[0, ROWS + 1 : ROWS + 2, 0:128] + t[0, ROWS + 2 : ROWS + 3, 0:128]
    for move in moves:
        move.wait()


def call(kernel, outs, scratch, ins, place=None, kept=(), limit=None):
    place = place or {}
    vmem = pl.BlockSpec(memory_space=pltpu.VMEM)
    left = pl.BlockSpec(memory_space=pl.ANY)
    ins = [
        pltpu.with_memory_space_constraint(v, pltpu.VMEM if i in kept else pltpu.HBM)
        for i, v in enumerate(ins)
    ]
    return pl.pallas_call(
        kernel,
        out_shape=[
            pltpu.VMEM(o[0], o[1]) if len(o) > 2 else jax.ShapeDtypeStruct(*o) for o in outs
        ],
        in_specs=[left if ("in", i) in place else vmem for i in range(len(ins))],
        out_specs=[left if ("out", i) in place else vmem for i in range(len(outs))],
        scratch_shapes=scratch,
        compiler_params=params(limit),
    )(*ins)


f16 = jnp.float16


def is_last():
    return (jnp.arange(BR, dtype=jnp.int32) == BR - 1)[:, None]


def coded(s):
    e = exponent(s[BR - 1 : BR, :])
    return jnp.where(is_last(), e, s * jnp.exp2(14.0 - e)).astype(f16)


def decoded(msg):
    q = jnp.exp2(msg[..., BR - 1 : BR, :].astype(f32) - 14.0)
    return jnp.where(is_last(), 2.0**14, msg.astype(f32)) * q


def sum_all(mine, theirs, e):
    xy = ("xl", "y", "xh")

    def other(z, xl, lat, xh):
        return (z, xl, lat ^ 1, xh)

    e = (jnp.maximum(e, send(e, other)) + 1.0)[0:1]
    tag = jnp.where(is_last(), e, 0.0)
    s = (mine + send(theirs, other)) * jnp.exp2(14.0 - e)[None] + tag[None]
    got = lax.all_to_all(s.astype(f16), xy, 0, 0, tiled=True)
    s = jnp.sum(decoded(got), axis=0)
    s = coded(s)
    r0, r1, r2, r3 = (
        decoded(send(s, lambda z, xl, lat, xh, k=k: (z ^ k, xl, lat, xh)) if k else s)
        for k in range(4)
    )
    s = coded((r0 + r1) + (r2 + r3))
    s = coded(decoded(s) + decoded(send(s, lambda z, xl, lat, xh: (7 - z, xl, lat, xh))))
    half = lax.all_to_all(jnp.broadcast_to(s[None], (16,) + s.shape), xy, 0, 0, tiled=True)
    far = send(half, other)
    return half.astype(f32), far.astype(f32)


def body(state, target, land, seeds, w_in, w_mid, w_out, w_noise):
    x, edge, seeds, w_in, w_out, w_noise = call(
        prep_kernel,
        [
            ((2, 384, 256), f32, 1), ((32, 256), f32, 1), ((M, 32), jnp.int32, 1),
            ((9, V, C), bf16, 1), ((V, C), bf16, 1), ((NB, C), f32, 1),
        ],
        [pltpu.VMEM((128, 384), f32), pltpu.SemaphoreType.DMA((3,))],
        (state, target, land, seeds, w_in, w_out, w_noise),
        {("in", 4), ("in", 5), ("in", 6)},
    )
    edge = send(edge, lambda z, xl, lat, xh: (z, xl, lat, xh ^ 1))
    seeds = lax.all_to_all(seeds, ("z", "xl"), 0, 0, tiled=True)
    (win,) = call(window_kernel, [((2 * WP, 256), bf16, 1)], [], (x, edge), kept=(0, 1))
    win, seeds = lax.optimization_barrier((win, seeds))
    n2, n1, s1, s2 = (lat_shift(win, d) for d in (2, 1, -1, -2))
    g, e = call(
        main_kernel, [((2, 16, BR, C), f32, 1), ((8, C), f32, 1)],
        [
            pltpu.VMEM((264, 128), f32),
            pltpu.VMEM((264, 128), f32),
            pltpu.VMEM((3, 256, 128), bf16),
            pltpu.VMEM((192, C), f32),
            pltpu.VMEM((164 * M, C), bf16),
            pltpu.VMEM((108 * M, C), bf16),
            pltpu.VMEM((108 * M, C), f32),
            pltpu.VMEM((108 * M, C), f32),
            pltpu.VMEM((108 * M, 128), f32),
            pltpu.VMEM((108 * M, 128), bf16),
            pltpu.VMEM((112 * M, C), bf16),
            pltpu.VMEM((54 * M, C), f32),
            pltpu.VMEM((64, C), f32),
            pltpu.VMEM((264, 128), f32),
            pltpu.VMEM((M, C), f32),
        ],
        (n2, n1, win, s1, s2, seeds, w_in, w_mid, w_out, w_noise),
        kept=range(10),
        limit=32,
    )
    half, far = sum_all(g[0], g[1], e)
    o_in, o_mid, o_out, o_noise, o_loss = call(
        final_kernel,
        [((9, V, C), f32), ((9, C, C), f32), ((V, C), f32), ((NB, C), f32), ((1, 128), f32)],
        [
            pltpu.VMEM((NB, BR, C), f32),
            pltpu.VMEM((9, C, C), f32),
            pltpu.SemaphoreType.DMA((9,)),
        ],
        (half, far),
        {("out", 1)},
        kept=(0, 1),
    )
    return o_in, o_mid, o_out, o_noise, o_loss[0, 0]


def solution(mesh):
    fine = Mesh(mesh.devices.reshape(8, 2, 4, 2, 2), AX)
    lat = ("y", "c")
    placed = (
        P(None, lat, "xh"), P(None, lat, "xh"), P(lat, "xh"), P(("z", "xl"), None),
        P(), P(), P(), P(),
    )
    return jax.shard_map(
        body, mesh=fine, in_specs=placed, out_specs=(P(), P(), P(), P(), P()), check_vma=False
    )
```

```python
import jax
import jax.numpy as jnp
from jax import lax
from jax.experimental import pallas as pl
from jax.experimental.pallas import tpu as pltpu
from jax.sharding import Mesh, PartitionSpec as P

f32 = jnp.float32
bf16 = jnp.bfloat16
SQ = 0.0625
GC = 0.7978845608028654
GA = 0.044715
V = 100
C = 256
M = 16
TC = 360
WP = 32
WH = 27
ROWS = 104
BR = 112
NB = 32
AX = ("z", "xl", "y", "c", "xh")


def perm(f):
    out = []
    for i in range(256):
        z, xl, lat, xh = i >> 5, (i >> 4) & 1, (i >> 1) & 7, i & 1
        z2, xl2, lat2, xh2 = f(z, xl, lat, xh)
        out.append((i, (z2 % 8) * 32 + xl2 * 16 + lat2 * 2 + xh2))
    return out


def send(v, f):
    return lax.ppermute(v, AX, perm(f))


def lat_shift(v, d):
    def f(z, xl, lat, xh):
        return (z, xl, (lat + d) % 8, xh)

    return send(v, f)


def member_index():
    return lax.axis_index("z") * 2 + lax.axis_index("xl")


def lat_index():
    return lax.axis_index("y") * 2 + lax.axis_index("c")


def params(limit=None):
    return pltpu.CompilerParams(vmem_limit_bytes=(limit or 16) * 1024 * 1024)


def gelu(x):
    t = jnp.tanh(GC * (x + GA * x * x * x))
    return 0.5 * x * (1.0 + t)


def gelu_both(x):
    x2 = x * x
    t = jnp.tanh(GC * (x + GA * x2 * x))
    h = 0.5 * (1.0 + t)
    slope = h + 0.5 * x * (1.0 - t * t) * (GC * (1.0 + 3.0 * GA * x2))
    return x * h, slope


def gelu_slope(x):
    return gelu_both(x)[1]


def prep_kernel(
    state, target, land, seeds, w_in, w_out, w_noise,
    x_out, edge_out, seeds_out, w_in_out, w_out_out, w_noise_out, sc, sems,
):
    moves = [
        pltpu.make_async_copy(w, out, sems.at[i])
        for i, (w, out) in enumerate(((w_in, w_in_out), (w_out, w_out_out), (w_noise, w_noise_out)))
    ]
    for move in moves:
        move.start()
    sc[...] = jnp.zeros(sc.shape, f32)
    edge_out[...] = jnp.zeros(edge_out.shape, f32)
    seeds_out[...] = jnp.broadcast_to(seeds[...], seeds_out.shape)
    for r in range(2):
        x_out[r, 0:8, :] = jnp.zeros((8, 256), f32)
        x_out[r, 8 + TC : 384, :] = jnp.zeros((376 - TC, 256), f32)
        sc[0:V, 0:TC] = state[:, r, :].astype(f32)
        sc[104:105, 0:TC] = 1.0 + land[r : r + 1, :].astype(f32)
        x_out[r, 8 : 8 + TC, 0:128] = sc[...].T[0:TC]
        sc[0:V, 0:TC] = target[:, r, :].astype(f32)
        x_out[r, 8 : 8 + TC, 128:256] = sc[...].T[0:TC]
        edge_out[16 * r : 16 * r + 3, :] = x_out[r, TC + 5 : TC + 8, :]
        edge_out[16 * r + 10 : 16 * r + 13, :] = x_out[r, 8:11, :]
    for move in moves:
        move.wait()


def window_kernel(x, edge, win):
    m = member_index()
    start = (45 * m) // 2
    row = lax.broadcasted_iota(jnp.int32, (16, 256), 0)
    low = (row < 3) & (m == 0)
    high = (row >= 10) & (row < 13) & (m == M - 1)
    for r in range(2):
        base = pl.multiple_of(((start + 5) // 8) * 8, 8)
        near = x[r, pl.ds(base, WP + 8), :]
        w = pltpu.roll(near, WP + 8 - (start + 5 - base), 0)[0:WP]
        e = edge[16 * r : 16 * r + 16, :]
        win[WP * r : WP * r + 16, :] = jnp.where(low, e, w[0:16]).astype(bf16)
        win[WP * r + 16 : WP * r + 32, :] = jnp.where(high, e, w[16:32]).astype(bf16)


def main_kernel(
    n2, next_chip, own, near, s2, seeds, w_in, w_mid, w_out, w_noise, g_out, e_out,
    S, T, SB, PB, HID, HO, SL, UP, OUT, DO, DM, INC, DS, QB, BIAS,
):
    own22 = member_index() % 2
    lat = lat_index()
    core = lax.axis_index("c")
    rows = (
        (n2, n2, 1, -2), (next_chip, near, 0, -1), (next_chip, near, 1, -1), (own, own, 0, 0),
        (own, own, 1, 0), (near, next_chip, 0, 1), (near, next_chip, 1, 1), (s2, s2, 0, 2),
    )
    for k, (first, second, r, d) in enumerate(rows):
        inside = jnp.where((lat + d >= 0) & (lat + d < 8), 1.0, 0.0)
        row = first[WP * r : WP * r + WP, :].astype(f32)
        if second is not first:
            row = jnp.where(core == 0, row, second[WP * r : WP * r + WP, :].astype(f32))
        row = row * inside
        S[WP * k : WP * k + WP, :] = row[:, 0:128]
        T[WP * k : WP * k + WP, :] = row[:, 128:256]
    S[256:264, :] = jnp.zeros((8, 128), f32)
    T[256:264, :] = jnp.zeros((8, 128), f32)
    QB[...] = jnp.broadcast_to(S[:, 104:105], QB.shape)
    for b in range(3):
        SB[b] = S[b : b + 256, :].astype(bf16)
    latents = (seeds[...].astype(f32) - 32767.5) / 18918.0
    BIAS[...] = jnp.dot(
        latents, w_noise[...], precision=lax.Precision.HIGHEST, preferred_element_type=f32
    )
    acc = None
    for a in range(3):
        for b in range(3):
            part = jnp.dot(
                SB[b, a * 32 : a * 32 + 192, 0:V], w_in[3 * a + b], preferred_element_type=f32
            )
            acc = part if acc is None else acc + part
    PB[...] = acc

    bias = BIAS[...]
    HID[162 * M : 164 * M, :] = jnp.zeros((2 * M, C), bf16)
    for r in range(6):
        gr = lat * 2 - 2 + r
        valid = jnp.where((gr >= 0) & (gr < 16), 1.0, 0.0).astype(f32)

        def hid_cell(i, carry, r=r, valid=valid):
            row = PB[pl.ds(r * 32 + i, 1), :]
            h = gelu(jnp.broadcast_to(row, (M, C)) + bias) * valid
            HID[pl.ds(pl.multiple_of((r * WH + i) * M, M), M), :] = h.astype(bf16)
            return carry

        lax.fori_loop(0, WH, hid_cell, 0, unroll=27)

    NR = WH * M

    MC = 54 * M

    def mid_row(r, carry):
        base = pl.multiple_of(r * MC, M)
        lhs = jnp.concatenate(
            [
                HID[pl.ds(pl.multiple_of(base + (a * WH + b) * M, M), MC), :]
                for a in range(3)
                for b in range(3)
            ],
            axis=1,
        )
        pre = jnp.dot(lhs, w_mid[...].reshape(9 * C, C), preferred_element_type=f32)
        act, slope = gelu_both(pre)
        hid = HID[pl.ds(pl.multiple_of(base + (WH + 1) * M, M), MC), :].astype(f32)
        ho = (act + hid).astype(bf16)
        HO[pl.ds(base, MC), :] = ho
        SL[pl.ds(base, MC), :] = slope
        OUT[pl.ds(base, MC), 0:V] = lax.dot_general(
            ho, w_out[...], (((1,), (1,)), ((), ())), preferred_element_type=f32
        )
        return carry

    lax.fori_loop(0, 2, mid_row, 0)

    def cell_terms(r, i, with_loss):
        base = pl.multiple_of((r * WH + i) * M, M)
        srow = (r + 2) * 32 + i + 2
        st = S[pl.ds(srow, 1), :]
        tg = T[pl.ds(srow, 1), :]
        q = QB[pl.ds(srow, 1), :]
        o = (OUT[pl.ds(base, M), :] + st).astype(bf16).astype(f32)
        miss = o - tg
        e = miss * miss + SQ
        inv = lax.rsqrt(e)
        slope = miss * inv
        dist = e * inv - 0.25 if with_loss else None
        total = None
        spread = None
        for k in range(1, 9):
            u = o - pltpu.roll(o, k, 0)
            e = u * u + SQ
            inv = lax.rsqrt(e)
            s = u * inv
            if k < 8:
                s = s - pltpu.roll(s, M - k, 0)
            total = s if total is None else total + s
            if with_loss:
                d = e * inv - 0.25
                if k == 8:
                    d = 0.5 * d
                spread = d if spread is None else spread + d
        g = q * (slope * (1.0 / M) - total * (1.0 / (M * (M - 1))))
        DO[pl.ds(base, M), :] = g.astype(bf16)
        if with_loss:
            return q * (dist * (1.0 / M) - spread * (1.0 / (M * (M - 1))))
        return None

    loss = jnp.zeros((M, 128), f32)
    for r in (1, 2):

        def loss_cell(i, total, r=r):
            term = cell_terms(r, i, True)
            mine = (i >= 1) & ((i < 23) | ((i == 23) & (own22 > 0)))
            return total + jnp.where(mine, 1.0, 0.0) * term

        loss = lax.fori_loop(0, WH, loss_cell, loss, unroll=9)
    for r in (0, 3):

        def grad_cell(i, carry, r=r):
            cell_terms(r, i, False)
            return carry

        lax.fori_loop(0, WH, grad_cell, 0, unroll=9)
    lane = lax.broadcasted_iota(jnp.int32, (M, 128), 1)
    loss = jnp.sum(jnp.sum(jnp.where(lane < V, loss, 0.0), axis=0, keepdims=True), axis=1, keepdims=True)

    UP[...] = jnp.dot(DO[:, 0:V], w_out[...], preferred_element_type=f32)

    def mid_cell(i, carry):
        at = pl.multiple_of(i * 2 * M, M)
        DM[pl.ds(at, 2 * M), :] = (UP[pl.ds(at, 2 * M), :] * SL[pl.ds(at, 2 * M), :]).astype(bf16)
        return carry

    lax.fori_loop(0, 54, mid_cell, 0, unroll=6)
    DM[108 * M : 112 * M, :] = jnp.zeros((4 * M, C), bf16)

    wcat = jnp.concatenate([w_mid[t] for t in range(9)], axis=1)
    for r in range(2):
        lhs = jnp.concatenate(
            [
                DM[((r + 2 - a) * WH + 2 - b) * M : ((r + 2 - a) * WH + 2 - b) * M + NR, :]
                for a in range(3)
                for b in range(3)
            ],
            axis=1,
        )
        INC[r * NR : (r + 1) * NR, :] = lax.dot_general(
            lhs, wcat, (((1,), (1,)), ((), ())), preferred_element_type=f32
        )
    DS[...] = jnp.zeros(DS.shape, f32)
    dsum = jnp.zeros((M, C), f32)
    for r in range(2):

        def in_cell(i, total, r=r):
            x = jnp.broadcast_to(PB[pl.ds((r + 2) * 32 + i + 2, 1), :], (M, C)) + bias
            base = pl.multiple_of((r * WH + i) * M, M)
            upb = pl.multiple_of(((r + 1) * WH + 1 + i) * M, M)
            d = (INC[pl.ds(base, M), :] + UP[pl.ds(upb, M), :]) * gelu_slope(x)
            mine = jnp.where((i < 22) | (own22 > 0), 1.0, 0.0)
            d = d.astype(bf16).astype(f32) * mine
            DS[pl.ds(r * 32 + i + 2, 1), :] = jnp.sum(d, axis=0, keepdims=True)
            return total + d

        dsum = lax.fori_loop(0, 23, in_cell, dsum, unroll=4)

    def store(k, lo, hi, value):
        g_out[(k // 16) ^ core, k % 16, lo:hi, :] = value

    g_out[:, :, ROWS:BR, :] = jnp.zeros((2, 16, BR - ROWS, C), f32)
    peaks = []

    def put(row, value):
        done = 0
        n = value.shape[0]
        peaks.append(jnp.max(jnp.abs(value), axis=0, keepdims=True))
        while done < n:
            k, i = divmod(row + done, ROWS)
            take = min(n - done, ROWS - i)
            store(k, i, i + take, value[done : done + take, :])
            done += take

    cell = lax.broadcasted_iota(jnp.int32, (NR, C), 0) >> 4
    mine = (cell < 22) | ((cell == 22) & (own22 > 0))
    start = (WH + 1) * M
    dmc = jnp.concatenate(
        [
            jnp.where(mine, DM[start + r * NR : start + (r + 1) * NR, :].astype(f32), 0.0)
            for r in range(2)
        ],
        axis=0,
    )
    dmt = dmc.T.astype(bf16)
    for a in range(3):
        for b in range(3):
            hs = ((a + 1) * WH + b + 1) * M
            g = jnp.dot(dmt, HID[hs : hs + 2 * NR, :], preferred_element_type=f32)
            put((3 * a + b) * C, g.T)
    doc = jnp.concatenate(
        [
            jnp.where(
                mine[:, 0:128], DO[start + r * NR : start + (r + 1) * NR, :].astype(f32), 0.0
            )
            for r in range(2)
        ],
        axis=0,
    )
    dot_ = doc.T.astype(bf16)
    go = jnp.dot(dot_, HO[start : start + 2 * NR, :], preferred_element_type=f32)
    ds = DS[...]
    hi = ds.astype(bf16)
    lo = (ds - hi.astype(f32)).astype(bf16)
    both = jnp.concatenate([hi, lo], axis=1)
    for a in range(3):
        for b in range(3):
            g = lax.dot_general(
                SB[b, (a + 2) * 32 : (a + 2) * 32 + 64, :], both,
                (((0,), (0,)), ((), ())), preferred_element_type=f32,
            )
            put(9 * C + V * (3 * a + b), (g[:, 0:C] + g[:, C : 2 * C])[0:V, :])
    put(9 * C + 9 * V, go[0:V, :])
    put(9 * C + 10 * V, jnp.zeros((NB * ROWS - 9 * C - 10 * V, C), f32))
    gn = lax.dot_general(
        latents, dsum, (((0,), (0,)), ((), ())),
        precision=lax.Precision.HIGHEST, preferred_element_type=f32,
    )
    peaks.append(jnp.max(jnp.abs(gn), axis=0, keepdims=True))
    for k in range(NB):
        store(k, ROWS, ROWS + 1, gn[k : k + 1, :])
    loss = jnp.broadcast_to(loss * (1.0 / (V * 16 * 720)), (1, C))
    first = loss.astype(bf16).astype(f32)
    store(0, ROWS + 1, ROWS + 2, first)
    store(0, ROWS + 2, ROWS + 3, loss - first)
    peaks.append(jnp.abs(loss))
    peak = peaks[0]
    for p in peaks[1:]:
        peak = jnp.maximum(peak, p)
    peak = jnp.broadcast_to(jnp.max(peak, axis=1, keepdims=True), (8, C))
    e_out[...] = exponent(peak)


def exponent(bound):
    return jnp.ceil(jnp.log2(jnp.maximum(bound, 1e-30)))


def final_kernel(half, far, o_in, o_mid, o_out, o_noise, o_loss, t, u, out_sems):
    core = lax.axis_index("c")
    for slot, ref in ((core, half), (1 - core, far)):
        for k in range(16):
            f = jnp.exp2(ref[k, BR - 1 : BR, :] - 14.0)
            t[slot * 16 + k] = ref[k] * f

    def get(row, n):
        parts = []
        done = 0
        while done < n:
            k, i = divmod(row + done, ROWS)
            take = min(n - done, ROWS - i)
            parts.append((done, take, k, i))
            done += take
        return parts

    def scale_of(pieces, count):
        total = jnp.zeros((8, C), f32)
        ragged = jnp.zeros((1, C), f32)
        for p in pieces:
            for _, take, k, i in p:
                v = t[k, i : i + take, :]
                v = v * v
                if take % 8 == 0:
                    total = total + jnp.sum(v.reshape(take // 8, 8, C), axis=0)
                else:
                    ragged = ragged + jnp.sum(v, axis=0, keepdims=True)
        total = jnp.sum(total, axis=0, keepdims=True) + ragged
        ms = jnp.sum(total, axis=1, keepdims=True) * (1.0 / count)
        return lax.rsqrt(ms + 1e-6)

    moves = []

    def emit(pieces, scale, buf, out, k):
        for done, take, b, i in pieces:
            buf[done : done + take, :] = t[b, i : i + take, :] * scale
        if out is not None:
            move = pltpu.make_async_copy(buf, out, out_sems.at[k])
            move.start()
            moves.append(move)

    pieces = [get(C * k, C) for k in range(9)]
    scale = scale_of(pieces, 9 * C * C)
    for k in range(9):
        emit(pieces[k], scale, u.at[k], o_mid.at[k], k)
    pieces = [get(9 * C + V * k, V) for k in range(9)]
    scale = scale_of(pieces, 9 * V * C)
    for k in range(9):
        emit(pieces[k], scale, o_in.at[k], None, 0)
    pieces = get(9 * C + 9 * V, V)
    emit(pieces, scale_of([pieces], V * C), o_out, None, 0)
    pieces = [(k, 1, k, ROWS) for k in range(NB)]
    emit(pieces, scale_of([pieces], NB * C), o_noise, None, 0)
    o_loss[...] = t[0, ROWS + 1 : ROWS + 2, 0:128] + t[0, ROWS + 2 : ROWS + 3, 0:128]
    for move in moves:
        move.wait()


def call(kernel, outs, scratch, ins, place=None, kept=(), limit=None):
    place = place or {}
    vmem = pl.BlockSpec(memory_space=pltpu.VMEM)
    left = pl.BlockSpec(memory_space=pl.ANY)
    ins = [
        pltpu.with_memory_space_constraint(v, pltpu.VMEM if i in kept else pltpu.HBM)
        for i, v in enumerate(ins)
    ]
    return pl.pallas_call(
        kernel,
        out_shape=[
            pltpu.VMEM(o[0], o[1]) if len(o) > 2 else jax.ShapeDtypeStruct(*o) for o in outs
        ],
        in_specs=[left if ("in", i) in place else vmem for i in range(len(ins))],
        out_specs=[left if ("out", i) in place else vmem for i in range(len(outs))],
        scratch_shapes=scratch,
        compiler_params=params(limit),
    )(*ins)


f16 = jnp.float16


def is_last():
    return (jnp.arange(BR, dtype=jnp.int32) == BR - 1)[:, None]


def coded(s):
    e = exponent(s[BR - 1 : BR, :])
    return jnp.where(is_last(), e, s * jnp.exp2(14.0 - e)).astype(f16)


def decoded(msg):
    q = jnp.exp2(msg[..., BR - 1 : BR, :].astype(f32) - 14.0)
    return jnp.where(is_last(), 2.0**14, msg.astype(f32)) * q


def sum_all(mine, theirs, e):
    xy = ("xl", "y", "xh")

    def other(z, xl, lat, xh):
        return (z, xl, lat ^ 1, xh)

    e = (jnp.maximum(e, send(e, other)) + 1.0)[0:1]
    tag = jnp.where(is_last(), e, 0.0)
    s = (mine + send(theirs, other)) * jnp.exp2(14.0 - e)[None] + tag[None]
    got = lax.all_to_all(s.astype(f16), xy, 0, 0, tiled=True)
    s = jnp.sum(decoded(got), axis=0)
    s = coded(s)
    r0, r1, r2, r3 = (
        decoded(send(s, lambda z, xl, lat, xh, k=k: (z ^ k, xl, lat, xh)) if k else s)
        for k in range(4)
    )
    s = coded((r0 + r1) + (r2 + r3))
    s = coded(decoded(s) + decoded(send(s, lambda z, xl, lat, xh: (7 - z, xl, lat, xh))))
    half = lax.all_to_all(jnp.broadcast_to(s[None], (16,) + s.shape), xy, 0, 0, tiled=True)
    far = send(half, other)
    return half.astype(f32), far.astype(f32)


def body(state, target, land, seeds, w_in, w_mid, w_out, w_noise):
    x, edge, seeds, w_in, w_out, w_noise = call(
        prep_kernel,
        [
            ((2, 384, 256), f32, 1), ((32, 256), f32, 1), ((M, 32), jnp.int32, 1),
            ((9, V, C), bf16, 1), ((V, C), bf16, 1), ((NB, C), f32, 1),
        ],
        [pltpu.VMEM((128, 384), f32), pltpu.SemaphoreType.DMA((3,))],
        (state, target, land, seeds, w_in, w_out, w_noise),
        {("in", 4), ("in", 5), ("in", 6)},
    )
    edge = send(edge, lambda z, xl, lat, xh: (z, xl, lat, xh ^ 1))
    seeds = lax.all_to_all(seeds, ("z", "xl"), 0, 0, tiled=True)
    (win,) = call(window_kernel, [((2 * WP, 256), bf16, 1)], [], (x, edge), kept=(0, 1))
    win, seeds = lax.optimization_barrier((win, seeds))
    n2, s2 = (lat_shift(win, d) for d in (2, -2))
    near = send(win, lambda z, xl, lat, xh: (z, xl, lat ^ 1, xh))
    next_chip = send(win, lambda z, xl, lat, xh: (z, xl, (lat + 2 * (lat % 2) - 1) % 8, xh))
    g, e = call(
        main_kernel, [((2, 16, BR, C), f32, 1), ((8, C), f32, 1)],
        [
            pltpu.VMEM((264, 128), f32),
            pltpu.VMEM((264, 128), f32),
            pltpu.VMEM((3, 256, 128), bf16),
            pltpu.VMEM((192, C), f32),
            pltpu.VMEM((164 * M, C), bf16),
            pltpu.VMEM((108 * M, C), bf16),
            pltpu.VMEM((108 * M, C), f32),
            pltpu.VMEM((108 * M, C), f32),
            pltpu.VMEM((108 * M, 128), f32),
            pltpu.VMEM((108 * M, 128), bf16),
            pltpu.VMEM((112 * M, C), bf16),
            pltpu.VMEM((54 * M, C), f32),
            pltpu.VMEM((64, C), f32),
            pltpu.VMEM((264, 128), f32),
            pltpu.VMEM((M, C), f32),
        ],
        (n2, next_chip, win, near, s2, seeds, w_in, w_mid, w_out, w_noise),
        kept=range(10),
        limit=32,
    )
    half, far = sum_all(g[0], g[1], e)
    o_in, o_mid, o_out, o_noise, o_loss = call(
        final_kernel,
        [((9, V, C), f32), ((9, C, C), f32), ((V, C), f32), ((NB, C), f32), ((1, 128), f32)],
        [
            pltpu.VMEM((NB, BR, C), f32),
            pltpu.VMEM((9, C, C), f32),
            pltpu.SemaphoreType.DMA((9,)),
        ],
        (half, far),
        {("out", 1)},
        kept=(0, 1),
    )
    return o_in, o_mid, o_out, o_noise, o_loss[0, 0]


def solution(mesh):
    fine = Mesh(mesh.devices.reshape(8, 2, 4, 2, 2), AX)
    lat = ("y", "c")
    placed = (
        P(None, lat, "xh"), P(None, lat, "xh"), P(lat, "xh"), P(("z", "xl"), None),
        P(), P(), P(), P(),
    )
    return jax.shard_map(
        body, mesh=fine, in_specs=placed, out_specs=(P(), P(), P(), P(), P()), check_vma=False
    )
```

```python
import jax
import jax.numpy as jnp
from jax import lax
from jax.experimental import pallas as pl
from jax.experimental.pallas import tpu as pltpu
from jax.sharding import Mesh, PartitionSpec as P

f32 = jnp.float32
bf16 = jnp.bfloat16
SQ = 0.0625
GC = 0.7978845608028654
GA = 0.044715
V = 100
C = 256
M = 16
TC = 360
WP = 32
WH = 27
ROWS = 104
BR = 112
NB = 32
AX = ("z", "xl", "y", "c", "xh")


def perm(f):
    out = []
    for i in range(256):
        z, xl, lat, xh = i >> 5, (i >> 4) & 1, (i >> 1) & 7, i & 1
        z2, xl2, lat2, xh2 = f(z, xl, lat, xh)
        out.append((i, (z2 % 8) * 32 + xl2 * 16 + lat2 * 2 + xh2))
    return out


def send(v, f):
    return lax.ppermute(v, AX, perm(f))


def lat_shift(v, d):
    def f(z, xl, lat, xh):
        return (z, xl, (lat + d) % 8, xh)

    return send(v, f)


def member_index():
    return lax.axis_index("z") * 2 + lax.axis_index("xl")


def lat_index():
    return lax.axis_index("y") * 2 + lax.axis_index("c")


def params(limit=None):
    return pltpu.CompilerParams(vmem_limit_bytes=(limit or 16) * 1024 * 1024)


def gelu(x):
    t = jnp.tanh(GC * (x + GA * x * x * x))
    return 0.5 * x * (1.0 + t)


def gelu_both(x):
    x2 = x * x
    t = jnp.tanh(GC * (x + GA * x2 * x))
    h = 0.5 * (1.0 + t)
    slope = h + 0.5 * x * (1.0 - t * t) * (GC * (1.0 + 3.0 * GA * x2))
    return x * h, slope


def gelu_slope(x):
    return gelu_both(x)[1]


def prep_kernel(
    state, target, land, seeds, w_in, w_out, w_noise,
    x_out, edge_out, seeds_out, w_in_out, w_out_out, w_noise_out, sc, sems,
):
    moves = [
        pltpu.make_async_copy(w, out, sems.at[i])
        for i, (w, out) in enumerate(((w_in, w_in_out), (w_out, w_out_out), (w_noise, w_noise_out)))
    ]
    for move in moves:
        move.start()
    sc[...] = jnp.zeros(sc.shape, f32)
    edge_out[...] = jnp.zeros(edge_out.shape, f32)
    seeds_out[...] = jnp.broadcast_to(seeds[...], seeds_out.shape)
    for r in range(2):
        x_out[r, 0:8, :] = jnp.zeros((8, 256), f32)
        x_out[r, 8 + TC : 384, :] = jnp.zeros((376 - TC, 256), f32)
        sc[0:V, 0:TC] = state[:, r, :].astype(f32)
        sc[104:105, 0:TC] = 1.0 + land[r : r + 1, :].astype(f32)
        x_out[r, 8 : 8 + TC, 0:128] = sc[...].T[0:TC]
        sc[0:V, 0:TC] = target[:, r, :].astype(f32)
        x_out[r, 8 : 8 + TC, 128:256] = sc[...].T[0:TC]
        edge_out[16 * r : 16 * r + 3, :] = x_out[r, TC + 5 : TC + 8, :]
        edge_out[16 * r + 10 : 16 * r + 13, :] = x_out[r, 8:11, :]
    for move in moves:
        move.wait()


def window_kernel(x, edge, win):
    m = member_index()
    start = (45 * m) // 2
    row = lax.broadcasted_iota(jnp.int32, (16, 256), 0)
    low = (row < 3) & (m == 0)
    high = (row >= 10) & (row < 13) & (m == M - 1)
    for r in range(2):
        base = pl.multiple_of(((start + 5) // 8) * 8, 8)
        near = x[r, pl.ds(base, WP + 8), :]
        w = pltpu.roll(near, WP + 8 - (start + 5 - base), 0)[0:WP]
        e = edge[16 * r : 16 * r + 16, :]
        win[WP * r : WP * r + 16, :] = jnp.where(low, e, w[0:16]).astype(bf16)
        win[WP * r + 16 : WP * r + 32, :] = jnp.where(high, e, w[16:32]).astype(bf16)


def main_kernel(
    n2, n1, own, s1, s2, seeds, w_in, w_mid, w_out, w_noise, g_out, e_out,
    S, T, SB, PB, HID, HO, SL, UP, OUT, DO, DM, INC, DS, QB, BIAS,
):
    own22 = member_index() % 2
    lat = lat_index()
    core = lax.axis_index("c")
    rows = ((n2, 1, -2), (n1, 0, -1), (n1, 1, -1), (own, 0, 0), (own, 1, 0),
            (s1, 0, 1), (s1, 1, 1), (s2, 0, 2))
    for k, (ref, r, d) in enumerate(rows):
        inside = (lat + d >= 0) & (lat + d < 8)
        row = ref[WP * r : WP * r + WP, :].astype(f32) * jnp.where(inside, 1.0, 0.0)
        S[WP * k : WP * k + WP, :] = row[:, 0:128]
        T[WP * k : WP * k + WP, :] = row[:, 128:256]
    S[256:264, :] = jnp.zeros((8, 128), f32)
    T[256:264, :] = jnp.zeros((8, 128), f32)
    QB[...] = jnp.broadcast_to(S[:, 104:105], QB.shape)
    for b in range(3):
        SB[b] = S[b : b + 256, :].astype(bf16)
    latents = (seeds[...].astype(f32) - 32767.5) / 18918.0
    BIAS[...] = jnp.dot(
        latents, w_noise[...], precision=lax.Precision.HIGHEST, preferred_element_type=f32
    )
    acc = None
    for a in range(3):
        for b in range(3):
            part = jnp.dot(
                SB[b, a * 32 : a * 32 + 192, 0:V], w_in[3 * a + b], preferred_element_type=f32
            )
            acc = part if acc is None else acc + part
    PB[...] = acc

    bias = BIAS[...]
    HID[162 * M : 164 * M, :] = jnp.zeros((2 * M, C), bf16)
    for r in range(6):
        gr = lat * 2 - 2 + r
        valid = jnp.where((gr >= 0) & (gr < 16), 1.0, 0.0).astype(f32)

        def hid_cell(i, carry, r=r, valid=valid):
            row = PB[pl.ds(r * 32 + i, 1), :]
            h = gelu(jnp.broadcast_to(row, (M, C)) + bias) * valid
            HID[pl.ds(pl.multiple_of((r * WH + i) * M, M), M), :] = h.astype(bf16)
            return carry

        lax.fori_loop(0, WH, hid_cell, 0, unroll=27)

    NR = WH * M

    MC = 54 * M

    def mid_row(r, carry):
        base = pl.multiple_of(r * MC, M)
        lhs = jnp.concatenate(
            [
                HID[pl.ds(pl.multiple_of(base + (a * WH + b) * M, M), MC), :]
                for a in range(3)
                for b in range(3)
            ],
            axis=1,
        )
        pre = jnp.dot(lhs, w_mid[...].reshape(9 * C, C), preferred_element_type=f32)
        act, slope = gelu_both(pre)
        hid = HID[pl.ds(pl.multiple_of(base + (WH + 1) * M, M), MC), :].astype(f32)
        ho = (act + hid).astype(bf16)
        HO[pl.ds(base, MC), :] = ho
        SL[pl.ds(base, MC), :] = slope
        OUT[pl.ds(base, MC), 0:V] = lax.dot_general(
            ho, w_out[...], (((1,), (1,)), ((), ())), preferred_element_type=f32
        )
        return carry

    lax.fori_loop(0, 2, mid_row, 0)

    def cell_terms(r, i, with_loss):
        base = pl.multiple_of((r * WH + i) * M, M)
        srow = (r + 2) * 32 + i + 2
        st = S[pl.ds(srow, 1), :]
        tg = T[pl.ds(srow, 1), :]
        q = QB[pl.ds(srow, 1), :]
        o = (OUT[pl.ds(base, M), :] + st).astype(bf16).astype(f32)
        miss = o - tg
        e = miss * miss + SQ
        inv = lax.rsqrt(e)
        slope = miss * inv
        dist = e * inv - 0.25 if with_loss else None
        total = None
        spread = None
        for k in range(1, 9):
            u = o - pltpu.roll(o, k, 0)
            e = u * u + SQ
            inv = lax.rsqrt(e)
            s = u * inv
            if k < 8:
                s = s - pltpu.roll(s, M - k, 0)
            total = s if total is None else total + s
            if with_loss:
                d = e * inv - 0.25
                if k == 8:
                    d = 0.5 * d
                spread = d if spread is None else spread + d
        g = q * (slope * (1.0 / M) - total * (1.0 / (M * (M - 1))))
        DO[pl.ds(base, M), :] = g.astype(bf16)
        if with_loss:
            return q * (dist * (1.0 / M) - spread * (1.0 / (M * (M - 1))))
        return None

    loss = jnp.zeros((M, 128), f32)
    for r in (1, 2):

        def loss_cell(i, total, r=r):
            term = cell_terms(r, i, True)
            mine = (i >= 1) & ((i < 23) | ((i == 23) & (own22 > 0)))
            return total + jnp.where(mine, 1.0, 0.0) * term

        loss = lax.fori_loop(0, WH, loss_cell, loss, unroll=9)
    for r in (0, 3):

        def grad_cell(i, carry, r=r):
            cell_terms(r, i, False)
            return carry

        lax.fori_loop(0, WH, grad_cell, 0, unroll=9)
    lane = lax.broadcasted_iota(jnp.int32, (M, 128), 1)
    loss = jnp.sum(jnp.sum(jnp.where(lane < V, loss, 0.0), axis=0, keepdims=True), axis=1, keepdims=True)

    UP[...] = jnp.dot(DO[:, 0:V], w_out[...], preferred_element_type=f32)

    def mid_cell(i, carry):
        at = pl.multiple_of(i * 2 * M, M)
        DM[pl.ds(at, 2 * M), :] = (UP[pl.ds(at, 2 * M), :] * SL[pl.ds(at, 2 * M), :]).astype(bf16)
        return carry

    lax.fori_loop(0, 54, mid_cell, 0, unroll=6)
    DM[108 * M : 112 * M, :] = jnp.zeros((4 * M, C), bf16)

    wcat = jnp.concatenate([w_mid[t] for t in range(9)], axis=1)
    for r in range(2):
        lhs = jnp.concatenate(
            [
                DM[((r + 2 - a) * WH + 2 - b) * M : ((r + 2 - a) * WH + 2 - b) * M + NR, :]
                for a in range(3)
                for b in range(3)
            ],
            axis=1,
        )
        INC[r * NR : (r + 1) * NR, :] = lax.dot_general(
            lhs, wcat, (((1,), (1,)), ((), ())), preferred_element_type=f32
        )
    DS[...] = jnp.zeros(DS.shape, f32)
    dsum = jnp.zeros((M, C), f32)
    for r in range(2):

        def in_cell(i, total, r=r):
            x = jnp.broadcast_to(PB[pl.ds((r + 2) * 32 + i + 2, 1), :], (M, C)) + bias
            base = pl.multiple_of((r * WH + i) * M, M)
            upb = pl.multiple_of(((r + 1) * WH + 1 + i) * M, M)
            d = (INC[pl.ds(base, M), :] + UP[pl.ds(upb, M), :]) * gelu_slope(x)
            mine = jnp.where((i < 22) | (own22 > 0), 1.0, 0.0)
            d = d.astype(bf16).astype(f32) * mine
            DS[pl.ds(r * 32 + i + 2, 1), :] = jnp.sum(d, axis=0, keepdims=True)
            return total + d

        dsum = lax.fori_loop(0, 23, in_cell, dsum, unroll=4)

    def store(k, lo, hi, value):
        g_out[(k // 16) ^ core, k % 16, lo:hi, :] = value

    g_out[:, :, ROWS:BR, :] = jnp.zeros((2, 16, BR - ROWS, C), f32)
    peaks = []

    def put(row, value):
        done = 0
        n = value.shape[0]
        peaks.append(jnp.max(jnp.abs(value), axis=0, keepdims=True))
        while done < n:
            k, i = divmod(row + done, ROWS)
            take = min(n - done, ROWS - i)
            store(k, i, i + take, value[done : done + take, :])
            done += take

    cell = lax.broadcasted_iota(jnp.int32, (NR, C), 0) >> 4
    mine = (cell < 22) | ((cell == 22) & (own22 > 0))
    start = (WH + 1) * M
    dmc = jnp.concatenate(
        [
            jnp.where(mine, DM[start + r * NR : start + (r + 1) * NR, :].astype(f32), 0.0)
            for r in range(2)
        ],
        axis=0,
    )
    dmt = dmc.T.astype(bf16)
    for a in range(3):
        for b in range(3):
            hs = ((a + 1) * WH + b + 1) * M
            g = jnp.dot(dmt, HID[hs : hs + 2 * NR, :], preferred_element_type=f32)
            put((3 * a + b) * C, g.T)
    doc = jnp.concatenate(
        [
            jnp.where(
                mine[:, 0:128], DO[start + r * NR : start + (r + 1) * NR, :].astype(f32), 0.0
            )
            for r in range(2)
        ],
        axis=0,
    )
    dot_ = doc.T.astype(bf16)
    go = jnp.dot(dot_, HO[start : start + 2 * NR, :], preferred_element_type=f32)
    ds = DS[...]
    hi = ds.astype(bf16)
    lo = (ds - hi.astype(f32)).astype(bf16)
    both = jnp.concatenate([hi, lo], axis=1)
    for a in range(3):
        for b in range(3):
            g = lax.dot_general(
                SB[b, (a + 2) * 32 : (a + 2) * 32 + 64, :], both,
                (((0,), (0,)), ((), ())), preferred_element_type=f32,
            )
            put(9 * C + V * (3 * a + b), (g[:, 0:C] + g[:, C : 2 * C])[0:V, :])
    put(9 * C + 9 * V, go[0:V, :])
    put(9 * C + 10 * V, jnp.zeros((NB * ROWS - 9 * C - 10 * V, C), f32))
    gn = lax.dot_general(
        latents, dsum, (((0,), (0,)), ((), ())),
        precision=lax.Precision.HIGHEST, preferred_element_type=f32,
    )
    peaks.append(jnp.max(jnp.abs(gn), axis=0, keepdims=True))
    for k in range(NB):
        store(k, ROWS, ROWS + 1, gn[k : k + 1, :])
    loss = jnp.broadcast_to(loss * (1.0 / (V * 16 * 720)), (1, C))
    first = loss.astype(bf16).astype(f32)
    store(0, ROWS + 1, ROWS + 2, first)
    store(0, ROWS + 2, ROWS + 3, loss - first)
    peaks.append(jnp.abs(loss))
    peak = peaks[0]
    for p in peaks[1:]:
        peak = jnp.maximum(peak, p)
    peak = jnp.broadcast_to(jnp.max(peak, axis=1, keepdims=True), (8, C))
    e_out[...] = exponent(peak)


def exponent(bound):
    return jnp.ceil(jnp.log2(jnp.maximum(bound, 1e-30)))


def final_kernel(half, far, o_in, o_mid, o_out, o_noise, o_loss, t, u, w, out_sems):
    core = lax.axis_index("c")
    for slot, ref in ((core, half), (1 - core, far)):
        for k in range(16):
            f = jnp.exp2(ref[k, BR - 1 : BR, :] - 14.0)
            t[slot * 16 + k] = ref[k] * f

    def get(row, n):
        parts = []
        done = 0
        while done < n:
            k, i = divmod(row + done, ROWS)
            take = min(n - done, ROWS - i)
            parts.append((done, take, k, i))
            done += take
        return parts

    def scale_of(pieces, count):
        total = jnp.zeros((8, C), f32)
        ragged = jnp.zeros((1, C), f32)
        for p in pieces:
            for _, take, k, i in p:
                v = t[k, i : i + take, :]
                v = v * v
                if take % 8 == 0:
                    total = total + jnp.sum(v.reshape(take // 8, 8, C), axis=0)
                else:
                    ragged = ragged + jnp.sum(v, axis=0, keepdims=True)
        total = jnp.sum(total, axis=0, keepdims=True) + ragged
        ms = jnp.sum(total, axis=1, keepdims=True) * (1.0 / count)
        return lax.rsqrt(ms + 1e-6)

    moves = []

    def emit(pieces, scale, buf, out, k):
        for done, take, b, i in pieces:
            buf[done : done + take, :] = t[b, i : i + take, :] * scale
        if out is not None:
            move = pltpu.make_async_copy(buf, out, out_sems.at[k])
            move.start()
            moves.append(move)

    pieces = [get(C * k, C) for k in range(9)]
    scale = scale_of(pieces, 9 * C * C)
    for k in range(9):
        emit(pieces[k], scale, u.at[k], o_mid.at[k], k)
    pieces = [get(9 * C + V * k, V) for k in range(9)]
    scale = scale_of(pieces, 9 * V * C)
    for k in range(9):
        emit(pieces[k], scale, w.at[k], o_in.at[k], 9 + k)
    pieces = get(9 * C + 9 * V, V)
    emit(pieces, scale_of([pieces], V * C), o_out, None, 0)
    pieces = [(k, 1, k, ROWS) for k in range(NB)]
    emit(pieces, scale_of([pieces], NB * C), o_noise, None, 0)
    o_loss[...] = t[0, ROWS + 1 : ROWS + 2, 0:128] + t[0, ROWS + 2 : ROWS + 3, 0:128]
    for move in moves:
        move.wait()


def call(kernel, outs, scratch, ins, place=None, kept=(), limit=None):
    place = place or {}
    vmem = pl.BlockSpec(memory_space=pltpu.VMEM)
    left = pl.BlockSpec(memory_space=pl.ANY)
    ins = [
        pltpu.with_memory_space_constraint(v, pltpu.VMEM if i in kept else pltpu.HBM)
        for i, v in enumerate(ins)
    ]
    return pl.pallas_call(
        kernel,
        out_shape=[
            pltpu.VMEM(o[0], o[1]) if len(o) > 2 else jax.ShapeDtypeStruct(*o) for o in outs
        ],
        in_specs=[left if ("in", i) in place else vmem for i in range(len(ins))],
        out_specs=[left if ("out", i) in place else vmem for i in range(len(outs))],
        scratch_shapes=scratch,
        compiler_params=params(limit),
    )(*ins)


f16 = jnp.float16


def is_last():
    return (jnp.arange(BR, dtype=jnp.int32) == BR - 1)[:, None]


def coded(s):
    e = exponent(s[BR - 1 : BR, :])
    return jnp.where(is_last(), e, s * jnp.exp2(14.0 - e)).astype(f16)


def decoded(msg):
    q = jnp.exp2(msg[..., BR - 1 : BR, :].astype(f32) - 14.0)
    return jnp.where(is_last(), 2.0**14, msg.astype(f32)) * q


def sum_all(mine, theirs, e):
    xy = ("xl", "y", "xh")

    def other(z, xl, lat, xh):
        return (z, xl, lat ^ 1, xh)

    e = (jnp.maximum(e, send(e, other)) + 1.0)[0:1]
    tag = jnp.where(is_last(), e, 0.0)
    s = (mine + send(theirs, other)) * jnp.exp2(14.0 - e)[None] + tag[None]
    got = lax.all_to_all(s.astype(f16), xy, 0, 0, tiled=True)
    s = jnp.sum(decoded(got), axis=0)
    s = coded(s)
    r0, r1, r2, r3 = (
        decoded(send(s, lambda z, xl, lat, xh, k=k: (z ^ k, xl, lat, xh)) if k else s)
        for k in range(4)
    )
    s = coded((r0 + r1) + (r2 + r3))
    s = coded(decoded(s) + decoded(send(s, lambda z, xl, lat, xh: (7 - z, xl, lat, xh))))
    half = lax.all_to_all(jnp.broadcast_to(s[None], (16,) + s.shape), xy, 0, 0, tiled=True)
    far = send(half, other)
    return half.astype(f32), far.astype(f32)


def body(state, target, land, seeds, w_in, w_mid, w_out, w_noise):
    x, edge, seeds, w_in, w_out, w_noise = call(
        prep_kernel,
        [
            ((2, 384, 256), f32, 1), ((32, 256), f32, 1), ((M, 32), jnp.int32, 1),
            ((9, V, C), bf16, 1), ((V, C), bf16, 1), ((NB, C), f32, 1),
        ],
        [pltpu.VMEM((128, 384), f32), pltpu.SemaphoreType.DMA((3,))],
        (state, target, land, seeds, w_in, w_out, w_noise),
        {("in", 4), ("in", 5), ("in", 6)},
    )
    edge = send(edge, lambda z, xl, lat, xh: (z, xl, lat, xh ^ 1))
    seeds = lax.all_to_all(seeds, ("z", "xl"), 0, 0, tiled=True)
    (win,) = call(window_kernel, [((2 * WP, 256), bf16, 1)], [], (x, edge), kept=(0, 1))
    win, seeds = lax.optimization_barrier((win, seeds))
    n2, n1, s1, s2 = (lat_shift(win, d) for d in (2, 1, -1, -2))
    g, e = call(
        main_kernel, [((2, 16, BR, C), f32, 1), ((8, C), f32, 1)],
        [
            pltpu.VMEM((264, 128), f32),
            pltpu.VMEM((264, 128), f32),
            pltpu.VMEM((3, 256, 128), bf16),
            pltpu.VMEM((192, C), f32),
            pltpu.VMEM((164 * M, C), bf16),
            pltpu.VMEM((108 * M, C), bf16),
            pltpu.VMEM((108 * M, C), f32),
            pltpu.VMEM((108 * M, C), f32),
            pltpu.VMEM((108 * M, 128), f32),
            pltpu.VMEM((108 * M, 128), bf16),
            pltpu.VMEM((112 * M, C), bf16),
            pltpu.VMEM((54 * M, C), f32),
            pltpu.VMEM((64, C), f32),
            pltpu.VMEM((264, 128), f32),
            pltpu.VMEM((M, C), f32),
        ],
        (n2, n1, win, s1, s2, seeds, w_in, w_mid, w_out, w_noise),
        kept=range(10),
        limit=32,
    )
    half, far = sum_all(g[0], g[1], e)
    o_in, o_mid, o_out, o_noise, o_loss = call(
        final_kernel,
        [((9, V, C), f32), ((9, C, C), f32), ((V, C), f32), ((NB, C), f32), ((1, 128), f32)],
        [
            pltpu.VMEM((NB, BR, C), f32),
            pltpu.VMEM((9, C, C), f32),
            pltpu.VMEM((9, V, C), f32),
            pltpu.SemaphoreType.DMA((18,)),
        ],
        (half, far),
        {("out", 0), ("out", 1)},
        kept=(0, 1),
    )
    return o_in, o_mid, o_out, o_noise, o_loss[0, 0]


def solution(mesh):
    fine = Mesh(mesh.devices.reshape(8, 2, 4, 2, 2), AX)
    lat = ("y", "c")
    placed = (
        P(None, lat, "xh"), P(None, lat, "xh"), P(lat, "xh"), P(("z", "xl"), None),
        P(), P(), P(), P(),
    )
    return jax.shard_map(
        body, mesh=fine, in_specs=placed, out_specs=(P(), P(), P(), P(), P()), check_vma=False
    )
```
